32 devices in a mesh: rows: 8 (over z, x), cols: 4 (over y, core).
Axes of the slice: x: 2, y: 2, z: 4, core: 2. Of those that a mesh axis runs over, the one named last changes fastest.
Arguments:
- panel_cols: float32 [65536, 256], P(('rows', 'cols')), may hold values from -10000 to 10000, as said below
- trailing: float32 [65536, 1024], P('rows', 'cols'), may hold values from -200000 to 200000
Outputs:
- r_factor: float32 [256, 256], replicated
- r_cross: float32 [256, 1024], P(None, 'cols')
- updated: float32 [65536, 1024], P('rows', 'cols')
The draws below stay inside these ranges and needn't reach their ends.
Inputs may be any that keep to these rules, and one draw needn't show every extreme that they name: panel_cols has full column rank.
All inputs are finite; a program needn't handle non-finite values.
Results may differ from the reference program's by a relative error of at most 0.0003.
Values sent between devices are 32-bit elements; how exact they have to be, the bound alone decides.
A program may use at most 128 MiB of HBM per device.

```python
import math
import jax
import jax.numpy as jnp
from jax import lax

B = 256
NC = 1024
ROWS = 65536


def panel_matrix(key):
    keys = jax.random.split(jax.random.fold_in(key, 11), 4)
    position = jnp.arange(ROWS, dtype=jnp.float32) / ROWS
    base_entries = jnp.clip(jax.random.normal(keys[0], (ROWS, B), jnp.float32), -6.0, 6.0)
    spread = jax.random.uniform(keys[1], (ROWS, 1), jnp.float32, 0.0, 1.0)
    row_scale = jnp.power(10.0, spread) * jnp.power(3.0, 0.5 * position)[:, None] / 6.0
    column_scale = jnp.exp(jax.random.uniform(keys[2], (B,), jnp.float32, 0.0, math.log(10.0)))
    perturb = jnp.clip(jax.random.normal(keys[3], (B, B), jnp.float32), -6.0, 6.0) * (0.35 / math.sqrt(B))
    mixing = (jnp.eye(B, dtype=jnp.float32) + perturb) * column_scale[None, :]
    return jnp.dot(base_entries * row_scale, mixing, precision=lax.Precision.HIGHEST)


def draw_panel_cols(key, part):
    return panel_matrix(key)


def draw_trailing(key, part):
    matrix = panel_matrix(key)
    keys = jax.random.split(jax.random.fold_in(key, 23), 2)
    coeffs = jnp.clip(jax.random.normal(keys[0], (B, NC), jnp.float32), -6.0, 6.0) * (0.6 / (4.6 * math.sqrt(B)))
    noise = jnp.clip(jax.random.normal(keys[1], (ROWS, NC), jnp.float32), -6.0, 6.0)
    return jnp.dot(matrix, coeffs, precision=lax.Precision.HIGHEST) + noise


def setup_inputs(seed: int = 0) -> dict:
    splits = jax.random.split(jax.random.key(seed), 3)
    return {
        "panel_cols": draw_panel_cols(jax.random.fold_in(splits[2], 71), 0),
        "trailing": draw_trailing(jax.random.fold_in(splits[2], 71), 0),
    }


def reference(panel_cols, trailing):
    orthonormal, upper_factor = jnp.linalg.qr(panel_cols, mode='reduced')
    sign_flip = jnp.where(jnp.diagonal(upper_factor) < 0, -1.0, 1.0).astype(upper_factor.dtype)
    upper_factor = upper_factor * sign_flip[:, None]
    orthonormal = orthonormal * sign_flip[None, :]
    coupling = jnp.dot(orthonormal.T, trailing, precision=lax.Precision.HIGHEST)
    updated = trailing - jnp.dot(orthonormal, coupling, precision=lax.Precision.HIGHEST)
    shrink = 1.0 / math.sqrt(ROWS)
    return (upper_factor * shrink, coupling * shrink, updated)
```

```python
import functools
import math

import jax
import jax.numpy as jnp
from jax import lax
from jax.experimental import pallas as pl
from jax.experimental.pallas import tpu as pltpu

MESH = pl.DeviceIdType.MESH
HIGHEST = lax.Precision.HIGHEST
CHUNKS = 8
ITEMS = 8
EARLY = 3
MORE = (1, 1, 1, 0, 1, 0, 1, 0)
GROUP = 4
TILES = 8
PARTS = 4
AHEAD = 2


def dot(left, right):
    return lax.dot_general(left, right, (((1,), (0,)), ((), ())), precision=HIGHEST, preferred_element_type=jnp.float32)


def dot_t(left, right):
    return lax.dot_general(left, right, (((0,), (0,)), ((), ())), precision=HIGHEST, preferred_element_type=jnp.float32)


def split(x):
    high = x.astype(jnp.bfloat16)
    return high, (x - high.astype(jnp.float32)).astype(jnp.bfloat16)


def mul(left, right):
    return jnp.dot(left, right, preferred_element_type=jnp.float32)


def dot3(left, right):
    left_hi, left_lo = split(left)
    right_hi, right_lo = split(right)
    count = left.shape[0]
    both = mul(jnp.concatenate([left_hi, left_lo], axis=0), right_hi)
    return both[:count] + (both[count:] + mul(left_hi, right_lo))


def turn_plan(width):
    quarter = width // 8
    counts = (quarter, quarter, quarter, quarter // 2, quarter // 2)
    return [(sum(counts[:t]), counts[t]) for t in range(len(counts))]


def eliminate(a_ref, m_ref, first, last):
    size = a_ref.shape[0]
    sub = lax.broadcasted_iota(jnp.int32, (size, 1), 0)
    lane = lax.broadcasted_iota(jnp.int32, (size, size), 1)
    lane_row = lax.broadcasted_iota(jnp.int32, (1, size), 1)

    def step(index, carry):
        j = index * GROUP
        a = a_ref[...]
        rows = [a_ref[pl.ds(j + t, 1), :] for t in range(GROUP)]
        mrows = [m_ref[pl.ds(j + t, 1), :] for t in range(GROUP)]
        cols = [jnp.sum(jnp.where(lane == j + t, a, 0.0), axis=1, keepdims=True) for t in range(GROUP)]
        head = {
            (t, u): jnp.sum(jnp.where(lane_row == j + u, rows[t], 0.0), axis=1, keepdims=True)
            for t in range(GROUP)
            for u in range(t, GROUP)
        }
        m = m_ref[...]
        for t in range(GROUP):
            inverse = 1.0 / head[t, t]
            factor = jnp.where(sub > j + t, cols[t] * inverse, 0.0)
            ratio = {u: head[t, u] * inverse for u in range(t + 1, GROUP)}
            for u in range(t + 1, GROUP):
                cols[u] = cols[u] - factor * head[t, u]
            for u in range(t + 1, GROUP):
                for v in range(u, GROUP):
                    head[u, v] = head[u, v] - ratio[u] * head[t, v]
            for u in range(t + 1, GROUP):
                rows[u] = rows[u] - ratio[u] * rows[t]
                mrows[u] = mrows[u] - ratio[u] * mrows[t]
            a = a - factor * rows[t]
            m = m - factor * mrows[t]
        a_ref[...] = a
        m_ref[...] = m
        return carry

    lax.fori_loop(first // GROUP, last // GROUP, step, 0)


def scale_rows(a_ref, m_ref):
    size = a_ref.shape[0]
    sub = lax.broadcasted_iota(jnp.int32, (size, size), 0)
    lane = lax.broadcasted_iota(jnp.int32, (size, size), 1)
    a = a_ref[...]
    diagonal = jnp.sum(jnp.where(lane == sub, a, 0.0), axis=1, keepdims=True)
    scale = 1.0 / jnp.sqrt(diagonal)
    return jnp.where(lane >= sub, a * scale, 0.0), m_ref[...] * scale


def unit(size):
    sub = lax.broadcasted_iota(jnp.int32, (size, size), 0)
    lane = lax.broadcasted_iota(jnp.int32, (size, size), 1)
    return jnp.where(lane == sub, 1.0, 0.0).astype(jnp.float32)


def factor_kernel(
    nr, nc,
    panel, trailing, block, trail, upper_out, coupling_out, weights_out,
    gram, gram_stage, col_stage, gram_sum, cross, cross_stage, cross_sum, work, minv, inv, square,
    load_sem, y_send, y_recv, half_send, half_recv, fwd_send, fwd_recv,
    rs_send, rs_recv, cx_send, cx_recv, ag_send, ag_recv, xrs_send, xrs_recv, xag_send, xag_recv,
):
    me_r, me_c = lax.axis_index("rows"), lax.axis_index("cols")
    depth, width = panel.shape
    half = nc // 2
    side, place = me_c // half, lax.rem(me_c, half)
    across = lax.rem(me_c + half, nc)
    chunk = depth // CHUNKS
    piece = width // nr
    groups = cross.shape[0]
    per_group = ITEMS // groups
    deep = depth // per_group
    wide = width // groups
    cross_piece = wide // nr
    hw = width // 2
    sends = []

    def remote(src, dst, send, recv, where):
        copy = pltpu.make_async_remote_copy(
            src_ref=src, dst_ref=dst, send_sem=send, recv_sem=recv, device_id=where, device_id_type=MESH
        )
        copy.start()
        sends.append(copy)
        return copy

    load_panel = pltpu.make_async_copy(panel, block.at[me_c], load_sem.at[0])
    load_panel.start()
    load_trail = pltpu.make_async_copy(trailing, trail, load_sem.at[1])
    load_trail.start()

    barrier = pltpu.get_barrier_semaphore()
    for d in range(1, nr):
        pl.semaphore_signal(barrier, inc=1, device_id={"rows": lax.rem(me_r + d, nr)}, device_id_type=MESH)
    for d in range(1, nc):
        pl.semaphore_signal(barrier, inc=1, device_id={"cols": lax.rem(me_c + d, nc)}, device_id_type=MESH)
    pl.semaphore_wait(barrier, nr + nc - 2)

    def item(k):
        return pl.ds((k % per_group) * deep, deep), pl.ds((k // per_group) * wide, wide)

    y_copies = []

    def send_across(k):
        rows, lanes = item(k)
        y_copies.append(
            remote(panel.at[rows, lanes], block.at[me_c, rows, lanes], y_send.at[k], y_recv.at[k], {"cols": across})
        )

    for k in range(EARLY):
        send_across(k)
    half_copies = []
    for d in range(1, half):
        peer = side * half + lax.rem(place + d, half)
        half_copies.append(remote(panel, block.at[me_c], half_send.at[d], half_recv.at[d], {"cols": peer}))

    def add_cross(source):
        def step(i, carry):
            rows = pl.ds(pl.multiple_of(i * chunk, chunk), chunk)
            long = pl.ds(pl.multiple_of(source * depth + i * chunk, chunk), chunk)
            product = dot_t(block[source, rows, :], trail[long, :])
            for g in range(groups):
                cross[g] += product[g * wide : (g + 1) * wide, :]
            return carry

        lax.fori_loop(0, CHUNKS, step, 0)

    def add_item(source, k):
        rows, lanes = item(k)
        long = pl.ds(pl.multiple_of(source * depth + (k % per_group) * deep, deep), deep)
        cross[k // per_group] += dot_t(block[source, rows, lanes], trail[long, :])

    load_panel.wait()
    gram[...] = jnp.zeros_like(gram)

    def gram_step(i, carry):
        rows = block[me_c, pl.ds(pl.multiple_of(i * chunk, chunk), chunk), :]
        gram[...] += dot_t(rows, rows)
        return carry

    lax.fori_loop(0, CHUNKS, gram_step, 0)

    def scatter(total, stage, send, recv, piece=piece):
        copies = []
        for d in range(1, nr):
            peer = lax.rem(me_r + d, nr)
            rows = pl.ds(pl.multiple_of(peer * piece, piece), piece)
            copies.append(remote(total.at[rows], stage.at[d], send.at[d], recv.at[d], {"rows": peer}))
        return copies

    def gather(total, send, recv, piece=piece):
        rows = pl.ds(pl.multiple_of(me_r * piece, piece), piece)
        return [
            remote(total.at[rows], total.at[rows], send.at[d], recv.at[d], {"rows": lax.rem(me_r + d, nr)})
            for d in range(1, nr)
        ]

    def arrived(copies):
        for copy in copies:
            copy.wait_recv()

    mine = pl.ds(pl.multiple_of(me_r * piece, piece), piece)
    cross_mine = pl.ds(pl.multiple_of(me_r * cross_piece, cross_piece), cross_piece)

    def summed(total, stage, mine=mine):
        value = total[mine, :]
        for d in range(1, nr):
            value = value + stage[d]
        return value

    gram_rs = scatter(gram, gram_stage, rs_send, rs_recv)
    load_trail.wait()
    cross[...] = jnp.zeros_like(cross)
    add_cross(me_c)
    arrived(gram_rs)
    col_stage[me_c] = summed(gram, gram_stage)
    exchange = [
        remote(col_stage.at[me_c], col_stage.at[me_c], cx_send.at[d], cx_recv.at[d], {"cols": lax.rem(me_c + d, nc)})
        for d in range(1, nc)
    ]
    for k in range(EARLY, ITEMS):
        send_across(k)
    for d in range(1, half):
        half_copies[d - 1].wait_recv()
        source = side * half + lax.rem(place + half - d, half)
        add_cross(source)
    arrived(exchange)
    value = col_stage[0]
    for c in range(1, nc):
        value = value + col_stage[c]
    gram_sum[mine, :] = value
    gram_ag = gather(gram_sum, ag_send, ag_recv)

    forwards = {}

    def take(k):
        y_copies[k].wait_recv()
        rows, lanes = item(k)
        for d in range(1, half):
            peer = side * half + lax.rem(place + d, half)
            slot = (d - 1) * ITEMS + k
            part = block.at[across, rows, lanes]
            forwards[d, k] = remote(part, part, fwd_send.at[slot], fwd_recv.at[slot], {"cols": peer})
        add_item(across, k)

    def take_forward(k):
        for d in range(1, half):
            forwards[d, k].wait_recv()
            source = (1 - side) * half + lax.rem(place + half - d, half)
            add_item(source, k)

    cross_rs, cross_ag = {}, {}

    def start_cross(g):
        cross_rs[g] = scatter(cross.at[g], cross_stage.at[g], xrs_send.at[g], xrs_recv.at[g], cross_piece)

    def share_cross(g):
        arrived(cross_rs[g])
        cross_sum[g, cross_mine, :] = summed(cross.at[g], cross_stage.at[g], cross_mine)
        cross_ag[g] = gather(cross_sum.at[g], xag_send.at[g], xag_recv.at[g], cross_piece)

    pending = []
    for k in range(ITEMS):
        pending.append(([functools.partial(take_forward, k - 1)] if k % per_group else []) + [functools.partial(take, k)])
        if k % per_group == per_group - 1:
            pending[-1].append(functools.partial(take_forward, k))
            pending[-1].append(functools.partial(start_cross, k // per_group))
    for g in range(groups - 1):
        pending[(g + 1) * per_group + 2].append(functools.partial(share_cross, g))

    def advance():
        for task in pending.pop(0):
            task()

    def run(first, last, more):
        eliminate(work, minv, first, last)
        for _ in range(more):
            advance()

    for _ in range(EARLY):
        advance()
    arrived(gram_ag)
    work[...] = gram_sum[pl.ds(0, hw), pl.ds(0, hw)]
    minv[...] = unit(hw)
    quarter = hw // 4
    for q in range(4):
        run(q * quarter, (q + 1) * quarter, MORE[q])
    upper1, inverse1 = scale_rows(work, minv)
    cross1 = dot(inverse1, gram_sum[pl.ds(0, hw), pl.ds(hw, hw)])
    upper_out[pl.ds(0, hw), pl.ds(0, hw)] = upper1
    upper_out[pl.ds(0, hw), pl.ds(hw, hw)] = cross1
    upper_out[pl.ds(hw, hw), pl.ds(0, hw)] = jnp.zeros_like(upper1)
    work[...] = gram_sum[pl.ds(hw, hw), pl.ds(hw, hw)] - dot_t(cross1, cross1)
    inv[pl.ds(0, hw), pl.ds(0, hw)] = inverse1
    minv[...] = unit(hw)
    for q in range(4):
        run(q * quarter, (q + 1) * quarter, MORE[4 + q])
    upper2, inverse2 = scale_rows(work, minv)
    upper_out[pl.ds(hw, hw), pl.ds(hw, hw)] = upper2
    inverse1 = inv[pl.ds(0, hw), pl.ds(0, hw)]
    corner = -dot(inverse2, dot_t(upper_out[pl.ds(0, hw), pl.ds(hw, hw)], inverse1))
    inv[pl.ds(0, hw), pl.ds(hw, hw)] = jnp.zeros_like(inverse1)
    inv[pl.ds(hw, hw), pl.ds(0, hw)] = corner
    inv[pl.ds(hw, hw), pl.ds(hw, hw)] = inverse2
    while pending:
        advance()
    inverse = inv[...]
    square[...] = dot_t(inverse, inverse)
    last = slice((groups - 1) * wide, groups * wide)
    coupling_out[...] = jnp.zeros_like(coupling_out)
    weights_out[...] = jnp.zeros_like(weights_out)
    for g in range(groups - 1):
        arrived(cross_ag[g])
        part = cross_sum[g]
        coupling_out[...] += dot(inv[:, g * wide : (g + 1) * wide], part)
        weights_out[...] += dot(square[:, g * wide : (g + 1) * wide], part)
    share_cross(groups - 1)
    arrived(cross_ag[groups - 1])
    part = cross_sum[groups - 1]
    weights_out[...] += dot(square[:, last], part)
    coupling_out[...] += dot(inv[:, last], part)
    for copy in sends:
        copy.wait_send()


def transposed_kernel(
    nr, nc,
    panel, trailing, block, trail, upper_out, coupling_out, weights_out,
    gram, gram_stage, col_stage, gram_sum, cross, early_stage, next_stage, late_stage, cross_sum, turned,
    work, minv, inv, square,
    load_sem, y_send, y_recv, half_send, half_recv, fwd_send, fwd_recv,
    rs_send, rs_recv, cx_send, cx_recv, ag_send, ag_recv, xrs_send, xrs_recv, xag_send, xag_recv, late_send, late_recv,
):
    me_r, me_c = lax.axis_index("rows"), lax.axis_index("cols")
    depth, width = panel.shape
    side, place = me_c // 2, lax.rem(me_c, 2)
    partner = side * 2 + 1 - place
    across = (1 - side) * 2 + place
    behind = (1 - side) * 2 + 1 - place
    chunk = depth // CHUNKS
    piece = width // nr
    hw = width // 2
    quarter = hw // 4
    deep = depth // PARTS
    turns = turn_plan(width)
    sends = []

    def remote(src, dst, send, recv, where):
        copy = pltpu.make_async_remote_copy(
            src_ref=src, dst_ref=dst, send_sem=send, recv_sem=recv, device_id=where, device_id_type=MESH
        )
        copy.start()
        sends.append(copy)
        return copy

    load_panel = pltpu.make_async_copy(panel, block.at[me_c], load_sem.at[0])
    load_panel.start()
    load_trail = pltpu.make_async_copy(trailing, trail, load_sem.at[1])
    load_trail.start()

    barrier = pltpu.get_barrier_semaphore()
    for d in range(1, nr):
        pl.semaphore_signal(barrier, inc=1, device_id={"rows": lax.rem(me_r + d, nr)}, device_id_type=MESH)
    for d in range(1, nc):
        pl.semaphore_signal(barrier, inc=1, device_id={"cols": lax.rem(me_c + d, nc)}, device_id_type=MESH)
    pl.semaphore_wait(barrier, nr + nc - 2)

    y_copies = []

    def send_part(k):
        rows, lanes = pl.ds(k * deep, deep), pl.ds(0, hw)
        y_copies.append(
            remote(panel.at[rows, lanes], block.at[me_c, rows, lanes], y_send.at[k], y_recv.at[k], {"cols": across})
        )

    def send_turn(t):
        lanes = pl.ds(*turns[t])
        k = PARTS + t
        y_copies.append(
            remote(turned.at[me_c, lanes], turned.at[me_c, lanes], y_send.at[k], y_recv.at[k], {"cols": across})
        )

    for k in range(AHEAD):
        send_part(k)
    half_copy = remote(panel, block.at[me_c], half_send.at[0], half_recv.at[0], {"cols": partner})

    def add_cross(source):
        def step(i, carry):
            rows = pl.ds(pl.multiple_of(i * chunk, chunk), chunk)
            long = pl.ds(pl.multiple_of(source * depth + i * chunk, chunk), chunk)
            cross[...] += dot_t(block[source, rows, :], trail[long, :])
            return carry

        lax.fori_loop(0, CHUNKS, step, 0)

    def add_part(source, k):
        rows = pl.ds(k * deep, deep)
        long = pl.ds(pl.multiple_of(source * depth + k * deep, deep), deep)
        cross[pl.ds(0, hw), :] += dot_t(block[source, rows, pl.ds(0, hw)], trail[long, :])

    def add_turn(source, t):
        first, count = turns[t]
        long = pl.ds(pl.multiple_of(source * depth, depth), depth)
        cross[pl.ds(hw + first, count), :] += dot3(turned[source, pl.ds(first, count), :], trail[long, :])

    def turn(source, back):
        def step(i, carry):
            rows = pl.ds(pl.multiple_of(i * hw, hw), hw)
            if back:
                block[source, rows, pl.ds(hw, hw)] = turned[source, :, rows].T
            else:
                turned[source, :, rows] = block[source, rows, pl.ds(hw, hw)].T
            return carry

        lax.fori_loop(0, depth // hw, step, 0)

    load_panel.wait()
    gram[...] = jnp.zeros_like(gram)

    def gram_step(i, carry):
        rows = block[me_c, pl.ds(pl.multiple_of(i * chunk, chunk), chunk), :]
        gram[...] += dot_t(rows, rows)
        return carry

    lax.fori_loop(0, CHUNKS, gram_step, 0)

    def scatter(total, stage, send, recv, piece):
        copies = []
        for d in range(1, nr):
            peer = lax.rem(me_r + d, nr)
            rows = pl.ds(pl.multiple_of(peer * piece, piece), piece)
            copies.append(remote(total.at[rows], stage.at[d], send.at[d], recv.at[d], {"rows": peer}))
        return copies

    def gather(total, send, recv, piece):
        rows = pl.ds(pl.multiple_of(me_r * piece, piece), piece)
        return [
            remote(total.at[rows], total.at[rows], send.at[d], recv.at[d], {"rows": lax.rem(me_r + d, nr)})
            for d in range(1, nr)
        ]

    def arrived(copies):
        for copy in copies:
            copy.wait_recv()

    def summed(total, stage, piece):
        value = total[pl.ds(pl.multiple_of(me_r * piece, piece), piece), :]
        for d in range(1, nr):
            value = value + stage[d]
        return value

    gram_rs = scatter(gram, gram_stage, rs_send, rs_recv, piece)
    turn(me_c, False)
    load_trail.wait()
    cross[...] = jnp.zeros_like(cross)
    add_cross(me_c)
    arrived(gram_rs)
    col_stage[me_c] = summed(gram, gram_stage, piece)
    exchange = [
        remote(col_stage.at[me_c], col_stage.at[me_c], cx_send.at[d], cx_recv.at[d], {"cols": lax.rem(me_c + d, nc)})
        for d in range(1, nc)
    ]
    for k in range(AHEAD, PARTS):
        send_part(k)
    for t in range(len(turns)):
        send_turn(t)
    half_copy.wait_recv()
    add_cross(partner)

    forwards = {}

    def take(k):
        y_copies[k].wait_recv()
        if k < PARTS:
            part = block.at[across, pl.ds(k * deep, deep), pl.ds(0, hw)]
        else:
            part = turned.at[across, pl.ds(*turns[k - PARTS])]
        forwards[k] = remote(part, part, fwd_send.at[k], fwd_recv.at[k], {"cols": partner})
        if k < PARTS:
            add_part(across, k)
        else:
            add_turn(across, k - PARTS)

    def take_forward(k):
        forwards[k].wait_recv()
        if k < PARTS:
            add_part(behind, k)
        else:
            add_turn(behind, k - PARTS)

    bounds = ((0, hw), (hw, 2 * quarter))
    stages = (early_stage, next_stage)
    scatters, gathers, lates = {}, {}, {}

    def start_cross(g):
        first, count = bounds[g]
        scatters[g] = scatter(cross.at[pl.ds(first, count)], stages[g], xrs_send.at[g], xrs_recv.at[g], count // nr)

    def share_cross(g):
        first, count = bounds[g]
        arrived(scatters[g])
        p = count // nr
        total = cross_sum.at[pl.ds(first, count)]
        total[pl.ds(pl.multiple_of(me_r * p, p), p), :] = summed(cross.at[pl.ds(first, count)], stages[g], p)
        gathers[g] = gather(total, xag_send.at[g], xag_recv.at[g], p)

    late_first = 2 * quarter

    def spread(t):
        first, count = turns[t]
        mine = late_stage.at[me_r, pl.ds(first - late_first, count)]
        mine[...] = cross[pl.ds(hw + first, count), :]
        lates[t] = [
            remote(mine, mine, late_send.at[t, d], late_recv.at[t, d], {"rows": lax.rem(me_r + d, nr)})
            for d in range(1, nr)
        ]

    take(0)
    take_forward(0)
    take(1)
    arrived(exchange)
    value = col_stage[0]
    for c in range(1, nc):
        value = value + col_stage[c]
    gram_sum[pl.ds(pl.multiple_of(me_r * piece, piece), piece), :] = value
    gram_ag = gather(gram_sum, ag_send, ag_recv, piece)
    take_forward(1)
    arrived(gram_ag)
    work[...] = gram_sum[pl.ds(0, hw), pl.ds(0, hw)]
    minv[...] = unit(hw)
    eliminate(work, minv, 0, quarter)
    take(2)
    eliminate(work, minv, quarter, 2 * quarter)
    take_forward(2)
    eliminate(work, minv, 2 * quarter, hw)
    take(3)
    upper1, inverse1 = scale_rows(work, minv)
    cross1 = dot(inverse1, gram_sum[pl.ds(0, hw), pl.ds(hw, hw)])
    upper_out[pl.ds(0, hw), pl.ds(0, hw)] = upper1
    upper_out[pl.ds(0, hw), pl.ds(hw, hw)] = cross1
    upper_out[pl.ds(hw, hw), pl.ds(0, hw)] = jnp.zeros_like(upper1)
    work[...] = gram_sum[pl.ds(hw, hw), pl.ds(hw, hw)] - dot_t(cross1, cross1)
    inv[pl.ds(0, hw), pl.ds(0, hw)] = inverse1
    minv[...] = unit(hw)
    take_forward(3)
    start_cross(0)
    eliminate(work, minv, 0, 2 * quarter)
    take(PARTS)
    take_forward(PARTS)
    eliminate(work, minv, 2 * quarter, hw)
    share_cross(0)
    upper2, inverse2 = scale_rows(work, minv)
    upper_out[pl.ds(hw, hw), pl.ds(hw, hw)] = upper2
    inverse1 = inv[pl.ds(0, hw), pl.ds(0, hw)]
    corner = -dot(inverse2, dot_t(upper_out[pl.ds(0, hw), pl.ds(hw, hw)], inverse1))
    inv[pl.ds(0, hw), pl.ds(hw, hw)] = jnp.zeros_like(inverse1)
    inv[pl.ds(hw, hw), pl.ds(0, hw)] = corner
    inv[pl.ds(hw, hw), pl.ds(hw, hw)] = inverse2
    inverse = inv[...]
    square[...] = dot_t(inverse, inverse)
    take(PARTS + 1)
    take_forward(PARTS + 1)
    start_cross(1)
    arrived(gathers[0])
    part = cross_sum[pl.ds(0, hw), :]
    coupling_out[...] = dot(inv[:, :hw], part)
    weights_out[...] = dot(square[:, :hw], part)
    take(PARTS + 2)
    share_cross(1)
    take_forward(PARTS + 2)
    spread(2)
    for t in range(3, len(turns)):
        take(PARTS + t)
        take_forward(PARTS + t)
        spread(t)
    turn(across, True)
    turn(behind, True)
    arrived(gathers[1])
    part = cross_sum[pl.ds(hw, late_first), :]
    coupling_out[...] += dot(inv[:, hw : hw + late_first], part)
    weights_out[...] += dot(square[:, hw : hw + late_first], part)
    for t in range(2, len(turns)):
        arrived(lates[t])
    part = late_stage[0]
    for r in range(1, nr):
        part = part + late_stage[r]
    weights_out[...] += dot(square[:, hw + late_first :], part)
    coupling_out[...] += dot(inv[:, hw + late_first :], part)
    for copy in sends:
        copy.wait_send()


def update_kernel(
    shrink, block, trailing, upper, coupling, weights, r_factor, r_cross, updated,
    small, w_hi, w_lo, out, small_sem, out_sem,
):
    small[0] = upper[...] * shrink
    small[1] = coupling[...] * shrink
    copies = [
        pltpu.make_async_copy(small.at[0], r_factor, small_sem.at[0]),
        pltpu.make_async_copy(small.at[1], r_cross, small_sem.at[1]),
    ]
    for copy in copies:
        copy.start()
    w = weights[...]
    high = w.astype(jnp.bfloat16)
    w_hi[...] = high
    w_lo[...] = (w - high.astype(jnp.float32)).astype(jnp.bfloat16)
    tile = out.shape[0] // TILES

    def mul(left, right):
        return jnp.dot(left, right, preferred_element_type=jnp.float32)

    def window(i):
        return pl.ds(pl.multiple_of(i * tile, tile), tile)

    def store(i):
        return pltpu.make_async_copy(out.at[window(i)], updated.at[window(i)], out_sem.at[i])

    def step(i, carry):
        rows = window(i)
        p = block[rows, :]
        p_hi = p.astype(jnp.bfloat16)
        p_lo = (p - p_hi.astype(jnp.float32)).astype(jnp.bfloat16)
        product = mul(p_hi, w_hi[...]) + (mul(p_lo, w_hi[...]) + mul(p_hi, w_lo[...]))
        out[rows, :] = trailing[rows, :] - product
        store(i).start()
        return carry

    lax.fori_loop(0, TILES, step, 0)
    for i in range(TILES):
        store(i).wait()
    for copy in copies:
        copy.wait()


def local(nr, nc, panel_cols, trailing):
    depth, width = panel_cols.shape
    rows, cols = trailing.shape
    half = nc // 2
    piece = width // nr
    groups = 2 if width % (2 * 8 * nr) == 0 else 1
    wide = width // groups
    f32 = jnp.float32
    square = jax.ShapeDtypeStruct((width, width), f32)
    tall = jax.ShapeDtypeStruct((width, cols), f32)
    dma = pltpu.SemaphoreType.DMA
    vmem = pl.BlockSpec(memory_space=pltpu.VMEM)
    hbm = pl.BlockSpec(memory_space=pltpu.HBM)
    fine = nc == 4 and width % 256 == 0 and (width // 4) % (8 * nr) == 0 and depth % (width // 2) == 0
    if fine:
        body, quarter, turns = transposed_kernel, width // 8, len(turn_plan(width))
        cross_scratch = [
            pltpu.VMEM((width, cols), f32),
            pltpu.VMEM((nr, width // 2 // nr, cols), f32),
            pltpu.VMEM((nr, width // 4 // nr, cols), f32),
            pltpu.VMEM((nr, width // 4, cols), f32),
            pltpu.VMEM((width, cols), f32),
            pltpu.VMEM((nc, width // 2, depth), f32),
        ]
        items, extra = PARTS + turns, [dma((turns, nr)), dma((turns, nr))]
        groups, forwards = 2, PARTS + turns
    else:
        body, items, forwards, extra = factor_kernel, ITEMS, ITEMS * half, []
        cross_scratch = [
            pltpu.VMEM((groups, wide, cols), f32),
            pltpu.VMEM((groups, nr, wide // nr, cols), f32),
            pltpu.VMEM((groups, wide, cols), f32),
        ]
    block, trail, upper, coupling, weights = pl.pallas_call(
        functools.partial(body, nr, nc),
        out_shape=(jax.ShapeDtypeStruct((nc, depth, width), f32), jax.ShapeDtypeStruct((rows, cols), f32), square, tall, tall),
        in_specs=[hbm, hbm],
        out_specs=(vmem,) * 5,
        scratch_shapes=[
            pltpu.VMEM((width, width), f32),
            pltpu.VMEM((nr, piece, width), f32),
            pltpu.VMEM((nc, piece, width), f32),
            pltpu.VMEM((width, width), f32),
            *cross_scratch,
            pltpu.VMEM((width // 2, width // 2), f32),
            pltpu.VMEM((width // 2, width // 2), f32),
            pltpu.VMEM((width, width), f32),
            pltpu.VMEM((width, width), f32),
            dma((2,)),
            dma((items,)), dma((items,)),
            dma((half,)), dma((half,)),
            dma((forwards,)), dma((forwards,)),
            dma((nr,)), dma((nr,)),
            dma((nc,)), dma((nc,)),
            dma((nr,)), dma((nr,)),
            dma((groups, nr)), dma((groups, nr)),
            dma((groups, nr)), dma((groups, nr)),
            *extra,
        ],
        compiler_params=pltpu.CompilerParams(
            collective_id=0, has_side_effects=True, vmem_limit_bytes=(32 if fine else 20) * 1024 * 1024
        ),
        name="factor",
    )(*(pltpu.with_memory_space_constraint(x, pltpu.HBM) for x in (panel_cols, trailing)))

    shrink = 1.0 / math.sqrt(rows * nr)
    r_factor, r_cross, updated = pl.pallas_call(
        functools.partial(update_kernel, shrink),
        out_shape=(square, tall, jax.ShapeDtypeStruct((rows, cols), f32)),
        in_specs=[vmem] * 5,
        out_specs=(hbm,) * 3,
        scratch_shapes=[
            pltpu.VMEM((2, width, cols), f32),
            pltpu.VMEM((width, cols), jnp.bfloat16),
            pltpu.VMEM((width, cols), jnp.bfloat16),
            pltpu.VMEM((rows, cols), f32),
            dma((2,)),
            dma((TILES,)),
        ],
        compiler_params=pltpu.CompilerParams(vmem_limit_bytes=24 * 1024 * 1024),
        name="update",
    )(block.reshape(rows, width), trail, upper, coupling, weights)
    return r_factor, r_cross, updated


def solution(mesh):
    P = jax.sharding.PartitionSpec
    body = functools.partial(local, mesh.shape["rows"], mesh.shape["cols"])
    in_specs = (P(("rows", "cols"), None), P("rows", "cols"))
    out_specs = (P(), P(None, "cols"), P("rows", "cols"))
    return jax.shard_map(body, mesh=mesh, in_specs=in_specs, out_specs=out_specs, check_vma=False)
```

```python
import functools
import math

import jax
import jax.numpy as jnp
from jax import lax
from jax.experimental import pallas as pl
from jax.experimental.pallas import tpu as pltpu

MESH = pl.DeviceIdType.MESH
HIGHEST = lax.Precision.HIGHEST
CHUNKS = 8
ITEMS = 8
EARLY = 3
MORE = (1, 1, 1, 0, 1, 0, 1, 0)
GROUP = 4
TILES = 8
AHEAD = 1


def dot(left, right):
    return lax.dot_general(left, right, (((1,), (0,)), ((), ())), precision=HIGHEST, preferred_element_type=jnp.float32)


def dot_t(left, right):
    return lax.dot_general(left, right, (((0,), (0,)), ((), ())), precision=HIGHEST, preferred_element_type=jnp.float32)


def split(x):
    high = x.astype(jnp.bfloat16)
    return high, (x - high.astype(jnp.float32)).astype(jnp.bfloat16)


def mul(left, right):
    return jnp.dot(left, right, preferred_element_type=jnp.float32)


def dot3(left, right):
    left_hi, left_lo = split(left)
    right_hi, right_lo = split(right)
    count = left.shape[0]
    both = mul(jnp.concatenate([left_hi, left_lo], axis=0), right_hi)
    return both[:count] + (both[count:] + mul(left_hi, right_lo))


def turn_plan(width):
    eighth = width // 8
    counts = (eighth,) * 7 + (eighth // 2,) * 2
    return [(sum(counts[:t]), counts[t]) for t in range(len(counts))]


def eliminate(a_ref, m_ref, first, last):
    size = a_ref.shape[0]
    sub = lax.broadcasted_iota(jnp.int32, (size, 1), 0)
    lane = lax.broadcasted_iota(jnp.int32, (size, size), 1)
    lane_row = lax.broadcasted_iota(jnp.int32, (1, size), 1)

    def step(index, carry):
        j = index * GROUP
        a = a_ref[...]
        rows = [a_ref[pl.ds(j + t, 1), :] for t in range(GROUP)]
        mrows = [m_ref[pl.ds(j + t, 1), :] for t in range(GROUP)]
        cols = [jnp.sum(jnp.where(lane == j + t, a, 0.0), axis=1, keepdims=True) for t in range(GROUP)]
        head = {
            (t, u): jnp.sum(jnp.where(lane_row == j + u, rows[t], 0.0), axis=1, keepdims=True)
            for t in range(GROUP)
            for u in range(t, GROUP)
        }
        m = m_ref[...]
        for t in range(GROUP):
            inverse = 1.0 / head[t, t]
            factor = jnp.where(sub > j + t, cols[t] * inverse, 0.0)
            ratio = {u: head[t, u] * inverse for u in range(t + 1, GROUP)}
            for u in range(t + 1, GROUP):
                cols[u] = cols[u] - factor * head[t, u]
            for u in range(t + 1, GROUP):
                for v in range(u, GROUP):
                    head[u, v] = head[u, v] - ratio[u] * head[t, v]
            for u in range(t + 1, GROUP):
                rows[u] = rows[u] - ratio[u] * rows[t]
                mrows[u] = mrows[u] - ratio[u] * mrows[t]
            a = a - factor * rows[t]
            m = m - factor * mrows[t]
        a_ref[...] = a
        m_ref[...] = m
        return carry

    lax.fori_loop(first // GROUP, last // GROUP, step, 0)


def scale_rows(a_ref, m_ref):
    size = a_ref.shape[0]
    sub = lax.broadcasted_iota(jnp.int32, (size, size), 0)
    lane = lax.broadcasted_iota(jnp.int32, (size, size), 1)
    a = a_ref[...]
    diagonal = jnp.sum(jnp.where(lane == sub, a, 0.0), axis=1, keepdims=True)
    scale = 1.0 / jnp.sqrt(diagonal)
    return jnp.where(lane >= sub, a * scale, 0.0), m_ref[...] * scale


def unit(size):
    sub = lax.broadcasted_iota(jnp.int32, (size, size), 0)
    lane = lax.broadcasted_iota(jnp.int32, (size, size), 1)
    return jnp.where(lane == sub, 1.0, 0.0).astype(jnp.float32)


def factor_kernel(
    nr, nc,
    panel, trailing, block, trail, upper_out, coupling_out, weights_out,
    gram, gram_stage, col_stage, gram_sum, cross, cross_stage, cross_sum, work, minv, inv, square,
    load_sem, y_send, y_recv, half_send, half_recv, fwd_send, fwd_recv,
    rs_send, rs_recv, cx_send, cx_recv, ag_send, ag_recv, xrs_send, xrs_recv, xag_send, xag_recv,
):
    me_r, me_c = lax.axis_index("rows"), lax.axis_index("cols")
    depth, width = panel.shape
    half = nc // 2
    side, place = me_c // half, lax.rem(me_c, half)
    across = lax.rem(me_c + half, nc)
    chunk = depth // CHUNKS
    piece = width // nr
    groups = cross.shape[0]
    per_group = ITEMS // groups
    deep = depth // per_group
    wide = width // groups
    cross_piece = wide // nr
    hw = width // 2
    sends = []

    def remote(src, dst, send, recv, where):
        copy = pltpu.make_async_remote_copy(
            src_ref=src, dst_ref=dst, send_sem=send, recv_sem=recv, device_id=where, device_id_type=MESH
        )
        copy.start()
        sends.append(copy)
        return copy

    load_panel = pltpu.make_async_copy(panel, block.at[me_c], load_sem.at[0])
    load_panel.start()
    load_trail = pltpu.make_async_copy(trailing, trail, load_sem.at[1])
    load_trail.start()

    barrier = pltpu.get_barrier_semaphore()
    for d in range(1, nr):
        pl.semaphore_signal(barrier, inc=1, device_id={"rows": lax.rem(me_r + d, nr)}, device_id_type=MESH)
    for d in range(1, nc):
        pl.semaphore_signal(barrier, inc=1, device_id={"cols": lax.rem(me_c + d, nc)}, device_id_type=MESH)
    pl.semaphore_wait(barrier, nr + nc - 2)

    def item(k):
        return pl.ds((k % per_group) * deep, deep), pl.ds((k // per_group) * wide, wide)

    y_copies = []

    def send_across(k):
        rows, lanes = item(k)
        y_copies.append(
            remote(panel.at[rows, lanes], block.at[me_c, rows, lanes], y_send.at[k], y_recv.at[k], {"cols": across})
        )

    for k in range(EARLY):
        send_across(k)
    half_copies = []
    for d in range(1, half):
        peer = side * half + lax.rem(place + d, half)
        half_copies.append(remote(panel, block.at[me_c], half_send.at[d], half_recv.at[d], {"cols": peer}))

    def add_cross(source):
        def step(i, carry):
            rows = pl.ds(pl.multiple_of(i * chunk, chunk), chunk)
            long = pl.ds(pl.multiple_of(source * depth + i * chunk, chunk), chunk)
            product = dot_t(block[source, rows, :], trail[long, :])
            for g in range(groups):
                cross[g] += product[g * wide : (g + 1) * wide, :]
            return carry

        lax.fori_loop(0, CHUNKS, step, 0)

    def add_item(source, k):
        rows, lanes = item(k)
        long = pl.ds(pl.multiple_of(source * depth + (k % per_group) * deep, deep), deep)
        cross[k // per_group] += dot_t(block[source, rows, lanes], trail[long, :])

    load_panel.wait()
    gram[...] = jnp.zeros_like(gram)

    def gram_step(i, carry):
        rows = block[me_c, pl.ds(pl.multiple_of(i * chunk, chunk), chunk), :]
        gram[...] += dot_t(rows, rows)
        return carry

    lax.fori_loop(0, CHUNKS, gram_step, 0)

    def scatter(total, stage, send, recv, piece=piece):
        copies = []
        for d in range(1, nr):
            peer = lax.rem(me_r + d, nr)
            rows = pl.ds(pl.multiple_of(peer * piece, piece), piece)
            copies.append(remote(total.at[rows], stage.at[d], send.at[d], recv.at[d], {"rows": peer}))
        return copies

    def gather(total, send, recv, piece=piece):
        rows = pl.ds(pl.multiple_of(me_r * piece, piece), piece)
        return [
            remote(total.at[rows], total.at[rows], send.at[d], recv.at[d], {"rows": lax.rem(me_r + d, nr)})
            for d in range(1, nr)
        ]

    def arrived(copies):
        for copy in copies:
            copy.wait_recv()

    mine = pl.ds(pl.multiple_of(me_r * piece, piece), piece)
    cross_mine = pl.ds(pl.multiple_of(me_r * cross_piece, cross_piece), cross_piece)

    def summed(total, stage, mine=mine):
        value = total[mine, :]
        for d in range(1, nr):
            value = value + stage[d]
        return value

    gram_rs = scatter(gram, gram_stage, rs_send, rs_recv)
    load_trail.wait()
    cross[...] = jnp.zeros_like(cross)
    add_cross(me_c)
    arrived(gram_rs)
    col_stage[me_c] = summed(gram, gram_stage)
    exchange = [
        remote(col_stage.at[me_c], col_stage.at[me_c], cx_send.at[d], cx_recv.at[d], {"cols": lax.rem(me_c + d, nc)})
        for d in range(1, nc)
    ]
    for k in range(EARLY, ITEMS):
        send_across(k)
    for d in range(1, half):
        half_copies[d - 1].wait_recv()
        source = side * half + lax.rem(place + half - d, half)
        add_cross(source)
    arrived(exchange)
    value = col_stage[0]
    for c in range(1, nc):
        value = value + col_stage[c]
    gram_sum[mine, :] = value
    gram_ag = gather(gram_sum, ag_send, ag_recv)

    forwards = {}

    def take(k):
        y_copies[k].wait_recv()
        rows, lanes = item(k)
        for d in range(1, half):
            peer = side * half + lax.rem(place + d, half)
            slot = (d - 1) * ITEMS + k
            part = block.at[across, rows, lanes]
            forwards[d, k] = remote(part, part, fwd_send.at[slot], fwd_recv.at[slot], {"cols": peer})
        add_item(across, k)

    def take_forward(k):
        for d in range(1, half):
            forwards[d, k].wait_recv()
            source = (1 - side) * half + lax.rem(place + half - d, half)
            add_item(source, k)

    cross_rs, cross_ag = {}, {}

    def start_cross(g):
        cross_rs[g] = scatter(cross.at[g], cross_stage.at[g], xrs_send.at[g], xrs_recv.at[g], cross_piece)

    def share_cross(g):
        arrived(cross_rs[g])
        cross_sum[g, cross_mine, :] = summed(cross.at[g], cross_stage.at[g], cross_mine)
        cross_ag[g] = gather(cross_sum.at[g], xag_send.at[g], xag_recv.at[g], cross_piece)

    pending = []
    for k in range(ITEMS):
        pending.append(([functools.partial(take_forward, k - 1)] if k % per_group else []) + [functools.partial(take, k)])
        if k % per_group == per_group - 1:
            pending[-1].append(functools.partial(take_forward, k))
            pending[-1].append(functools.partial(start_cross, k // per_group))
    for g in range(groups - 1):
        pending[(g + 1) * per_group + 2].append(functools.partial(share_cross, g))

    def advance():
        for task in pending.pop(0):
            task()

    def run(first, last, more):
        eliminate(work, minv, first, last)
        for _ in range(more):
            advance()

    for _ in range(EARLY):
        advance()
    arrived(gram_ag)
    work[...] = gram_sum[pl.ds(0, hw), pl.ds(0, hw)]
    minv[...] = unit(hw)
    quarter = hw // 4
    for q in range(4):
        run(q * quarter, (q + 1) * quarter, MORE[q])
    upper1, inverse1 = scale_rows(work, minv)
    cross1 = dot(inverse1, gram_sum[pl.ds(0, hw), pl.ds(hw, hw)])
    upper_out[pl.ds(0, hw), pl.ds(0, hw)] = upper1
    upper_out[pl.ds(0, hw), pl.ds(hw, hw)] = cross1
    upper_out[pl.ds(hw, hw), pl.ds(0, hw)] = jnp.zeros_like(upper1)
    work[...] = gram_sum[pl.ds(hw, hw), pl.ds(hw, hw)] - dot_t(cross1, cross1)
    inv[pl.ds(0, hw), pl.ds(0, hw)] = inverse1
    minv[...] = unit(hw)
    for q in range(4):
        run(q * quarter, (q + 1) * quarter, MORE[4 + q])
    upper2, inverse2 = scale_rows(work, minv)
    upper_out[pl.ds(hw, hw), pl.ds(hw, hw)] = upper2
    inverse1 = inv[pl.ds(0, hw), pl.ds(0, hw)]
    corner = -dot(inverse2, dot_t(upper_out[pl.ds(0, hw), pl.ds(hw, hw)], inverse1))
    inv[pl.ds(0, hw), pl.ds(hw, hw)] = jnp.zeros_like(inverse1)
    inv[pl.ds(hw, hw), pl.ds(0, hw)] = corner
    inv[pl.ds(hw, hw), pl.ds(hw, hw)] = inverse2
    while pending:
        advance()
    inverse = inv[...]
    square[...] = dot_t(inverse, inverse)
    last = slice((groups - 1) * wide, groups * wide)
    coupling_out[...] = jnp.zeros_like(coupling_out)
    weights_out[...] = jnp.zeros_like(weights_out)
    for g in range(groups - 1):
        arrived(cross_ag[g])
        part = cross_sum[g]
        coupling_out[...] += dot(inv[:, g * wide : (g + 1) * wide], part)
        weights_out[...] += dot(square[:, g * wide : (g + 1) * wide], part)
    share_cross(groups - 1)
    arrived(cross_ag[groups - 1])
    part = cross_sum[groups - 1]
    weights_out[...] += dot(square[:, last], part)
    coupling_out[...] += dot(inv[:, last], part)
    for copy in sends:
        copy.wait_send()


def transposed_kernel(
    nr, nc,
    panel, trailing, block, trail, upper_out, coupling_out, weights_out,
    gram, half_stage, half_sum, gram_stage, col_stage, gram_sum, cross, early_stage, next_stage, pair_stage, late_stage, cross_sum, turned,
    quad_stage, work, minv, inv, square,
    load_sem, bulk_sem, small_sem, y_recv, half_recv, fwd_recv, gram_recv, cross_recv,
):
    me_r, me_c = lax.axis_index("rows"), lax.axis_index("cols")
    depth, width = panel.shape
    side, place = me_c // 2, lax.rem(me_c, 2)
    partner = side * 2 + 1 - place
    across = (1 - side) * 2 + place
    behind = (1 - side) * 2 + 1 - place
    hw = width // 2
    piece = hw // nr
    head = depth // 8
    tall = depth - head
    turns = turn_plan(width)
    small_rows = []

    def remote(src, dst, send, recv, where):
        copy = pltpu.make_async_remote_copy(
            src_ref=src, dst_ref=dst, send_sem=send, recv_sem=recv, device_id=where, device_id_type=MESH
        )
        copy.start()
        return copy

    def small(src, dst, recv, where):
        small_rows.append(math.prod(src.shape) // width)
        return remote(src, dst, small_sem, recv, where)

    def drain(ref, sem):
        pltpu.make_async_copy(ref, ref, sem).wait()

    load_panel = pltpu.make_async_copy(panel, block.at[me_c], load_sem.at[0])
    load_panel.start()
    load_trail = pltpu.make_async_copy(trailing, trail, load_sem.at[1])
    load_trail.start()

    barrier = pltpu.get_barrier_semaphore()
    for d in range(1, nr):
        pl.semaphore_signal(barrier, inc=1, device_id={"rows": lax.rem(me_r + d, nr)}, device_id_type=MESH)
    for d in range(1, nc):
        pl.semaphore_signal(barrier, inc=1, device_id={"cols": lax.rem(me_c + d, nc)}, device_id_type=MESH)
    pl.semaphore_wait(barrier, nr + nc - 2)

    top = pl.ds(0, head)
    rest = pl.ds(head, tall)
    head_copy = remote(panel.at[top], block.at[me_c, top], bulk_sem, y_recv.at[0], {"cols": across})
    y_copies = []

    def send_turn():
        t = len(y_copies)
        part = turned.at[me_c, pl.ds(*turns[t]), rest]
        y_copies.append(remote(part, part, bulk_sem, y_recv.at[1 + t], {"cols": across}))

    load_panel.wait()
    cut = depth // 16

    def turn_step(i, carry):
        rows = pl.ds(pl.multiple_of(i * cut, cut), cut)
        turned[me_c, :, rows] = block[me_c, rows, :].T
        return carry

    lax.fori_loop(0, 16, turn_step, 0)
    for _ in range(AHEAD):
        send_turn()
    gram[...] = jnp.zeros_like(gram)
    step_rows = depth // 4

    def gram_step(i, carry):
        rows = pl.ds(pl.multiple_of(i * step_rows, step_rows), step_rows)
        gram[...] += dot(turned[me_c, :, rows], block[me_c, rows, :])
        return carry

    lax.fori_loop(0, 4, gram_step, 0)

    def scatter(total, stage, recv, where):
        for d in range(1, nr):
            peer = lax.rem(me_r + d, nr)
            small(total.at[where(peer)], stage.at[d], recv, {"rows": peer})

    def gather(total, recv, where):
        part = total.at[where(me_r)]
        for d in range(1, nr):
            small(part, part, recv, {"rows": lax.rem(me_r + d, nr)})

    def arrived(stage, recv):
        drain(stage.at[pl.ds(1, nr - 1)], recv)

    def summed(total, stage, where):
        value = total[where(me_r)]
        for d in range(1, nr):
            value = value + stage[d]
        return value

    def bands(count):
        return lambda peer: (pl.ds(pl.multiple_of(peer * count, count), count), slice(None))

    def tiles(count):
        half = cross.shape[1] // 2
        return lambda peer: (
            pl.ds(pl.multiple_of(peer // 2 * count, count), count),
            pl.ds(pl.multiple_of(lax.rem(peer, 2) * half, half), half),
        )

    def long(source, first, count):
        return pl.ds(pl.multiple_of(source * depth + first, head), count)

    def add_all(source):
        def step(i, carry):
            first = i * step_rows
            rows = pl.ds(pl.multiple_of(first, step_rows), step_rows)
            cross[...] += dot3(turned[source, :, rows], trail[long(source, first, step_rows), :])
            return carry

        lax.fori_loop(0, 4, step, 0)

    def add_head(source):
        cross[...] += dot_t(block[source, top, :], trail[long(source, 0, head), :])

    def add_lanes(source, first, count):
        lanes = pl.ds(first, count)
        cross[lanes, :] += dot3(turned[source, lanes, rest], trail[long(source, head, tall), :])

    def turn_back(source, first):
        lanes = pl.ds(first, hw)

        def step(i, carry):
            rows = pl.ds(pl.multiple_of(head + i * cut, cut), cut)
            block[source, rows, lanes] = turned[source, lanes, rows].T
            return carry

        lax.fori_loop(0, tall // cut, step, 0)

    mine = pl.ds(pl.multiple_of(place * hw, hw), hw)
    other = pl.ds(pl.multiple_of(hw - place * hw, hw), hw)
    gram_pair = small(gram.at[other], half_stage, gram_recv.at[0], {"cols": partner})
    turned_copy = remote(turned.at[me_c], turned.at[me_c], bulk_sem, half_recv.at[1], {"cols": partner})
    load_trail.wait()
    cross[...] = jnp.zeros_like(cross)
    add_all(me_c)
    gram_pair.wait_recv()
    half_sum[...] = gram[mine, :] + half_stage[...]
    scatter(half_sum, gram_stage, gram_recv.at[1], bands(piece))
    head_copy.wait_recv()
    part = block.at[across, top]
    head_forward = remote(part, part, bulk_sem, fwd_recv.at[0], {"cols": partner})
    add_head(across)
    turned_copy.wait_recv()
    add_all(partner)
    arrived(gram_stage, gram_recv.at[1])
    col_stage[side] = summed(half_sum, gram_stage, bands(piece))
    exchange = small(col_stage.at[side], col_stage.at[side], gram_recv.at[2], {"cols": across})
    while len(y_copies) < len(turns):
        send_turn()
    head_forward.wait_recv()
    add_head(behind)

    forwards = {}

    def take(t):
        y_copies[t].wait_recv()
        part = turned.at[across, pl.ds(*turns[t]), rest]
        forwards[t] = remote(part, part, bulk_sem, fwd_recv.at[1 + t], {"cols": partner})

    def take_forward(t):
        forwards[t].wait_recv()

    late_first = hw + hw // 2
    twin = me_r + 1 - 2 * lax.rem(me_r, 2)
    bounds = ((0, hw), (hw, hw // 2), turns[6])
    stages = (early_stage, next_stage, quad_stage)
    wheres = (bands(hw // nr), bands(hw // 2 // nr), tiles(turns[6][1] * 2 // nr))

    def start_cross(g):
        scatter(cross.at[pl.ds(*bounds[g])], stages[g], cross_recv.at[2 * g], wheres[g])

    def share_cross(g):
        arrived(stages[g], cross_recv.at[2 * g])
        total = cross_sum.at[pl.ds(*bounds[g])]
        total[wheres[g](me_r)] = summed(cross.at[pl.ds(*bounds[g])], stages[g], wheres[g])
        gather(total, cross_recv.at[2 * g + 1], wheres[g])

    def shared(g):
        arrived(stages[g], cross_recv.at[2 * g + 1])

    def lanes_of(t):
        first, count = turns[t]
        return pl.ds(first, count), pl.ds(first - late_first, count)

    def start_pair(t):
        lanes, late = lanes_of(t)
        mine = pair_stage.at[lax.rem(me_r, 2), late]
        mine[...] = cross[lanes, :]
        return small(mine, mine, cross_recv.at[6], {"rows": twin})

    def spread_pair(t, pair):
        _, late = lanes_of(t)
        pair.wait_recv()
        mine = late_stage.at[me_r, late]
        mine[...] = pair_stage[0, late, :] + pair_stage[1, late, :]
        for d in range(2, nr, 2):
            small(mine, mine, cross_recv.at[7], {"rows": lax.rem(me_r + d, nr)})

    def finish_pair(t):
        lanes, late = lanes_of(t)
        drain(late_stage.at[pl.ds(1, nr // 2 - 1), late], cross_recv.at[7])
        value = late_stage[lax.rem(me_r, 2), late, :]
        for step in range(2, nr, 2):
            value = value + late_stage[lax.rem(me_r, 2) + step, late, :]
        cross_sum[lanes, :] = value

    def spread(t):
        lanes, late = lanes_of(t)
        mine = late_stage.at[me_r, late]
        mine[...] = cross[lanes, :]
        for d in range(1, nr):
            small(mine, mine, cross_recv.at[8], {"rows": lax.rem(me_r + d, nr)})

    def finish(t):
        lanes, late = lanes_of(t)
        drain(late_stage.at[pl.ds(1, nr - 1), late], cross_recv.at[8])
        value = late_stage[0, late, :]
        for step in range(1, nr):
            value = value + late_stage[step, late, :]
        cross_sum[lanes, :] = value

    exchange.wait_recv()
    gram_half = gram_sum.at[mine]
    gram_half[pl.ds(pl.multiple_of(me_r * piece, piece), piece), :] = col_stage[0] + col_stage[1]
    gather(gram_half, gram_recv.at[3], bands(piece))
    take(0)
    arrived(gram_stage, gram_recv.at[3])
    gram_swap = small(gram_half, gram_half, gram_recv.at[4], {"cols": partner})
    half_copy = remote(panel, block.at[me_c], bulk_sem, half_recv.at[0], {"cols": partner})
    gram_swap.wait_recv()
    work[...] = gram_sum[pl.ds(0, hw), pl.ds(0, hw)]
    minv[...] = unit(hw)
    eighth = hw // 8
    take_forward(0)
    eliminate(work, minv, 0, 2 * eighth)
    take(1)
    eliminate(work, minv, 2 * eighth, 8 * eighth)
    take_forward(1)
    upper1, inverse1 = scale_rows(work, minv)
    cross1 = dot(inverse1, gram_sum[pl.ds(0, hw), pl.ds(hw, hw)])
    upper_out[pl.ds(0, hw), pl.ds(0, hw)] = upper1
    upper_out[pl.ds(0, hw), pl.ds(hw, hw)] = cross1
    upper_out[pl.ds(hw, hw), pl.ds(0, hw)] = jnp.zeros_like(upper1)
    work[...] = gram_sum[pl.ds(hw, hw), pl.ds(hw, hw)] - dot_t(cross1, cross1)
    inv[pl.ds(0, hw), pl.ds(0, hw)] = inverse1
    minv[...] = unit(hw)
    take(2)
    eliminate(work, minv, 0, 5 * eighth)
    take_forward(2)
    take(3)
    add_lanes(across, 0, hw)
    eliminate(work, minv, 5 * eighth, 6 * eighth)
    take_forward(3)
    add_lanes(behind, 0, hw)
    start_cross(0)
    eliminate(work, minv, 6 * eighth, 8 * eighth)
    take(4)
    upper2, inverse2 = scale_rows(work, minv)
    upper_out[pl.ds(hw, hw), pl.ds(hw, hw)] = upper2
    inverse1 = inv[pl.ds(0, hw), pl.ds(0, hw)]
    corner = -dot(inverse2, dot_t(upper_out[pl.ds(0, hw), pl.ds(hw, hw)], inverse1))
    inv[pl.ds(0, hw), pl.ds(hw, hw)] = jnp.zeros_like(inverse1)
    inv[pl.ds(hw, hw), pl.ds(0, hw)] = corner
    inv[pl.ds(hw, hw), pl.ds(hw, hw)] = inverse2
    inverse = inv[...]
    square[...] = dot_t(inverse, inverse)
    take_forward(4)
    turn_back(across, 0)
    turn_back(behind, 0)
    share_cross(0)
    take(5)
    add_lanes(across, hw, hw // 2)
    take_forward(5)
    add_lanes(behind, hw, hw // 2)
    start_cross(1)
    half_copy.wait_recv()
    shared(0)
    weights_out[...] = dot(square[:, :hw], cross_sum[pl.ds(0, hw), :])
    take(6)
    add_lanes(across, *turns[6])
    take_forward(6)
    add_lanes(behind, *turns[6])
    start_cross(2)
    share_cross(1)
    take(7)
    add_lanes(across, *turns[7])
    take_forward(7)
    add_lanes(behind, *turns[7])
    pair = start_pair(7)
    share_cross(2)
    take(8)
    add_lanes(across, *turns[8])
    take_forward(8)
    add_lanes(behind, *turns[8])
    spread(8)
    spread_pair(7, pair)
    turn_back(across, hw)
    turn_back(behind, hw)
    shared(1)
    shared(2)
    finish_pair(7)
    finish(8)
    weights_out[...] += dot3(square[:, hw:], cross_sum[pl.ds(hw, hw), :])
    coupling_out[...] = dot(inv[...], cross_sum[...])
    drain(turned, bulk_sem)
    total = sum(small_rows)
    drain(block.at[0, pl.ds(0, total)], small_sem)


def update_kernel(
    shrink, block, trailing, upper, coupling, weights, r_factor, r_cross, updated,
    small, w_hi, w_lo, out, small_sem, out_sem,
):
    small[0] = upper[...] * shrink
    small[1] = coupling[...] * shrink
    copies = [
        pltpu.make_async_copy(small.at[0], r_factor, small_sem.at[0]),
        pltpu.make_async_copy(small.at[1], r_cross, small_sem.at[1]),
    ]
    for copy in copies:
        copy.start()
    w = weights[...]
    high = w.astype(jnp.bfloat16)
    w_hi[...] = high
    w_lo[...] = (w - high.astype(jnp.float32)).astype(jnp.bfloat16)
    tile = out.shape[0] // TILES

    def mul(left, right):
        return jnp.dot(left, right, preferred_element_type=jnp.float32)

    def window(i):
        return pl.ds(pl.multiple_of(i * tile, tile), tile)

    def store(i):
        return pltpu.make_async_copy(out.at[window(i)], updated.at[window(i)], out_sem.at[i])

    def step(i, carry):
        rows = window(i)
        p = block[rows, :]
        p_hi = p.astype(jnp.bfloat16)
        p_lo = (p - p_hi.astype(jnp.float32)).astype(jnp.bfloat16)
        product = mul(p_hi, w_hi[...]) + (mul(p_lo, w_hi[...]) + mul(p_hi, w_lo[...]))
        out[rows, :] = trailing[rows, :] - product
        store(i).start()
        return carry

    lax.fori_loop(0, TILES, step, 0)
    for i in range(TILES):
        store(i).wait()
    for copy in copies:
        copy.wait()


def local(nr, nc, panel_cols, trailing):
    depth, width = panel_cols.shape
    rows, cols = trailing.shape
    half = nc // 2
    piece = width // nr
    groups = 2 if width % (2 * 8 * nr) == 0 else 1
    wide = width // groups
    f32 = jnp.float32
    square = jax.ShapeDtypeStruct((width, width), f32)
    tall = jax.ShapeDtypeStruct((width, cols), f32)
    dma = pltpu.SemaphoreType.DMA
    vmem = pl.BlockSpec(memory_space=pltpu.VMEM)
    hbm = pl.BlockSpec(memory_space=pltpu.HBM)
    fine = nc == 4 and nr % 2 == 0 and width % 256 == 0 and (width // 2) % (8 * nr) == 0 and (width // 4) % (8 * nr) == 0 and depth % 2048 == 0 and width // 8 == 4 * nr and cols % 256 == 0
    if fine:
        gram_scratch = [
            pltpu.VMEM((width // 2, width), f32),
            pltpu.VMEM((width // 2, width), f32),
            pltpu.VMEM((nr, piece // 2, width), f32),
            pltpu.VMEM((2, piece // 2, width), f32),
        ]
        body, turns = transposed_kernel, len(turn_plan(width))
        cross_scratch = [
            pltpu.VMEM((width, cols), f32),
            pltpu.VMEM((nr, width // 2 // nr, cols), f32),
            pltpu.VMEM((nr, width // 4 // nr, cols), f32),
            pltpu.VMEM((2, width // 4, cols), f32),
            pltpu.VMEM((nr, width // 4, cols), f32),
            pltpu.VMEM((width, cols), f32),
            pltpu.VMEM((nc, width, depth), f32),
        ]
        items, early = 1 + turns, [pltpu.VMEM((nr, width // 4 // nr, cols // 2), f32)]
        sems = [dma((2,)), dma, dma, dma((items,)), dma((2,)), dma((items,)), dma((5,)), dma((9,))]
    else:
        body, early = factor_kernel, []
        gram_scratch = [pltpu.VMEM((nr, piece, width), f32), pltpu.VMEM((nc, piece, width), f32)]
        sems = [
            dma((2,)),
            dma((ITEMS,)), dma((ITEMS,)),
            dma((half,)), dma((half,)),
            dma((ITEMS * half,)), dma((ITEMS * half,)),
            dma((nr,)), dma((nr,)),
            dma((nc,)), dma((nc,)),
            dma((nr,)), dma((nr,)),
            dma((groups, nr)), dma((groups, nr)),
            dma((groups, nr)), dma((groups, nr)),
        ]
        cross_scratch = [
            pltpu.VMEM((groups, wide, cols), f32),
            pltpu.VMEM((groups, nr, wide // nr, cols), f32),
            pltpu.VMEM((groups, wide, cols), f32),
        ]
    block, trail, upper, coupling, weights = pl.pallas_call(
        functools.partial(body, nr, nc),
        out_shape=(jax.ShapeDtypeStruct((nc, depth, width), f32), jax.ShapeDtypeStruct((rows, cols), f32), square, tall, tall),
        in_specs=[hbm, hbm],
        out_specs=(vmem,) * 5,
        scratch_shapes=[
            pltpu.VMEM((width, width), f32),
            *gram_scratch,
            pltpu.VMEM((width, width), f32),
            *cross_scratch,
            *early,
            pltpu.VMEM((width // 2, width // 2), f32),
            pltpu.VMEM((width // 2, width // 2), f32),
            pltpu.VMEM((width, width), f32),
            pltpu.VMEM((width, width), f32),
            *sems,
        ],
        compiler_params=pltpu.CompilerParams(
            collective_id=0, has_side_effects=True, vmem_limit_bytes=(32 if fine else 20) * 1024 * 1024
        ),
        name="factor",
    )(*(pltpu.with_memory_space_constraint(x, pltpu.HBM) for x in (panel_cols, trailing)))

    shrink = 1.0 / math.sqrt(rows * nr)
    r_factor, r_cross, updated = pl.pallas_call(
        functools.partial(update_kernel, shrink),
        out_shape=(square, tall, jax.ShapeDtypeStruct((rows, cols), f32)),
        in_specs=[vmem] * 5,
        out_specs=(hbm,) * 3,
        scratch_shapes=[
            pltpu.VMEM((2, width, cols), f32),
            pltpu.VMEM((width, cols), jnp.bfloat16),
            pltpu.VMEM((width, cols), jnp.bfloat16),
            pltpu.VMEM((rows, cols), f32),
            dma((2,)),
            dma((TILES,)),
        ],
        compiler_params=pltpu.CompilerParams(vmem_limit_bytes=24 * 1024 * 1024),
        name="update",
    )(block.reshape(rows, width), trail, upper, coupling, weights)
    return r_factor, r_cross, updated


def solution(mesh):
    P = jax.sharding.PartitionSpec
    body = functools.partial(local, mesh.shape["rows"], mesh.shape["cols"])
    in_specs = (P(("rows", "cols"), None), P("rows", "cols"))
    out_specs = (P(), P(None, "cols"), P("rows", "cols"))
    return jax.shard_map(body, mesh=mesh, in_specs=in_specs, out_specs=out_specs, check_vma=False)
```

```python
import functools
import math

import jax
import jax.numpy as jnp
from jax import lax
from jax.experimental import pallas as pl
from jax.experimental.pallas import tpu as pltpu

MESH = pl.DeviceIdType.MESH
HIGHEST = lax.Precision.HIGHEST
CHUNKS = 8
ITEMS = 8
EARLY = 3
MORE = (1, 1, 1, 0, 1, 0, 1, 0)
GROUP = 4
TILES = 8
AHEAD = 1


def dot(left, right):
    return lax.dot_general(left, right, (((1,), (0,)), ((), ())), precision=HIGHEST, preferred_element_type=jnp.float32)


def dot_t(left, right):
    return lax.dot_general(left, right, (((0,), (0,)), ((), ())), precision=HIGHEST, preferred_element_type=jnp.float32)


def split(x):
    high = x.astype(jnp.bfloat16)
    return high, (x - high.astype(jnp.float32)).astype(jnp.bfloat16)


def mul(left, right):
    return jnp.dot(left, right, preferred_element_type=jnp.float32)


def dot3(left, right):
    left_hi, left_lo = split(left)
    right_hi, right_lo = split(right)
    count = left.shape[0]
    both = mul(jnp.concatenate([left_hi, left_lo], axis=0), right_hi)
    return both[:count] + (both[count:] + mul(left_hi, right_lo))


def turn_plan(width):
    eighth = width // 8
    counts = (eighth,) * 7 + (eighth - eighth // 4, eighth // 4)
    return [(sum(counts[:t]), counts[t]) for t in range(len(counts))]


def eliminate(a_ref, m_ref, first, last):
    size = a_ref.shape[0]
    sub = lax.broadcasted_iota(jnp.int32, (size, 1), 0)
    lane = lax.broadcasted_iota(jnp.int32, (size, size), 1)
    lane_row = lax.broadcasted_iota(jnp.int32, (1, size), 1)

    def step(index, carry):
        j = index * GROUP
        a = a_ref[...]
        rows = [a_ref[pl.ds(j + t, 1), :] for t in range(GROUP)]
        mrows = [m_ref[pl.ds(j + t, 1), :] for t in range(GROUP)]
        cols = [jnp.sum(jnp.where(lane == j + t, a, 0.0), axis=1, keepdims=True) for t in range(GROUP)]
        head = {
            (t, u): jnp.sum(jnp.where(lane_row == j + u, rows[t], 0.0), axis=1, keepdims=True)
            for t in range(GROUP)
            for u in range(t, GROUP)
        }
        m = m_ref[...]
        for t in range(GROUP):
            inverse = 1.0 / head[t, t]
            factor = jnp.where(sub > j + t, cols[t] * inverse, 0.0)
            ratio = {u: head[t, u] * inverse for u in range(t + 1, GROUP)}
            for u in range(t + 1, GROUP):
                cols[u] = cols[u] - factor * head[t, u]
            for u in range(t + 1, GROUP):
                for v in range(u, GROUP):
                    head[u, v] = head[u, v] - ratio[u] * head[t, v]
            for u in range(t + 1, GROUP):
                rows[u] = rows[u] - ratio[u] * rows[t]
                mrows[u] = mrows[u] - ratio[u] * mrows[t]
            a = a - factor * rows[t]
            m = m - factor * mrows[t]
        a_ref[...] = a
        m_ref[...] = m
        return carry

    lax.fori_loop(first // GROUP, last // GROUP, step, 0)


def scale_rows(a_ref, m_ref):
    size = a_ref.shape[0]
    sub = lax.broadcasted_iota(jnp.int32, (size, size), 0)
    lane = lax.broadcasted_iota(jnp.int32, (size, size), 1)
    a = a_ref[...]
    diagonal = jnp.sum(jnp.where(lane == sub, a, 0.0), axis=1, keepdims=True)
    scale = 1.0 / jnp.sqrt(diagonal)
    return jnp.where(lane >= sub, a * scale, 0.0), m_ref[...] * scale


def unit(size):
    sub = lax.broadcasted_iota(jnp.int32, (size, size), 0)
    lane = lax.broadcasted_iota(jnp.int32, (size, size), 1)
    return jnp.where(lane == sub, 1.0, 0.0).astype(jnp.float32)


def factor_kernel(
    nr, nc,
    panel, trailing, block, trail, upper_out, coupling_out, weights_out,
    gram, gram_stage, col_stage, gram_sum, cross, cross_stage, cross_sum, work, minv, inv, square,
    load_sem, y_send, y_recv, half_send, half_recv, fwd_send, fwd_recv,
    rs_send, rs_recv, cx_send, cx_recv, ag_send, ag_recv, xrs_send, xrs_recv, xag_send, xag_recv,
):
    me_r, me_c = lax.axis_index("rows"), lax.axis_index("cols")
    depth, width = panel.shape
    half = nc // 2
    side, place = me_c // half, lax.rem(me_c, half)
    across = lax.rem(me_c + half, nc)
    chunk = depth // CHUNKS
    piece = width // nr
    groups = cross.shape[0]
    per_group = ITEMS // groups
    deep = depth // per_group
    wide = width // groups
    cross_piece = wide // nr
    hw = width // 2
    sends = []

    def remote(src, dst, send, recv, where):
        copy = pltpu.make_async_remote_copy(
            src_ref=src, dst_ref=dst, send_sem=send, recv_sem=recv, device_id=where, device_id_type=MESH
        )
        copy.start()
        sends.append(copy)
        return copy

    load_panel = pltpu.make_async_copy(panel, block.at[me_c], load_sem.at[0])
    load_panel.start()
    load_trail = pltpu.make_async_copy(trailing, trail, load_sem.at[1])
    load_trail.start()

    barrier = pltpu.get_barrier_semaphore()
    for d in range(1, nr):
        pl.semaphore_signal(barrier, inc=1, device_id={"rows": lax.rem(me_r + d, nr)}, device_id_type=MESH)
    for d in range(1, nc):
        pl.semaphore_signal(barrier, inc=1, device_id={"cols": lax.rem(me_c + d, nc)}, device_id_type=MESH)
    pl.semaphore_wait(barrier, nr + nc - 2)

    def item(k):
        return pl.ds((k % per_group) * deep, deep), pl.ds((k // per_group) * wide, wide)

    y_copies = []

    def send_across(k):
        rows, lanes = item(k)
        y_copies.append(
            remote(panel.at[rows, lanes], block.at[me_c, rows, lanes], y_send.at[k], y_recv.at[k], {"cols": across})
        )

    for k in range(EARLY):
        send_across(k)
    half_copies = []
    for d in range(1, half):
        peer = side * half + lax.rem(place + d, half)
        half_copies.append(remote(panel, block.at[me_c], half_send.at[d], half_recv.at[d], {"cols": peer}))

    def add_cross(source):
        def step(i, carry):
            rows = pl.ds(pl.multiple_of(i * chunk, chunk), chunk)
            long = pl.ds(pl.multiple_of(source * depth + i * chunk, chunk), chunk)
            product = dot_t(block[source, rows, :], trail[long, :])
            for g in range(groups):
                cross[g] += product[g * wide : (g + 1) * wide, :]
            return carry

        lax.fori_loop(0, CHUNKS, step, 0)

    def add_item(source, k):
        rows, lanes = item(k)
        long = pl.ds(pl.multiple_of(source * depth + (k % per_group) * deep, deep), deep)
        cross[k // per_group] += dot_t(block[source, rows, lanes], trail[long, :])

    load_panel.wait()
    gram[...] = jnp.zeros_like(gram)

    def gram_step(i, carry):
        rows = block[me_c, pl.ds(pl.multiple_of(i * chunk, chunk), chunk), :]
        gram[...] += dot_t(rows, rows)
        return carry

    lax.fori_loop(0, CHUNKS, gram_step, 0)

    def scatter(total, stage, send, recv, piece=piece):
        copies = []
        for d in range(1, nr):
            peer = lax.rem(me_r + d, nr)
            rows = pl.ds(pl.multiple_of(peer * piece, piece), piece)
            copies.append(remote(total.at[rows], stage.at[d], send.at[d], recv.at[d], {"rows": peer}))
        return copies

    def gather(total, send, recv, piece=piece):
        rows = pl.ds(pl.multiple_of(me_r * piece, piece), piece)
        return [
            remote(total.at[rows], total.at[rows], send.at[d], recv.at[d], {"rows": lax.rem(me_r + d, nr)})
            for d in range(1, nr)
        ]

    def arrived(copies):
        for copy in copies:
            copy.wait_recv()

    mine = pl.ds(pl.multiple_of(me_r * piece, piece), piece)
    cross_mine = pl.ds(pl.multiple_of(me_r * cross_piece, cross_piece), cross_piece)

    def summed(total, stage, mine=mine):
        value = total[mine, :]
        for d in range(1, nr):
            value = value + stage[d]
        return value

    gram_rs = scatter(gram, gram_stage, rs_send, rs_recv)
    load_trail.wait()
    cross[...] = jnp.zeros_like(cross)
    add_cross(me_c)
    arrived(gram_rs)
    col_stage[me_c] = summed(gram, gram_stage)
    exchange = [
        remote(col_stage.at[me_c], col_stage.at[me_c], cx_send.at[d], cx_recv.at[d], {"cols": lax.rem(me_c + d, nc)})
        for d in range(1, nc)
    ]
    for k in range(EARLY, ITEMS):
        send_across(k)
    for d in range(1, half):
        half_copies[d - 1].wait_recv()
        source = side * half + lax.rem(place + half - d, half)
        add_cross(source)
    arrived(exchange)
    value = col_stage[0]
    for c in range(1, nc):
        value = value + col_stage[c]
    gram_sum[mine, :] = value
    gram_ag = gather(gram_sum, ag_send, ag_recv)

    forwards = {}

    def take(k):
        y_copies[k].wait_recv()
        rows, lanes = item(k)
        for d in range(1, half):
            peer = side * half + lax.rem(place + d, half)
            slot = (d - 1) * ITEMS + k
            part = block.at[across, rows, lanes]
            forwards[d, k] = remote(part, part, fwd_send.at[slot], fwd_recv.at[slot], {"cols": peer})
        add_item(across, k)

    def take_forward(k):
        for d in range(1, half):
            forwards[d, k].wait_recv()
            source = (1 - side) * half + lax.rem(place + half - d, half)
            add_item(source, k)

    cross_rs, cross_ag = {}, {}

    def start_cross(g):
        cross_rs[g] = scatter(cross.at[g], cross_stage.at[g], xrs_send.at[g], xrs_recv.at[g], cross_piece)

    def share_cross(g):
        arrived(cross_rs[g])
        cross_sum[g, cross_mine, :] = summed(cross.at[g], cross_stage.at[g], cross_mine)
        cross_ag[g] = gather(cross_sum.at[g], xag_send.at[g], xag_recv.at[g], cross_piece)

    pending = []
    for k in range(ITEMS):
        pending.append(([functools.partial(take_forward, k - 1)] if k % per_group else []) + [functools.partial(take, k)])
        if k % per_group == per_group - 1:
            pending[-1].append(functools.partial(take_forward, k))
            pending[-1].append(functools.partial(start_cross, k // per_group))
    for g in range(groups - 1):
        pending[(g + 1) * per_group + 2].append(functools.partial(share_cross, g))

    def advance():
        for task in pending.pop(0):
            task()

    def run(first, last, more):
        eliminate(work, minv, first, last)
        for _ in range(more):
            advance()

    for _ in range(EARLY):
        advance()
    arrived(gram_ag)
    work[...] = gram_sum[pl.ds(0, hw), pl.ds(0, hw)]
    minv[...] = unit(hw)
    quarter = hw // 4
    for q in range(4):
        run(q * quarter, (q + 1) * quarter, MORE[q])
    upper1, inverse1 = scale_rows(work, minv)
    cross1 = dot(inverse1, gram_sum[pl.ds(0, hw), pl.ds(hw, hw)])
    upper_out[pl.ds(0, hw), pl.ds(0, hw)] = upper1
    upper_out[pl.ds(0, hw), pl.ds(hw, hw)] = cross1
    upper_out[pl.ds(hw, hw), pl.ds(0, hw)] = jnp.zeros_like(upper1)
    work[...] = gram_sum[pl.ds(hw, hw), pl.ds(hw, hw)] - dot_t(cross1, cross1)
    inv[pl.ds(0, hw), pl.ds(0, hw)] = inverse1
    minv[...] = unit(hw)
    for q in range(4):
        run(q * quarter, (q + 1) * quarter, MORE[4 + q])
    upper2, inverse2 = scale_rows(work, minv)
    upper_out[pl.ds(hw, hw), pl.ds(hw, hw)] = upper2
    inverse1 = inv[pl.ds(0, hw), pl.ds(0, hw)]
    corner = -dot(inverse2, dot_t(upper_out[pl.ds(0, hw), pl.ds(hw, hw)], inverse1))
    inv[pl.ds(0, hw), pl.ds(hw, hw)] = jnp.zeros_like(inverse1)
    inv[pl.ds(hw, hw), pl.ds(0, hw)] = corner
    inv[pl.ds(hw, hw), pl.ds(hw, hw)] = inverse2
    while pending:
        advance()
    inverse = inv[...]
    square[...] = dot_t(inverse, inverse)
    last = slice((groups - 1) * wide, groups * wide)
    coupling_out[...] = jnp.zeros_like(coupling_out)
    weights_out[...] = jnp.zeros_like(weights_out)
    for g in range(groups - 1):
        arrived(cross_ag[g])
        part = cross_sum[g]
        coupling_out[...] += dot(inv[:, g * wide : (g + 1) * wide], part)
        weights_out[...] += dot(square[:, g * wide : (g + 1) * wide], part)
    share_cross(groups - 1)
    arrived(cross_ag[groups - 1])
    part = cross_sum[groups - 1]
    weights_out[...] += dot(square[:, last], part)
    coupling_out[...] += dot(inv[:, last], part)
    for copy in sends:
        copy.wait_send()


def transposed_kernel(
    nr, nc,
    panel, trailing, block, trail, upper_out, coupling_out, weights_out, inv, cross_sum,
    gram, half_stage, half_sum, gram_stage, col_stage, gram_sum, cross, early_stage, tile_stage, pair_stage, late_stage, turned,
    work, minv, square,
    load_sem, bulk_sem, small_sem, y_recv, half_recv, fwd_recv, gram_recv, cross_recv,
):
    me_r, me_c = lax.axis_index("rows"), lax.axis_index("cols")
    depth, width = panel.shape
    side, place = me_c // 2, lax.rem(me_c, 2)
    partner = side * 2 + 1 - place
    across = (1 - side) * 2 + place
    behind = (1 - side) * 2 + 1 - place
    hw = width // 2
    piece = hw // nr
    head = depth // 8
    tall = depth - head
    turns = turn_plan(width)
    small_rows = []

    def remote(src, dst, send, recv, where):
        copy = pltpu.make_async_remote_copy(
            src_ref=src, dst_ref=dst, send_sem=send, recv_sem=recv, device_id=where, device_id_type=MESH
        )
        copy.start()
        return copy

    def small(src, dst, recv, where):
        small_rows.append(math.prod(src.shape) // width)
        return remote(src, dst, small_sem, recv, where)

    def drain(ref, sem):
        pltpu.make_async_copy(ref, ref, sem).wait()

    load_panel = pltpu.make_async_copy(panel, block.at[me_c], load_sem.at[0])
    load_panel.start()
    load_trail = pltpu.make_async_copy(trailing, trail, load_sem.at[1])
    load_trail.start()

    barrier = pltpu.get_barrier_semaphore()
    for d in range(1, nr):
        pl.semaphore_signal(barrier, inc=1, device_id={"rows": lax.rem(me_r + d, nr)}, device_id_type=MESH)
    for d in range(1, nc):
        pl.semaphore_signal(barrier, inc=1, device_id={"cols": lax.rem(me_c + d, nc)}, device_id_type=MESH)
    pl.semaphore_wait(barrier, nr + nc - 2)

    top = pl.ds(0, head)
    rest = pl.ds(head, tall)
    head_copy = remote(panel.at[top], block.at[me_c, top], bulk_sem, y_recv.at[0], {"cols": across})
    y_copies = []

    def send_turn():
        t = len(y_copies)
        part = turned.at[me_c, pl.ds(*turns[t]), rest]
        y_copies.append(remote(part, part, bulk_sem, y_recv.at[1 + t], {"cols": across}))

    load_panel.wait()
    cut = depth // 16

    def turn_step(i, carry):
        rows = pl.ds(pl.multiple_of(i * cut, cut), cut)
        turned[me_c, :, rows] = block[me_c, rows, :].T
        return carry

    lax.fori_loop(0, 16, turn_step, 0)
    for _ in range(AHEAD):
        send_turn()
    gram[...] = jnp.zeros_like(gram)
    step_rows = depth // 4

    def gram_step(i, carry):
        rows = pl.ds(pl.multiple_of(i * step_rows, step_rows), step_rows)
        gram[...] += dot(turned[me_c, :, rows], block[me_c, rows, :])
        return carry

    lax.fori_loop(0, 4, gram_step, 0)

    def scatter(total, stage, recv, where):
        for d in range(1, nr):
            peer = lax.rem(me_r + d, nr)
            small(total.at[where(peer)], stage.at[d], recv, {"rows": peer})

    def gather(total, recv, where):
        part = total.at[where(me_r)]
        for d in range(1, nr):
            small(part, part, recv, {"rows": lax.rem(me_r + d, nr)})

    def arrived(stage, recv):
        drain(stage.at[pl.ds(1, nr - 1)], recv)

    def summed(total, stage, where):
        value = total[where(me_r)]
        for d in range(1, nr):
            value = value + stage[d]
        return value

    def bands(count):
        return lambda peer: (pl.ds(pl.multiple_of(peer * count, count), count), slice(None))

    def tiles(count):
        half = cross.shape[1] // 2
        return lambda peer: (
            pl.ds(pl.multiple_of(peer // 2 * count, count), count),
            pl.ds(pl.multiple_of(lax.rem(peer, 2) * half, half), half),
        )

    def long(source, first, count):
        return pl.ds(pl.multiple_of(source * depth + first, head), count)

    def add_all(source):
        def step(i, carry):
            first = i * step_rows
            rows = pl.ds(pl.multiple_of(first, step_rows), step_rows)
            cross[...] += dot3(turned[source, :, rows], trail[long(source, first, step_rows), :])
            return carry

        lax.fori_loop(0, 4, step, 0)

    def add_head(source):
        cross[...] += dot_t(block[source, top, :], trail[long(source, 0, head), :])

    def add_lanes(source, first, count):
        lanes = pl.ds(first, count)
        cross[lanes, :] += dot3(turned[source, lanes, rest], trail[long(source, head, tall), :])

    def turn_back(source, first):
        lanes = pl.ds(first, hw)

        def step(i, carry):
            rows = pl.ds(pl.multiple_of(head + i * cut, cut), cut)
            block[source, rows, lanes] = turned[source, lanes, rows].T
            return carry

        lax.fori_loop(0, tall // cut, step, 0)

    mine = pl.ds(pl.multiple_of(place * hw, hw), hw)
    other = pl.ds(pl.multiple_of(hw - place * hw, hw), hw)
    gram_pair = small(gram.at[other], half_stage, gram_recv.at[0], {"cols": partner})
    turned_copy = remote(turned.at[me_c], turned.at[me_c], bulk_sem, half_recv.at[1], {"cols": partner})
    load_trail.wait()
    cross[...] = jnp.zeros_like(cross)
    add_all(me_c)
    gram_pair.wait_recv()
    half_sum[...] = gram[mine, :] + half_stage[...]
    scatter(half_sum, gram_stage, gram_recv.at[1], bands(piece))
    head_copy.wait_recv()
    part = block.at[across, top]
    head_forward = remote(part, part, bulk_sem, fwd_recv.at[0], {"cols": partner})
    add_head(across)
    turned_copy.wait_recv()
    add_all(partner)
    arrived(gram_stage, gram_recv.at[1])
    col_stage[side] = summed(half_sum, gram_stage, bands(piece))
    exchange = small(col_stage.at[side], col_stage.at[side], gram_recv.at[2], {"cols": across})
    while len(y_copies) < len(turns):
        send_turn()
    head_forward.wait_recv()
    add_head(behind)

    forwards = {}

    def take(t):
        y_copies[t].wait_recv()
        part = turned.at[across, pl.ds(*turns[t]), rest]
        forwards[t] = remote(part, part, bulk_sem, fwd_recv.at[1 + t], {"cols": partner})

    def take_forward(t):
        forwards[t].wait_recv()

    late_first = turns[7][0]
    twin = me_r + 1 - 2 * lax.rem(me_r, 2)
    bounds = ((0, hw), turns[4], turns[5], turns[6])
    stages = (early_stage, tile_stage.at[0], tile_stage.at[1], tile_stage.at[2])
    wheres = (bands(hw // nr),) + (tiles(turns[6][1] * 2 // nr),) * 3

    def start_cross(g):
        scatter(cross.at[pl.ds(*bounds[g])], stages[g], cross_recv.at[2 * g], wheres[g])

    def share_cross(g):
        arrived(stages[g], cross_recv.at[2 * g])
        total = cross_sum.at[pl.ds(*bounds[g])]
        total[wheres[g](me_r)] = summed(cross.at[pl.ds(*bounds[g])], stages[g], wheres[g])
        gather(total, cross_recv.at[2 * g + 1], wheres[g])

    def shared(g):
        arrived(stages[g], cross_recv.at[2 * g + 1])

    def lanes_of(t):
        first, count = turns[t]
        return pl.ds(first, count), pl.ds(first - late_first, count)

    def start_pair(t):
        lanes, late = lanes_of(t)
        mine = pair_stage.at[lax.rem(me_r, 2), late]
        mine[...] = cross[lanes, :]
        return small(mine, mine, cross_recv.at[8], {"rows": twin})

    def spread_pair(t, pair):
        _, late = lanes_of(t)
        pair.wait_recv()
        mine = late_stage.at[me_r, late]
        mine[...] = pair_stage[0, late, :] + pair_stage[1, late, :]
        for d in range(2, nr, 2):
            small(mine, mine, cross_recv.at[9], {"rows": lax.rem(me_r + d, nr)})

    def finish_pair(t):
        lanes, late = lanes_of(t)
        drain(late_stage.at[pl.ds(1, nr // 2 - 1), late], cross_recv.at[9])
        value = late_stage[lax.rem(me_r, 2), late, :]
        for step in range(2, nr, 2):
            value = value + late_stage[lax.rem(me_r, 2) + step, late, :]
        cross_sum[lanes, :] = value

    def spread(t):
        lanes, late = lanes_of(t)
        mine = late_stage.at[me_r, late]
        mine[...] = cross[lanes, :]
        for d in range(1, nr):
            small(mine, mine, cross_recv.at[10], {"rows": lax.rem(me_r + d, nr)})

    def finish(t):
        lanes, late = lanes_of(t)
        drain(late_stage.at[pl.ds(1, nr - 1), late], cross_recv.at[10])
        value = late_stage[0, late, :]
        for step in range(1, nr):
            value = value + late_stage[step, late, :]
        cross_sum[lanes, :] = value

    exchange.wait_recv()
    gram_half = gram_sum.at[mine]
    gram_half[pl.ds(pl.multiple_of(me_r * piece, piece), piece), :] = col_stage[0] + col_stage[1]
    gather(gram_half, gram_recv.at[3], bands(piece))
    take(0)
    arrived(gram_stage, gram_recv.at[3])
    gram_swap = small(gram_half, gram_half, gram_recv.at[4], {"cols": partner})
    half_copy = remote(panel, block.at[me_c], bulk_sem, half_recv.at[0], {"cols": partner})
    gram_swap.wait_recv()
    work[...] = gram_sum[pl.ds(0, hw), pl.ds(0, hw)]
    minv[...] = unit(hw)
    eighth = hw // 8
    take_forward(0)
    eliminate(work, minv, 0, 2 * eighth)
    take(1)
    eliminate(work, minv, 2 * eighth, 8 * eighth)
    take_forward(1)
    upper1, inverse1 = scale_rows(work, minv)
    cross1 = dot(inverse1, gram_sum[pl.ds(0, hw), pl.ds(hw, hw)])
    upper_out[pl.ds(0, hw), pl.ds(0, hw)] = upper1
    upper_out[pl.ds(0, hw), pl.ds(hw, hw)] = cross1
    upper_out[pl.ds(hw, hw), pl.ds(0, hw)] = jnp.zeros_like(upper1)
    work[...] = gram_sum[pl.ds(hw, hw), pl.ds(hw, hw)] - dot_t(cross1, cross1)
    inv[pl.ds(0, hw), pl.ds(0, hw)] = inverse1
    minv[...] = unit(hw)
    take(2)
    eliminate(work, minv, 0, 5 * eighth)
    take_forward(2)
    take(3)
    add_lanes(across, 0, hw)
    eliminate(work, minv, 5 * eighth, 6 * eighth)
    take_forward(3)
    add_lanes(behind, 0, hw)
    start_cross(0)
    eliminate(work, minv, 6 * eighth, 8 * eighth)
    take(4)
    upper2, inverse2 = scale_rows(work, minv)
    upper_out[pl.ds(hw, hw), pl.ds(hw, hw)] = upper2
    inverse1 = inv[pl.ds(0, hw), pl.ds(0, hw)]
    corner = -dot(inverse2, dot_t(upper_out[pl.ds(0, hw), pl.ds(hw, hw)], inverse1))
    inv[pl.ds(0, hw), pl.ds(hw, hw)] = jnp.zeros_like(inverse1)
    inv[pl.ds(hw, hw), pl.ds(0, hw)] = corner
    inv[pl.ds(hw, hw), pl.ds(hw, hw)] = inverse2
    inverse = inv[...]
    square[...] = dot_t(inverse, inverse)
    add_lanes(across, *turns[4])
    take_forward(4)
    add_lanes(behind, *turns[4])
    start_cross(1)
    turn_back(across, 0)
    share_cross(0)
    take(5)
    add_lanes(across, *turns[5])
    turn_back(behind, 0)
    take_forward(5)
    add_lanes(behind, *turns[5])
    start_cross(2)
    half_copy.wait_recv()
    share_cross(1)
    take(6)
    add_lanes(across, *turns[6])
    shared(0)
    weights_out[...] = dot(square[:, :hw], cross_sum[pl.ds(0, hw), :])
    coupling_out[...] = dot(inv[:, :hw], cross_sum[pl.ds(0, hw), :])
    take_forward(6)
    add_lanes(behind, *turns[6])
    start_cross(3)
    share_cross(2)
    take(7)
    add_lanes(across, *turns[7])
    take_forward(7)
    add_lanes(behind, *turns[7])
    pair = start_pair(7)
    take(8)
    add_lanes(across, *turns[8])
    take_forward(8)
    add_lanes(behind, *turns[8])
    spread(8)
    share_cross(3)
    spread_pair(7, pair)
    turn_back(across, hw)
    turn_back(behind, hw)
    shared(1)
    shared(2)
    shared(3)
    finish_pair(7)
    finish(8)
    weights_out[...] += dot3(square[:, hw:], cross_sum[pl.ds(hw, hw), :])
    drain(turned, bulk_sem)
    total = sum(small_rows)
    drain(block.at[0, pl.ds(0, total)], small_sem)


def update_kernel(
    shrink, block, trailing, upper, coupling, weights, r_factor, r_cross, updated,
    small, w_hi, w_lo, out, small_sem, out_sem,
):
    small[0] = upper[...] * shrink
    small[1] = coupling[...] * shrink
    copies = [
        pltpu.make_async_copy(small.at[0], r_factor, small_sem.at[0]),
        pltpu.make_async_copy(small.at[1], r_cross, small_sem.at[1]),
    ]
    for copy in copies:
        copy.start()
    w = weights[...]
    high = w.astype(jnp.bfloat16)
    w_hi[...] = high
    w_lo[...] = (w - high.astype(jnp.float32)).astype(jnp.bfloat16)
    tile = out.shape[0] // TILES

    def mul(left, right):
        return jnp.dot(left, right, preferred_element_type=jnp.float32)

    def window(i):
        return pl.ds(pl.multiple_of(i * tile, tile), tile)

    def store(i):
        return pltpu.make_async_copy(out.at[window(i)], updated.at[window(i)], out_sem.at[i])

    def step(i, carry):
        rows = window(i)
        p = block[rows, :]
        p_hi = p.astype(jnp.bfloat16)
        p_lo = (p - p_hi.astype(jnp.float32)).astype(jnp.bfloat16)
        product = mul(p_hi, w_hi[...]) + (mul(p_lo, w_hi[...]) + mul(p_hi, w_lo[...]))
        out[rows, :] = trailing[rows, :] - product
        store(i).start()
        return carry

    lax.fori_loop(0, TILES, step, 0)
    for i in range(TILES):
        store(i).wait()
    for copy in copies:
        copy.wait()


def finish_kernel(
    shrink, block, trailing, upper, coupling, weights, inv, total, r_factor, r_cross, updated,
    small, w_hi, w_lo, out, small_sem, out_sem,
):
    small[0] = upper[...] * shrink
    factor_copy = pltpu.make_async_copy(small.at[0], r_factor, small_sem.at[0])
    factor_copy.start()
    w_hi[...], w_lo[...] = split(weights[...])
    depth = out.shape[0]
    tile = depth // TILES
    first = 0
    for count in (tile // 2,) + (tile,) * (TILES - 1) + (tile // 2,):
        rows = pl.ds(first, count)
        p_hi, p_lo = split(block[rows, :])
        product = mul(p_hi, w_hi[...]) + (mul(p_lo, w_hi[...]) + mul(p_hi, w_lo[...]))
        out[rows, :] = trailing[rows, :] - product
        pltpu.make_async_copy(out.at[rows], updated.at[rows], out_sem).start()
        first += count
    hw = inv.shape[0] // 2
    small[1] = (coupling[...] + dot3(inv[:, hw:], total[hw:, :])) * shrink
    cross_copy = pltpu.make_async_copy(small.at[1], r_cross, small_sem.at[1])
    cross_copy.start()
    pltpu.make_async_copy(out, updated, out_sem).wait()
    factor_copy.wait()
    cross_copy.wait()


def local(nr, nc, panel_cols, trailing):
    depth, width = panel_cols.shape
    rows, cols = trailing.shape
    half = nc // 2
    piece = width // nr
    groups = 2 if width % (2 * 8 * nr) == 0 else 1
    wide = width // groups
    f32 = jnp.float32
    square = jax.ShapeDtypeStruct((width, width), f32)
    tall = jax.ShapeDtypeStruct((width, cols), f32)
    dma = pltpu.SemaphoreType.DMA
    vmem = pl.BlockSpec(memory_space=pltpu.VMEM)
    hbm = pl.BlockSpec(memory_space=pltpu.HBM)
    fine = nc == 4 and nr % 2 == 0 and width % 256 == 0 and (width // 2) % (8 * nr) == 0 and (width // 4) % (8 * nr) == 0 and depth % 2048 == 0 and width // 8 == 4 * nr and cols % 256 == 0
    if fine:
        gram_scratch = [
            pltpu.VMEM((width // 2, width), f32),
            pltpu.VMEM((width // 2, width), f32),
            pltpu.VMEM((nr, piece // 2, width), f32),
            pltpu.VMEM((2, piece // 2, width), f32),
        ]
        body, turns = transposed_kernel, len(turn_plan(width))
        cross_scratch = [
            pltpu.VMEM((width, cols), f32),
            pltpu.VMEM((nr, width // 2 // nr, cols), f32),
            pltpu.VMEM((3, nr, width // 4 // nr, cols // 2), f32),
            pltpu.VMEM((2, width // 4, cols), f32),
            pltpu.VMEM((nr, width // 4, cols), f32),
            pltpu.VMEM((nc, width, depth), f32),
        ]
        items = 1 + turns
        sems = [dma((2,)), dma, dma, dma((items,)), dma((2,)), dma((items,)), dma((5,)), dma((11,))]
    else:
        body = factor_kernel
        gram_scratch = [pltpu.VMEM((nr, piece, width), f32), pltpu.VMEM((nc, piece, width), f32)]
        sems = [
            dma((2,)),
            dma((ITEMS,)), dma((ITEMS,)),
            dma((half,)), dma((half,)),
            dma((ITEMS * half,)), dma((ITEMS * half,)),
            dma((nr,)), dma((nr,)),
            dma((nc,)), dma((nc,)),
            dma((nr,)), dma((nr,)),
            dma((groups, nr)), dma((groups, nr)),
            dma((groups, nr)), dma((groups, nr)),
        ]
        cross_scratch = [
            pltpu.VMEM((groups, wide, cols), f32),
            pltpu.VMEM((groups, nr, wide // nr, cols), f32),
            pltpu.VMEM((groups, wide, cols), f32),
        ]
    shapes = (jax.ShapeDtypeStruct((nc, depth, width), f32), jax.ShapeDtypeStruct((rows, cols), f32), square, tall, tall)
    shapes += (square, tall) if fine else ()
    block, *results = pl.pallas_call(
        functools.partial(body, nr, nc),
        out_shape=shapes,
        in_specs=[hbm, hbm],
        out_specs=(vmem,) * len(shapes),
        scratch_shapes=[
            pltpu.VMEM((width, width), f32),
            *gram_scratch,
            pltpu.VMEM((width, width), f32),
            *cross_scratch,
            pltpu.VMEM((width // 2, width // 2), f32),
            pltpu.VMEM((width // 2, width // 2), f32),
            *[pltpu.VMEM((width, width), f32)] * (1 if fine else 2),
            *sems,
        ],
        compiler_params=pltpu.CompilerParams(
            collective_id=0, has_side_effects=True, vmem_limit_bytes=(32 if fine else 20) * 1024 * 1024
        ),
        name="factor",
    )(*(pltpu.with_memory_space_constraint(x, pltpu.HBM) for x in (panel_cols, trailing)))

    shrink = 1.0 / math.sqrt(rows * nr)
    r_factor, r_cross, updated = pl.pallas_call(
        functools.partial(finish_kernel if fine else update_kernel, shrink),
        out_shape=(square, tall, jax.ShapeDtypeStruct((rows, cols), f32)),
        in_specs=[vmem] * len(shapes),
        out_specs=(hbm,) * 3,
        scratch_shapes=[
            pltpu.VMEM((2, width, cols), f32),
            pltpu.VMEM((width, cols), jnp.bfloat16),
            pltpu.VMEM((width, cols), jnp.bfloat16),
            pltpu.VMEM((rows, cols), f32),
            dma((2,)),
            dma if fine else dma((TILES,)),
        ],
        compiler_params=pltpu.CompilerParams(vmem_limit_bytes=24 * 1024 * 1024),
        name="update",
    )(block.reshape(rows, width), *results)
    return r_factor, r_cross, updated


def solution(mesh):
    P = jax.sharding.PartitionSpec
    body = functools.partial(local, mesh.shape["rows"], mesh.shape["cols"])
    in_specs = (P(("rows", "cols"), None), P("rows", "cols"))
    out_specs = (P(), P(None, "cols"), P("rows", "cols"))
    return jax.shard_map(body, mesh=mesh, in_specs=in_specs, out_specs=out_specs, check_vma=False)
```

```python
import functools
import math

import jax
import jax.numpy as jnp
from jax import lax
from jax.experimental import pallas as pl
from jax.experimental.pallas import tpu as pltpu

MESH = pl.DeviceIdType.MESH
HIGHEST = lax.Precision.HIGHEST
CHUNKS = 8
ITEMS = 8
EARLY = 3
MORE = (1, 1, 1, 0, 1, 0, 1, 0)
GROUP = 4
TILES = 8
AHEAD = 1


def dot(left, right):
    return lax.dot_general(left, right, (((1,), (0,)), ((), ())), precision=HIGHEST, preferred_element_type=jnp.float32)


def dot_t(left, right):
    return lax.dot_general(left, right, (((0,), (0,)), ((), ())), precision=HIGHEST, preferred_element_type=jnp.float32)


def split(x):
    high = x.astype(jnp.bfloat16)
    return high, (x - high.astype(jnp.float32)).astype(jnp.bfloat16)


def mul(left, right):
    return jnp.dot(left, right, preferred_element_type=jnp.float32)


def dot3(left, right):
    left_hi, left_lo = split(left)
    right_hi, right_lo = split(right)
    count = left.shape[0]
    both = mul(jnp.concatenate([left_hi, left_lo], axis=0), right_hi)
    return both[:count] + (both[count:] + mul(left_hi, right_lo))


def turn_plan(width):
    eighth = width // 8
    counts = (eighth,) * 7 + (eighth - eighth // 4, eighth // 4)
    return [(sum(counts[:t]), counts[t]) for t in range(len(counts))]


def eliminate(a_ref, m_ref, first, last):
    size = a_ref.shape[0]
    sub = lax.broadcasted_iota(jnp.int32, (size, 1), 0)
    lane = lax.broadcasted_iota(jnp.int32, (size, size), 1)
    lane_row = lax.broadcasted_iota(jnp.int32, (1, size), 1)

    def step(index, carry):
        j = index * GROUP
        a = a_ref[...]
        rows = [a_ref[pl.ds(j + t, 1), :] for t in range(GROUP)]
        mrows = [m_ref[pl.ds(j + t, 1), :] for t in range(GROUP)]
        cols = [jnp.sum(jnp.where(lane == j + t, a, 0.0), axis=1, keepdims=True) for t in range(GROUP)]
        head = {
            (t, u): jnp.sum(jnp.where(lane_row == j + u, rows[t], 0.0), axis=1, keepdims=True)
            for t in range(GROUP)
            for u in range(t, GROUP)
        }
        m = m_ref[...]
        for t in range(GROUP):
            inverse = 1.0 / head[t, t]
            factor = jnp.where(sub > j + t, cols[t] * inverse, 0.0)
            ratio = {u: head[t, u] * inverse for u in range(t + 1, GROUP)}
            for u in range(t + 1, GROUP):
                cols[u] = cols[u] - factor * head[t, u]
            for u in range(t + 1, GROUP):
                for v in range(u, GROUP):
                    head[u, v] = head[u, v] - ratio[u] * head[t, v]
            for u in range(t + 1, GROUP):
                rows[u] = rows[u] - ratio[u] * rows[t]
                mrows[u] = mrows[u] - ratio[u] * mrows[t]
            a = a - factor * rows[t]
            m = m - factor * mrows[t]
        a_ref[...] = a
        m_ref[...] = m
        return carry

    lax.fori_loop(first // GROUP, last // GROUP, step, 0)


def scale_rows(a_ref, m_ref):
    size = a_ref.shape[0]
    sub = lax.broadcasted_iota(jnp.int32, (size, size), 0)
    lane = lax.broadcasted_iota(jnp.int32, (size, size), 1)
    a = a_ref[...]
    diagonal = jnp.sum(jnp.where(lane == sub, a, 0.0), axis=1, keepdims=True)
    scale = 1.0 / jnp.sqrt(diagonal)
    return jnp.where(lane >= sub, a * scale, 0.0), m_ref[...] * scale


def unit(size):
    sub = lax.broadcasted_iota(jnp.int32, (size, size), 0)
    lane = lax.broadcasted_iota(jnp.int32, (size, size), 1)
    return jnp.where(lane == sub, 1.0, 0.0).astype(jnp.float32)


def factor_kernel(
    nr, nc,
    panel, trailing, block, trail, upper_out, coupling_out, weights_out,
    gram, gram_stage, col_stage, gram_sum, cross, cross_stage, cross_sum, work, minv, inv, square,
    load_sem, y_send, y_recv, half_send, half_recv, fwd_send, fwd_recv,
    rs_send, rs_recv, cx_send, cx_recv, ag_send, ag_recv, xrs_send, xrs_recv, xag_send, xag_recv,
):
    me_r, me_c = lax.axis_index("rows"), lax.axis_index("cols")
    depth, width = panel.shape
    half = nc // 2
    side, place = me_c // half, lax.rem(me_c, half)
    across = lax.rem(me_c + half, nc)
    chunk = depth // CHUNKS
    piece = width // nr
    groups = cross.shape[0]
    per_group = ITEMS // groups
    deep = depth // per_group
    wide = width // groups
    cross_piece = wide // nr
    hw = width // 2
    sends = []

    def remote(src, dst, send, recv, where):
        copy = pltpu.make_async_remote_copy(
            src_ref=src, dst_ref=dst, send_sem=send, recv_sem=recv, device_id=where, device_id_type=MESH
        )
        copy.start()
        sends.append(copy)
        return copy

    load_panel = pltpu.make_async_copy(panel, block.at[me_c], load_sem.at[0])
    load_panel.start()
    load_trail = pltpu.make_async_copy(trailing, trail, load_sem.at[1])
    load_trail.start()

    barrier = pltpu.get_barrier_semaphore()
    for d in range(1, nr):
        pl.semaphore_signal(barrier, inc=1, device_id={"rows": lax.rem(me_r + d, nr)}, device_id_type=MESH)
    for d in range(1, nc):
        pl.semaphore_signal(barrier, inc=1, device_id={"cols": lax.rem(me_c + d, nc)}, device_id_type=MESH)
    pl.semaphore_wait(barrier, nr + nc - 2)

    def item(k):
        return pl.ds((k % per_group) * deep, deep), pl.ds((k // per_group) * wide, wide)

    y_copies = []

    def send_across(k):
        rows, lanes = item(k)
        y_copies.append(
            remote(panel.at[rows, lanes], block.at[me_c, rows, lanes], y_send.at[k], y_recv.at[k], {"cols": across})
        )

    for k in range(EARLY):
        send_across(k)
    half_copies = []
    for d in range(1, half):
        peer = side * half + lax.rem(place + d, half)
        half_copies.append(remote(panel, block.at[me_c], half_send.at[d], half_recv.at[d], {"cols": peer}))

    def add_cross(source):
        def step(i, carry):
            rows = pl.ds(pl.multiple_of(i * chunk, chunk), chunk)
            long = pl.ds(pl.multiple_of(source * depth + i * chunk, chunk), chunk)
            product = dot_t(block[source, rows, :], trail[long, :])
            for g in range(groups):
                cross[g] += product[g * wide : (g + 1) * wide, :]
            return carry

        lax.fori_loop(0, CHUNKS, step, 0)

    def add_item(source, k):
        rows, lanes = item(k)
        long = pl.ds(pl.multiple_of(source * depth + (k % per_group) * deep, deep), deep)
        cross[k // per_group] += dot_t(block[source, rows, lanes], trail[long, :])

    load_panel.wait()
    gram[...] = jnp.zeros_like(gram)

    def gram_step(i, carry):
        rows = block[me_c, pl.ds(pl.multiple_of(i * chunk, chunk), chunk), :]
        gram[...] += dot_t(rows, rows)
        return carry

    lax.fori_loop(0, CHUNKS, gram_step, 0)

    def scatter(total, stage, send, recv, piece=piece):
        copies = []
        for d in range(1, nr):
            peer = lax.rem(me_r + d, nr)
            rows = pl.ds(pl.multiple_of(peer * piece, piece), piece)
            copies.append(remote(total.at[rows], stage.at[d], send.at[d], recv.at[d], {"rows": peer}))
        return copies

    def gather(total, send, recv, piece=piece):
        rows = pl.ds(pl.multiple_of(me_r * piece, piece), piece)
        return [
            remote(total.at[rows], total.at[rows], send.at[d], recv.at[d], {"rows": lax.rem(me_r + d, nr)})
            for d in range(1, nr)
        ]

    def arrived(copies):
        for copy in copies:
            copy.wait_recv()

    mine = pl.ds(pl.multiple_of(me_r * piece, piece), piece)
    cross_mine = pl.ds(pl.multiple_of(me_r * cross_piece, cross_piece), cross_piece)

    def summed(total, stage, mine=mine):
        value = total[mine, :]
        for d in range(1, nr):
            value = value + stage[d]
        return value

    gram_rs = scatter(gram, gram_stage, rs_send, rs_recv)
    load_trail.wait()
    cross[...] = jnp.zeros_like(cross)
    add_cross(me_c)
    arrived(gram_rs)
    col_stage[me_c] = summed(gram, gram_stage)
    exchange = [
        remote(col_stage.at[me_c], col_stage.at[me_c], cx_send.at[d], cx_recv.at[d], {"cols": lax.rem(me_c + d, nc)})
        for d in range(1, nc)
    ]
    for k in range(EARLY, ITEMS):
        send_across(k)
    for d in range(1, half):
        half_copies[d - 1].wait_recv()
        source = side * half + lax.rem(place + half - d, half)
        add_cross(source)
    arrived(exchange)
    value = col_stage[0]
    for c in range(1, nc):
        value = value + col_stage[c]
    gram_sum[mine, :] = value
    gram_ag = gather(gram_sum, ag_send, ag_recv)

    forwards = {}

    def take(k):
        y_copies[k].wait_recv()
        rows, lanes = item(k)
        for d in range(1, half):
            peer = side * half + lax.rem(place + d, half)
            slot = (d - 1) * ITEMS + k
            part = block.at[across, rows, lanes]
            forwards[d, k] = remote(part, part, fwd_send.at[slot], fwd_recv.at[slot], {"cols": peer})
        add_item(across, k)

    def take_forward(k):
        for d in range(1, half):
            forwards[d, k].wait_recv()
            source = (1 - side) * half + lax.rem(place + half - d, half)
            add_item(source, k)

    cross_rs, cross_ag = {}, {}

    def start_cross(g):
        cross_rs[g] = scatter(cross.at[g], cross_stage.at[g], xrs_send.at[g], xrs_recv.at[g], cross_piece)

    def share_cross(g):
        arrived(cross_rs[g])
        cross_sum[g, cross_mine, :] = summed(cross.at[g], cross_stage.at[g], cross_mine)
        cross_ag[g] = gather(cross_sum.at[g], xag_send.at[g], xag_recv.at[g], cross_piece)

    pending = []
    for k in range(ITEMS):
        pending.append(([functools.partial(take_forward, k - 1)] if k % per_group else []) + [functools.partial(take, k)])
        if k % per_group == per_group - 1:
            pending[-1].append(functools.partial(take_forward, k))
            pending[-1].append(functools.partial(start_cross, k // per_group))
    for g in range(groups - 1):
        pending[(g + 1) * per_group + 2].append(functools.partial(share_cross, g))

    def advance():
        for task in pending.pop(0):
            task()

    def run(first, last, more):
        eliminate(work, minv, first, last)
        for _ in range(more):
            advance()

    for _ in range(EARLY):
        advance()
    arrived(gram_ag)
    work[...] = gram_sum[pl.ds(0, hw), pl.ds(0, hw)]
    minv[...] = unit(hw)
    quarter = hw // 4
    for q in range(4):
        run(q * quarter, (q + 1) * quarter, MORE[q])
    upper1, inverse1 = scale_rows(work, minv)
    cross1 = dot(inverse1, gram_sum[pl.ds(0, hw), pl.ds(hw, hw)])
    upper_out[pl.ds(0, hw), pl.ds(0, hw)] = upper1
    upper_out[pl.ds(0, hw), pl.ds(hw, hw)] = cross1
    upper_out[pl.ds(hw, hw), pl.ds(0, hw)] = jnp.zeros_like(upper1)
    work[...] = gram_sum[pl.ds(hw, hw), pl.ds(hw, hw)] - dot_t(cross1, cross1)
    inv[pl.ds(0, hw), pl.ds(0, hw)] = inverse1
    minv[...] = unit(hw)
    for q in range(4):
        run(q * quarter, (q + 1) * quarter, MORE[4 + q])
    upper2, inverse2 = scale_rows(work, minv)
    upper_out[pl.ds(hw, hw), pl.ds(hw, hw)] = upper2
    inverse1 = inv[pl.ds(0, hw), pl.ds(0, hw)]
    corner = -dot(inverse2, dot_t(upper_out[pl.ds(0, hw), pl.ds(hw, hw)], inverse1))
    inv[pl.ds(0, hw), pl.ds(hw, hw)] = jnp.zeros_like(inverse1)
    inv[pl.ds(hw, hw), pl.ds(0, hw)] = corner
    inv[pl.ds(hw, hw), pl.ds(hw, hw)] = inverse2
    while pending:
        advance()
    inverse = inv[...]
    square[...] = dot_t(inverse, inverse)
    last = slice((groups - 1) * wide, groups * wide)
    coupling_out[...] = jnp.zeros_like(coupling_out)
    weights_out[...] = jnp.zeros_like(weights_out)
    for g in range(groups - 1):
        arrived(cross_ag[g])
        part = cross_sum[g]
        coupling_out[...] += dot(inv[:, g * wide : (g + 1) * wide], part)
        weights_out[...] += dot(square[:, g * wide : (g + 1) * wide], part)
    share_cross(groups - 1)
    arrived(cross_ag[groups - 1])
    part = cross_sum[groups - 1]
    weights_out[...] += dot(square[:, last], part)
    coupling_out[...] += dot(inv[:, last], part)
    for copy in sends:
        copy.wait_send()


def transposed_kernel(
    nr, nc,
    panel, trailing, block, trail, upper_out, coupling_out, weights_out, inv, cross_sum,
    gram, half_stage, half_sum, gram_stage, col_stage, gram_sum, cross, early_stage, tile_stage, pair_stage, late_stage, turned,
    work, minv, square,
    load_sem, greet_sem, bulk_sem, small_sem, y_recv, half_recv, fwd_recv, gram_recv, cross_recv,
):
    me_r, me_c = lax.axis_index("rows"), lax.axis_index("cols")
    depth, width = panel.shape
    side, place = me_c // 2, lax.rem(me_c, 2)
    partner = side * 2 + 1 - place
    across = (1 - side) * 2 + place
    behind = (1 - side) * 2 + 1 - place
    hw = width // 2
    piece = hw // nr
    head = depth // 8
    tall = depth - head
    turns = turn_plan(width)
    small_rows = []

    def remote(src, dst, send, recv, where):
        copy = pltpu.make_async_remote_copy(
            src_ref=src, dst_ref=dst, send_sem=send, recv_sem=recv, device_id=where, device_id_type=MESH
        )
        copy.start()
        return copy

    def small(src, dst, recv, where):
        small_rows.append(math.prod(src.shape) // width)
        return remote(src, dst, small_sem, recv, where)

    def drain(ref, sem):
        pltpu.make_async_copy(ref, ref, sem).wait()

    load_panel = pltpu.make_async_copy(panel, block.at[me_c], load_sem.at[0])
    load_panel.start()
    load_trail = pltpu.make_async_copy(trailing, trail, load_sem.at[1])
    load_trail.start()

    barrier = pltpu.get_barrier_semaphore()
    bits = [1 << b for b in range(nr.bit_length() - 1)]
    near = [me_r + bit - 2 * bit * lax.rem(me_r // bit, 2) for bit in bits]

    def greet(semaphore):
        for peer in near:
            pl.semaphore_signal(semaphore, inc=1, device_id={"rows": peer}, device_id_type=MESH)

    greet(barrier)
    for peer in (partner, across):
        pl.semaphore_signal(barrier, inc=1, device_id={"cols": peer}, device_id_type=MESH)
    pl.semaphore_wait(barrier, len(near) + 2)

    top = pl.ds(0, head)
    rest = pl.ds(head, tall)
    head_copy = remote(panel.at[top], block.at[me_c, top], bulk_sem, y_recv.at[0], {"cols": across})
    y_copies = []

    def send_turn():
        t = len(y_copies)
        part = turned.at[me_c, pl.ds(*turns[t]), rest]
        y_copies.append(remote(part, part, bulk_sem, y_recv.at[1 + t], {"cols": across}))

    greet(greet_sem.at[0])
    load_panel.wait()
    cut = depth // 16

    def turn_step(i, carry):
        rows = pl.ds(pl.multiple_of(i * cut, cut), cut)
        turned[me_c, :, rows] = block[me_c, rows, :].T
        return carry

    lax.fori_loop(0, 16, turn_step, 0)
    for met in range(len(near) - 2):
        pl.semaphore_wait(greet_sem.at[met], len(near))
        greet(greet_sem.at[met + 1])
    for _ in range(AHEAD):
        send_turn()
    gram[...] = jnp.zeros_like(gram)
    step_rows = depth // 4

    def gram_step(i, carry):
        rows = pl.ds(pl.multiple_of(i * step_rows, step_rows), step_rows)
        gram[...] += dot(turned[me_c, :, rows], block[me_c, rows, :])
        return carry

    lax.fori_loop(0, 4, gram_step, 0)
    pl.semaphore_wait(greet_sem.at[len(near) - 2], len(near))

    def scatter(total, stage, recv, where):
        for d in range(1, nr):
            peer = lax.rem(me_r + d, nr)
            small(total.at[where(peer)], stage.at[d], recv, {"rows": peer})

    def gather(total, recv, where):
        part = total.at[where(me_r)]
        for d in range(1, nr):
            small(part, part, recv, {"rows": lax.rem(me_r + d, nr)})

    def arrived(stage, recv):
        drain(stage.at[pl.ds(1, nr - 1)], recv)

    def summed(total, stage, where):
        value = total[where(me_r)]
        for d in range(1, nr):
            value = value + stage[d]
        return value

    def bands(count):
        return lambda peer: (pl.ds(pl.multiple_of(peer * count, count), count), slice(None))

    def tiles(count):
        half = cross.shape[1] // 2
        return lambda peer: (
            pl.ds(pl.multiple_of(peer // 2 * count, count), count),
            pl.ds(pl.multiple_of(lax.rem(peer, 2) * half, half), half),
        )

    def long(source, first, count):
        return pl.ds(pl.multiple_of(source * depth + first, head), count)

    def add_all(source):
        def step(i, carry):
            first = i * step_rows
            rows = pl.ds(pl.multiple_of(first, step_rows), step_rows)
            cross[...] += dot3(turned[source, :, rows], trail[long(source, first, step_rows), :])
            return carry

        lax.fori_loop(0, 4, step, 0)

    def add_head(source):
        cross[...] += dot_t(block[source, top, :], trail[long(source, 0, head), :])

    def add_lanes(source, first, count):
        lanes = pl.ds(first, count)
        cross[lanes, :] += dot3(turned[source, lanes, rest], trail[long(source, head, tall), :])

    def turn_back(source, first):
        lanes = pl.ds(first, hw)

        def step(i, carry):
            rows = pl.ds(pl.multiple_of(head + i * head, head), head)
            block[source, rows, lanes] = turned[source, lanes, rows].T
            return carry

        lax.fori_loop(0, tall // head, step, 0)

    mine = pl.ds(pl.multiple_of(place * hw, hw), hw)
    other = pl.ds(pl.multiple_of(hw - place * hw, hw), hw)
    gram_pair = small(gram.at[other], half_stage, gram_recv.at[0], {"cols": partner})
    turned_copy = remote(turned.at[me_c], turned.at[me_c], bulk_sem, half_recv.at[1], {"cols": partner})
    load_trail.wait()
    cross[...] = jnp.zeros_like(cross)
    add_all(me_c)
    gram_pair.wait_recv()
    half_sum[...] = gram[mine, :] + half_stage[...]
    scatter(half_sum, gram_stage, gram_recv.at[1], bands(piece))
    head_copy.wait_recv()
    part = block.at[across, top]
    head_forward = remote(part, part, bulk_sem, fwd_recv.at[0], {"cols": partner})
    add_head(across)
    turned_copy.wait_recv()
    add_all(partner)
    arrived(gram_stage, gram_recv.at[1])
    col_stage[side] = summed(half_sum, gram_stage, bands(piece))
    exchange = small(col_stage.at[side], col_stage.at[side], gram_recv.at[2], {"cols": across})
    while len(y_copies) < len(turns):
        send_turn()
    head_forward.wait_recv()
    add_head(behind)

    forwards = {}

    def take(t):
        y_copies[t].wait_recv()
        part = turned.at[across, pl.ds(*turns[t]), rest]
        forwards[t] = remote(part, part, bulk_sem, fwd_recv.at[1 + t], {"cols": partner})

    def take_forward(t):
        forwards[t].wait_recv()

    late_first = turns[7][0]
    twin = me_r + 1 - 2 * lax.rem(me_r, 2)
    bounds = ((0, hw), turns[4], turns[5], turns[6])
    stages = (early_stage, tile_stage.at[0], tile_stage.at[1], tile_stage.at[2])
    wheres = (bands(hw // nr),) + (tiles(turns[6][1] * 2 // nr),) * 3

    def start_cross(g):
        scatter(cross.at[pl.ds(*bounds[g])], stages[g], cross_recv.at[2 * g], wheres[g])

    def share_cross(g):
        arrived(stages[g], cross_recv.at[2 * g])
        total = cross_sum.at[pl.ds(*bounds[g])]
        total[wheres[g](me_r)] = summed(cross.at[pl.ds(*bounds[g])], stages[g], wheres[g])
        gather(total, cross_recv.at[2 * g + 1], wheres[g])

    def shared(g):
        arrived(stages[g], cross_recv.at[2 * g + 1])

    def lanes_of(t):
        first, count = turns[t]
        return pl.ds(first, count), pl.ds(first - late_first, count)

    def start_pair(t):
        lanes, late = lanes_of(t)
        mine = pair_stage.at[lax.rem(me_r, 2), late]
        mine[...] = cross[lanes, :]
        return small(mine, mine, cross_recv.at[8], {"rows": twin})

    def spread_pair(t, pair):
        _, late = lanes_of(t)
        pair.wait_recv()
        mine = late_stage.at[me_r, late]
        mine[...] = pair_stage[0, late, :] + pair_stage[1, late, :]
        for d in range(2, nr, 2):
            small(mine, mine, cross_recv.at[9], {"rows": lax.rem(me_r + d, nr)})

    def finish_pair(t):
        lanes, late = lanes_of(t)
        drain(late_stage.at[pl.ds(1, nr // 2 - 1), late], cross_recv.at[9])
        value = late_stage[lax.rem(me_r, 2), late, :]
        for step in range(2, nr, 2):
            value = value + late_stage[lax.rem(me_r, 2) + step, late, :]
        cross_sum[lanes, :] = value

    def spread(t):
        lanes, late = lanes_of(t)
        mine = late_stage.at[me_r, late]
        mine[...] = cross[lanes, :]
        for d in range(1, nr):
            small(mine, mine, cross_recv.at[10], {"rows": lax.rem(me_r + d, nr)})

    def finish(t):
        lanes, late = lanes_of(t)
        drain(late_stage.at[pl.ds(1, nr - 1), late], cross_recv.at[10])
        value = late_stage[0, late, :]
        for step in range(1, nr):
            value = value + late_stage[step, late, :]
        cross_sum[lanes, :] = value

    exchange.wait_recv()
    gram_half = gram_sum.at[mine]
    gram_half[pl.ds(pl.multiple_of(me_r * piece, piece), piece), :] = col_stage[0] + col_stage[1]
    gather(gram_half, gram_recv.at[3], bands(piece))
    take(0)
    arrived(gram_stage, gram_recv.at[3])
    gram_swap = small(gram_half, gram_half, gram_recv.at[4], {"cols": partner})
    half_copy = remote(panel, block.at[me_c], bulk_sem, half_recv.at[0], {"cols": partner})
    gram_swap.wait_recv()
    work[...] = gram_sum[pl.ds(0, hw), pl.ds(0, hw)]
    minv[...] = unit(hw)
    eighth = hw // 8
    take_forward(0)
    eliminate(work, minv, 0, 2 * eighth)
    take(1)
    eliminate(work, minv, 2 * eighth, 8 * eighth)
    take_forward(1)
    upper1, inverse1 = scale_rows(work, minv)
    cross1 = dot(inverse1, gram_sum[pl.ds(0, hw), pl.ds(hw, hw)])
    upper_out[pl.ds(0, hw), pl.ds(0, hw)] = upper1
    upper_out[pl.ds(0, hw), pl.ds(hw, hw)] = cross1
    upper_out[pl.ds(hw, hw), pl.ds(0, hw)] = jnp.zeros_like(upper1)
    work[...] = gram_sum[pl.ds(hw, hw), pl.ds(hw, hw)] - dot_t(cross1, cross1)
    inv[pl.ds(0, hw), pl.ds(0, hw)] = inverse1
    minv[...] = unit(hw)
    take(2)
    eliminate(work, minv, 0, 5 * eighth)
    take_forward(2)
    take(3)
    add_lanes(across, 0, hw)
    eliminate(work, minv, 5 * eighth, 6 * eighth)
    take_forward(3)
    add_lanes(behind, 0, hw)
    start_cross(0)
    eliminate(work, minv, 6 * eighth, 8 * eighth)
    take(4)
    upper2, inverse2 = scale_rows(work, minv)
    upper_out[pl.ds(hw, hw), pl.ds(hw, hw)] = upper2
    inverse1 = inv[pl.ds(0, hw), pl.ds(0, hw)]
    corner = -dot(inverse2, dot_t(upper_out[pl.ds(0, hw), pl.ds(hw, hw)], inverse1))
    inv[pl.ds(0, hw), pl.ds(hw, hw)] = jnp.zeros_like(inverse1)
    inv[pl.ds(hw, hw), pl.ds(0, hw)] = corner
    inv[pl.ds(hw, hw), pl.ds(hw, hw)] = inverse2
    inverse = inv[...]
    square[...] = dot_t(inverse, inverse)
    add_lanes(across, *turns[4])
    take_forward(4)
    add_lanes(behind, *turns[4])
    start_cross(1)
    turn_back(across, 0)
    share_cross(0)
    take(5)
    add_lanes(across, *turns[5])
    turn_back(behind, 0)
    take_forward(5)
    add_lanes(behind, *turns[5])
    start_cross(2)
    half_copy.wait_recv()
    share_cross(1)
    take(6)
    add_lanes(across, *turns[6])
    shared(0)
    weights_out[...] = dot(square[:, :hw], cross_sum[pl.ds(0, hw), :])
    coupling_out[...] = dot(inv[:, :hw], cross_sum[pl.ds(0, hw), :])
    take_forward(6)
    add_lanes(behind, *turns[6])
    start_cross(3)
    share_cross(2)
    take(7)
    add_lanes(across, *turns[7])
    take(8)
    add_lanes(across, *turns[8])
    take_forward(7)
    add_lanes(behind, *turns[7])
    pair = start_pair(7)
    take_forward(8)
    add_lanes(behind, *turns[8])
    spread(8)
    share_cross(3)
    spread_pair(7, pair)
    turn_back(across, hw)
    turn_back(behind, hw)
    shared(1)
    shared(2)
    shared(3)
    finish_pair(7)
    finish(8)
    weights_out[...] += dot3(square[:, hw:], cross_sum[pl.ds(hw, hw), :])
    drain(turned, bulk_sem)
    total = sum(small_rows)
    drain(block.at[0, pl.ds(0, total)], small_sem)


def update_kernel(
    shrink, block, trailing, upper, coupling, weights, r_factor, r_cross, updated,
    small, w_hi, w_lo, out, small_sem, out_sem,
):
    small[0] = upper[...] * shrink
    small[1] = coupling[...] * shrink
    copies = [
        pltpu.make_async_copy(small.at[0], r_factor, small_sem.at[0]),
        pltpu.make_async_copy(small.at[1], r_cross, small_sem.at[1]),
    ]
    for copy in copies:
        copy.start()
    w = weights[...]
    high = w.astype(jnp.bfloat16)
    w_hi[...] = high
    w_lo[...] = (w - high.astype(jnp.float32)).astype(jnp.bfloat16)
    tile = out.shape[0] // TILES

    def mul(left, right):
        return jnp.dot(left, right, preferred_element_type=jnp.float32)

    def window(i):
        return pl.ds(pl.multiple_of(i * tile, tile), tile)

    def store(i):
        return pltpu.make_async_copy(out.at[window(i)], updated.at[window(i)], out_sem.at[i])

    def step(i, carry):
        rows = window(i)
        p = block[rows, :]
        p_hi = p.astype(jnp.bfloat16)
        p_lo = (p - p_hi.astype(jnp.float32)).astype(jnp.bfloat16)
        product = mul(p_hi, w_hi[...]) + (mul(p_lo, w_hi[...]) + mul(p_hi, w_lo[...]))
        out[rows, :] = trailing[rows, :] - product
        store(i).start()
        return carry

    lax.fori_loop(0, TILES, step, 0)
    for i in range(TILES):
        store(i).wait()
    for copy in copies:
        copy.wait()


def finish_kernel(
    shrink, block, trailing, upper, coupling, weights, inv, total, r_factor, r_cross, updated,
    small, w_hi, w_lo, out, small_sem, out_sem,
):
    small[0] = upper[...] * shrink
    factor_copy = pltpu.make_async_copy(small.at[0], r_factor, small_sem.at[0])
    factor_copy.start()
    w_hi[...], w_lo[...] = split(weights[...])
    depth = out.shape[0]
    tile = depth // TILES
    first = 0
    for count in (tile // 2,) + (tile,) * (TILES - 1) + (tile // 2,):
        rows = pl.ds(first, count)
        p_hi, p_lo = split(block[rows, :])
        product = mul(p_hi, w_hi[...]) + (mul(p_lo, w_hi[...]) + mul(p_hi, w_lo[...]))
        out[rows, :] = trailing[rows, :] - product
        pltpu.make_async_copy(out.at[rows], updated.at[rows], out_sem).start()
        first += count
    hw = inv.shape[0] // 2
    small[1] = (coupling[...] + dot3(inv[:, hw:], total[hw:, :])) * shrink
    cross_copy = pltpu.make_async_copy(small.at[1], r_cross, small_sem.at[1])
    cross_copy.start()
    pltpu.make_async_copy(out, updated, out_sem).wait()
    factor_copy.wait()
    cross_copy.wait()


def local(nr, nc, panel_cols, trailing):
    depth, width = panel_cols.shape
    rows, cols = trailing.shape
    half = nc // 2
    piece = width // nr
    groups = 2 if width % (2 * 8 * nr) == 0 else 1
    wide = width // groups
    f32 = jnp.float32
    square = jax.ShapeDtypeStruct((width, width), f32)
    tall = jax.ShapeDtypeStruct((width, cols), f32)
    dma = pltpu.SemaphoreType.DMA
    vmem = pl.BlockSpec(memory_space=pltpu.VMEM)
    hbm = pl.BlockSpec(memory_space=pltpu.HBM)
    fine = nc == 4 and nr >= 4 and nr & (nr - 1) == 0 and width % 256 == 0 and (width // 2) % (8 * nr) == 0 and (width // 4) % (8 * nr) == 0 and depth % 2048 == 0 and width // 8 == 4 * nr and cols % 256 == 0
    if fine:
        gram_scratch = [
            pltpu.VMEM((width // 2, width), f32),
            pltpu.VMEM((width // 2, width), f32),
            pltpu.VMEM((nr, piece // 2, width), f32),
            pltpu.VMEM((2, piece // 2, width), f32),
        ]
        body, turns = transposed_kernel, len(turn_plan(width))
        cross_scratch = [
            pltpu.VMEM((width, cols), f32),
            pltpu.VMEM((nr, width // 2 // nr, cols), f32),
            pltpu.VMEM((3, nr, width // 4 // nr, cols // 2), f32),
            pltpu.VMEM((2, width // 4, cols), f32),
            pltpu.VMEM((nr, width // 4, cols), f32),
            pltpu.VMEM((nc, width, depth), f32),
        ]
        items = 1 + turns
        sems = [dma((2,)), pltpu.SemaphoreType.REGULAR((nr.bit_length() - 2,)), dma, dma, dma((items,)), dma((2,)), dma((items,)), dma((5,)), dma((11,))]
    else:
        body = factor_kernel
        gram_scratch = [pltpu.VMEM((nr, piece, width), f32), pltpu.VMEM((nc, piece, width), f32)]
        sems = [
            dma((2,)),
            dma((ITEMS,)), dma((ITEMS,)),
            dma((half,)), dma((half,)),
            dma((ITEMS * half,)), dma((ITEMS * half,)),
            dma((nr,)), dma((nr,)),
            dma((nc,)), dma((nc,)),
            dma((nr,)), dma((nr,)),
            dma((groups, nr)), dma((groups, nr)),
            dma((groups, nr)), dma((groups, nr)),
        ]
        cross_scratch = [
            pltpu.VMEM((groups, wide, cols), f32),
            pltpu.VMEM((groups, nr, wide // nr, cols), f32),
            pltpu.VMEM((groups, wide, cols), f32),
        ]
    shapes = (jax.ShapeDtypeStruct((nc, depth, width), f32), jax.ShapeDtypeStruct((rows, cols), f32), square, tall, tall)
    shapes += (square, tall) if fine else ()
    block, *results = pl.pallas_call(
        functools.partial(body, nr, nc),
        out_shape=shapes,
        in_specs=[hbm, hbm],
        out_specs=(vmem,) * len(shapes),
        scratch_shapes=[
            pltpu.VMEM((width, width), f32),
            *gram_scratch,
            pltpu.VMEM((width, width), f32),
            *cross_scratch,
            pltpu.VMEM((width // 2, width // 2), f32),
            pltpu.VMEM((width // 2, width // 2), f32),
            *[pltpu.VMEM((width, width), f32)] * (1 if fine else 2),
            *sems,
        ],
        compiler_params=pltpu.CompilerParams(
            collective_id=0, has_side_effects=True, vmem_limit_bytes=(32 if fine else 20) * 1024 * 1024
        ),
        name="factor",
    )(*(pltpu.with_memory_space_constraint(x, pltpu.HBM) for x in (panel_cols, trailing)))

    shrink = 1.0 / math.sqrt(rows * nr)
    r_factor, r_cross, updated = pl.pallas_call(
        functools.partial(finish_kernel if fine else update_kernel, shrink),
        out_shape=(square, tall, jax.ShapeDtypeStruct((rows, cols), f32)),
        in_specs=[vmem] * len(shapes),
        out_specs=(hbm,) * 3,
        scratch_shapes=[
            pltpu.VMEM((2, width, cols), f32),
            pltpu.VMEM((width, cols), jnp.bfloat16),
            pltpu.VMEM((width, cols), jnp.bfloat16),
            pltpu.VMEM((rows, cols), f32),
            dma((2,)),
            dma if fine else dma((TILES,)),
        ],
        compiler_params=pltpu.CompilerParams(vmem_limit_bytes=24 * 1024 * 1024),
        name="update",
    )(block.reshape(rows, width), *results)
    return r_factor, r_cross, updated


def solution(mesh):
    P = jax.sharding.PartitionSpec
    body = functools.partial(local, mesh.shape["rows"], mesh.shape["cols"])
    in_specs = (P(("rows", "cols"), None), P("rows", "cols"))
    out_specs = (P(), P(None, "cols"), P("rows", "cols"))
    return jax.shard_map(body, mesh=mesh, in_specs=in_specs, out_specs=out_specs, check_vma=False)
```

```python
import functools
import math

import jax
import jax.numpy as jnp
from jax import lax
from jax.experimental import pallas as pl
from jax.experimental.pallas import tpu as pltpu

MESH = pl.DeviceIdType.MESH
HIGHEST = lax.Precision.HIGHEST
CHUNKS = 8
ITEMS = 8
EARLY = 3
MORE = (1, 1, 1, 0, 1, 0, 1, 0)
GROUP = 4
TILES = 8
AHEAD = 1


def dot(left, right):
    return lax.dot_general(left, right, (((1,), (0,)), ((), ())), precision=HIGHEST, preferred_element_type=jnp.float32)


def dot_t(left, right):
    return lax.dot_general(left, right, (((0,), (0,)), ((), ())), precision=HIGHEST, preferred_element_type=jnp.float32)


def split(x):
    high = x.astype(jnp.bfloat16)
    return high, (x - high.astype(jnp.float32)).astype(jnp.bfloat16)


def mul(left, right):
    return jnp.dot(left, right, preferred_element_type=jnp.float32)


def dot3(left, right):
    left_hi, left_lo = split(left)
    right_hi, right_lo = split(right)
    count = left.shape[0]
    both = mul(jnp.concatenate([left_hi, left_lo], axis=0), right_hi)
    return both[:count] + (both[count:] + mul(left_hi, right_lo))


def turn_plan(width):
    eighth = width // 8
    counts = (eighth,) * 7 + (eighth - eighth // 4, eighth // 4)
    return [(sum(counts[:t]), counts[t]) for t in range(len(counts))]


def eliminate(a_ref, m_ref, first, last):
    size = a_ref.shape[0]
    sub = lax.broadcasted_iota(jnp.int32, (size, 1), 0)
    lane = lax.broadcasted_iota(jnp.int32, (size, size), 1)
    lane_row = lax.broadcasted_iota(jnp.int32, (1, size), 1)

    def step(index, carry):
        j = index * GROUP
        a = a_ref[...]
        rows = [a_ref[pl.ds(j + t, 1), :] for t in range(GROUP)]
        mrows = [m_ref[pl.ds(j + t, 1), :] for t in range(GROUP)]
        cols = [jnp.sum(jnp.where(lane == j + t, a, 0.0), axis=1, keepdims=True) for t in range(GROUP)]
        head = {
            (t, u): jnp.sum(jnp.where(lane_row == j + u, rows[t], 0.0), axis=1, keepdims=True)
            for t in range(GROUP)
            for u in range(t, GROUP)
        }
        m = m_ref[...]
        for t in range(GROUP):
            inverse = 1.0 / head[t, t]
            factor = jnp.where(sub > j + t, cols[t] * inverse, 0.0)
            ratio = {u: head[t, u] * inverse for u in range(t + 1, GROUP)}
            for u in range(t + 1, GROUP):
                cols[u] = cols[u] - factor * head[t, u]
            for u in range(t + 1, GROUP):
                for v in range(u, GROUP):
                    head[u, v] = head[u, v] - ratio[u] * head[t, v]
            for u in range(t + 1, GROUP):
                rows[u] = rows[u] - ratio[u] * rows[t]
                mrows[u] = mrows[u] - ratio[u] * mrows[t]
            a = a - factor * rows[t]
            m = m - factor * mrows[t]
        a_ref[...] = a
        m_ref[...] = m
        return carry

    lax.fori_loop(first // GROUP, last // GROUP, step, 0)


def scale_rows(a_ref, m_ref):
    size = a_ref.shape[0]
    sub = lax.broadcasted_iota(jnp.int32, (size, size), 0)
    lane = lax.broadcasted_iota(jnp.int32, (size, size), 1)
    a = a_ref[...]
    diagonal = jnp.sum(jnp.where(lane == sub, a, 0.0), axis=1, keepdims=True)
    scale = 1.0 / jnp.sqrt(diagonal)
    return jnp.where(lane >= sub, a * scale, 0.0), m_ref[...] * scale


def unit(size):
    sub = lax.broadcasted_iota(jnp.int32, (size, size), 0)
    lane = lax.broadcasted_iota(jnp.int32, (size, size), 1)
    return jnp.where(lane == sub, 1.0, 0.0).astype(jnp.float32)


def factor_kernel(
    nr, nc,
    panel, trailing, block, trail, upper_out, coupling_out, weights_out,
    gram, gram_stage, col_stage, gram_sum, cross, cross_stage, cross_sum, work, minv, inv, square,
    load_sem, y_send, y_recv, half_send, half_recv, fwd_send, fwd_recv,
    rs_send, rs_recv, cx_send, cx_recv, ag_send, ag_recv, xrs_send, xrs_recv, xag_send, xag_recv,
):
    me_r, me_c = lax.axis_index("rows"), lax.axis_index("cols")
    depth, width = panel.shape
    half = nc // 2
    side, place = me_c // half, lax.rem(me_c, half)
    across = lax.rem(me_c + half, nc)
    chunk = depth // CHUNKS
    piece = width // nr
    groups = cross.shape[0]
    per_group = ITEMS // groups
    deep = depth // per_group
    wide = width // groups
    cross_piece = wide // nr
    hw = width // 2
    sends = []

    def remote(src, dst, send, recv, where):
        copy = pltpu.make_async_remote_copy(
            src_ref=src, dst_ref=dst, send_sem=send, recv_sem=recv, device_id=where, device_id_type=MESH
        )
        copy.start()
        sends.append(copy)
        return copy

    load_panel = pltpu.make_async_copy(panel, block.at[me_c], load_sem.at[0])
    load_panel.start()
    load_trail = pltpu.make_async_copy(trailing, trail, load_sem.at[1])
    load_trail.start()

    barrier = pltpu.get_barrier_semaphore()
    for d in range(1, nr):
        pl.semaphore_signal(barrier, inc=1, device_id={"rows": lax.rem(me_r + d, nr)}, device_id_type=MESH)
    for d in range(1, nc):
        pl.semaphore_signal(barrier, inc=1, device_id={"cols": lax.rem(me_c + d, nc)}, device_id_type=MESH)
    pl.semaphore_wait(barrier, nr + nc - 2)

    def item(k):
        return pl.ds((k % per_group) * deep, deep), pl.ds((k // per_group) * wide, wide)

    y_copies = []

    def send_across(k):
        rows, lanes = item(k)
        y_copies.append(
            remote(panel.at[rows, lanes], block.at[me_c, rows, lanes], y_send.at[k], y_recv.at[k], {"cols": across})
        )

    for k in range(EARLY):
        send_across(k)
    half_copies = []
    for d in range(1, half):
        peer = side * half + lax.rem(place + d, half)
        half_copies.append(remote(panel, block.at[me_c], half_send.at[d], half_recv.at[d], {"cols": peer}))

    def add_cross(source):
        def step(i, carry):
            rows = pl.ds(pl.multiple_of(i * chunk, chunk), chunk)
            long = pl.ds(pl.multiple_of(source * depth + i * chunk, chunk), chunk)
            product = dot_t(block[source, rows, :], trail[long, :])
            for g in range(groups):
                cross[g] += product[g * wide : (g + 1) * wide, :]
            return carry

        lax.fori_loop(0, CHUNKS, step, 0)

    def add_item(source, k):
        rows, lanes = item(k)
        long = pl.ds(pl.multiple_of(source * depth + (k % per_group) * deep, deep), deep)
        cross[k // per_group] += dot_t(block[source, rows, lanes], trail[long, :])

    load_panel.wait()
    gram[...] = jnp.zeros_like(gram)

    def gram_step(i, carry):
        rows = block[me_c, pl.ds(pl.multiple_of(i * chunk, chunk), chunk), :]
        gram[...] += dot_t(rows, rows)
        return carry

    lax.fori_loop(0, CHUNKS, gram_step, 0)

    def scatter(total, stage, send, recv, piece=piece):
        copies = []
        for d in range(1, nr):
            peer = lax.rem(me_r + d, nr)
            rows = pl.ds(pl.multiple_of(peer * piece, piece), piece)
            copies.append(remote(total.at[rows], stage.at[d], send.at[d], recv.at[d], {"rows": peer}))
        return copies

    def gather(total, send, recv, piece=piece):
        rows = pl.ds(pl.multiple_of(me_r * piece, piece), piece)
        return [
            remote(total.at[rows], total.at[rows], send.at[d], recv.at[d], {"rows": lax.rem(me_r + d, nr)})
            for d in range(1, nr)
        ]

    def arrived(copies):
        for copy in copies:
            copy.wait_recv()

    mine = pl.ds(pl.multiple_of(me_r * piece, piece), piece)
    cross_mine = pl.ds(pl.multiple_of(me_r * cross_piece, cross_piece), cross_piece)

    def summed(total, stage, mine=mine):
        value = total[mine, :]
        for d in range(1, nr):
            value = value + stage[d]
        return value

    gram_rs = scatter(gram, gram_stage, rs_send, rs_recv)
    load_trail.wait()
    cross[...] = jnp.zeros_like(cross)
    add_cross(me_c)
    arrived(gram_rs)
    col_stage[me_c] = summed(gram, gram_stage)
    exchange = [
        remote(col_stage.at[me_c], col_stage.at[me_c], cx_send.at[d], cx_recv.at[d], {"cols": lax.rem(me_c + d, nc)})
        for d in range(1, nc)
    ]
    for k in range(EARLY, ITEMS):
        send_across(k)
    for d in range(1, half):
        half_copies[d - 1].wait_recv()
        source = side * half + lax.rem(place + half - d, half)
        add_cross(source)
    arrived(exchange)
    value = col_stage[0]
    for c in range(1, nc):
        value = value + col_stage[c]
    gram_sum[mine, :] = value
    gram_ag = gather(gram_sum, ag_send, ag_recv)

    forwards = {}

    def take(k):
        y_copies[k].wait_recv()
        rows, lanes = item(k)
        for d in range(1, half):
            peer = side * half + lax.rem(place + d, half)
            slot = (d - 1) * ITEMS + k
            part = block.at[across, rows, lanes]
            forwards[d, k] = remote(part, part, fwd_send.at[slot], fwd_recv.at[slot], {"cols": peer})
        add_item(across, k)

    def take_forward(k):
        for d in range(1, half):
            forwards[d, k].wait_recv()
            source = (1 - side) * half + lax.rem(place + half - d, half)
            add_item(source, k)

    cross_rs, cross_ag = {}, {}

    def start_cross(g):
        cross_rs[g] = scatter(cross.at[g], cross_stage.at[g], xrs_send.at[g], xrs_recv.at[g], cross_piece)

    def share_cross(g):
        arrived(cross_rs[g])
        cross_sum[g, cross_mine, :] = summed(cross.at[g], cross_stage.at[g], cross_mine)
        cross_ag[g] = gather(cross_sum.at[g], xag_send.at[g], xag_recv.at[g], cross_piece)

    pending = []
    for k in range(ITEMS):
        pending.append(([functools.partial(take_forward, k - 1)] if k % per_group else []) + [functools.partial(take, k)])
        if k % per_group == per_group - 1:
            pending[-1].append(functools.partial(take_forward, k))
            pending[-1].append(functools.partial(start_cross, k // per_group))
    for g in range(groups - 1):
        pending[(g + 1) * per_group + 2].append(functools.partial(share_cross, g))

    def advance():
        for task in pending.pop(0):
            task()

    def run(first, last, more):
        eliminate(work, minv, first, last)
        for _ in range(more):
            advance()

    for _ in range(EARLY):
        advance()
    arrived(gram_ag)
    work[...] = gram_sum[pl.ds(0, hw), pl.ds(0, hw)]
    minv[...] = unit(hw)
    quarter = hw // 4
    for q in range(4):
        run(q * quarter, (q + 1) * quarter, MORE[q])
    upper1, inverse1 = scale_rows(work, minv)
    cross1 = dot(inverse1, gram_sum[pl.ds(0, hw), pl.ds(hw, hw)])
    upper_out[pl.ds(0, hw), pl.ds(0, hw)] = upper1
    upper_out[pl.ds(0, hw), pl.ds(hw, hw)] = cross1
    upper_out[pl.ds(hw, hw), pl.ds(0, hw)] = jnp.zeros_like(upper1)
    work[...] = gram_sum[pl.ds(hw, hw), pl.ds(hw, hw)] - dot_t(cross1, cross1)
    inv[pl.ds(0, hw), pl.ds(0, hw)] = inverse1
    minv[...] = unit(hw)
    for q in range(4):
        run(q * quarter, (q + 1) * quarter, MORE[4 + q])
    upper2, inverse2 = scale_rows(work, minv)
    upper_out[pl.ds(hw, hw), pl.ds(hw, hw)] = upper2
    inverse1 = inv[pl.ds(0, hw), pl.ds(0, hw)]
    corner = -dot(inverse2, dot_t(upper_out[pl.ds(0, hw), pl.ds(hw, hw)], inverse1))
    inv[pl.ds(0, hw), pl.ds(hw, hw)] = jnp.zeros_like(inverse1)
    inv[pl.ds(hw, hw), pl.ds(0, hw)] = corner
    inv[pl.ds(hw, hw), pl.ds(hw, hw)] = inverse2
    while pending:
        advance()
    inverse = inv[...]
    square[...] = dot_t(inverse, inverse)
    last = slice((groups - 1) * wide, groups * wide)
    coupling_out[...] = jnp.zeros_like(coupling_out)
    weights_out[...] = jnp.zeros_like(weights_out)
    for g in range(groups - 1):
        arrived(cross_ag[g])
        part = cross_sum[g]
        coupling_out[...] += dot(inv[:, g * wide : (g + 1) * wide], part)
        weights_out[...] += dot(square[:, g * wide : (g + 1) * wide], part)
    share_cross(groups - 1)
    arrived(cross_ag[groups - 1])
    part = cross_sum[groups - 1]
    weights_out[...] += dot(square[:, last], part)
    coupling_out[...] += dot(inv[:, last], part)
    for copy in sends:
        copy.wait_send()


def transposed_kernel(
    nr, nc,
    panel, trailing, block, trail, upper_out, coupling_out, weights_out, inv, cross_sum, square, mixed,
    gram, half_stage, half_sum, gram_stage, col_stage, gram_sum, cross, early_stage, tile_stage, pair_stage, late_stage, turned,
    work, minv,
    load_sem, greet_sem, bulk_sem, small_sem, y_recv, half_recv, fwd_recv, gram_recv, cross_recv,
):
    me_r, me_c = lax.axis_index("rows"), lax.axis_index("cols")
    depth, width = panel.shape
    side, place = me_c // 2, lax.rem(me_c, 2)
    partner = side * 2 + 1 - place
    across = (1 - side) * 2 + place
    behind = (1 - side) * 2 + 1 - place
    hw = width // 2
    piece = hw // nr
    head = depth // 8
    tall = depth - head
    turns = turn_plan(width)
    small_rows = []

    def remote(src, dst, send, recv, where):
        copy = pltpu.make_async_remote_copy(
            src_ref=src, dst_ref=dst, send_sem=send, recv_sem=recv, device_id=where, device_id_type=MESH
        )
        copy.start()
        return copy

    def small(src, dst, recv, where):
        small_rows.append(math.prod(src.shape) // width)
        return remote(src, dst, small_sem, recv, where)

    def drain(ref, sem):
        pltpu.make_async_copy(ref, ref, sem).wait()

    load_panel = pltpu.make_async_copy(panel, block.at[me_c], load_sem.at[0])
    load_panel.start()
    load_trail = pltpu.make_async_copy(trailing, trail, load_sem.at[1])
    load_trail.start()

    barrier = pltpu.get_barrier_semaphore()
    bits = [1 << b for b in range(nr.bit_length() - 1)]
    near = [me_r + bit - 2 * bit * lax.rem(me_r // bit, 2) for bit in bits]

    def greet(semaphore):
        for peer in near:
            pl.semaphore_signal(semaphore, inc=1, device_id={"rows": peer}, device_id_type=MESH)

    greet(barrier)
    for peer in (partner, across):
        pl.semaphore_signal(barrier, inc=1, device_id={"cols": peer}, device_id_type=MESH)
    pl.semaphore_wait(barrier, len(near) + 2)

    top = pl.ds(0, head)
    rest = pl.ds(head, tall)
    head_copy = remote(panel.at[top], block.at[me_c, top], bulk_sem, y_recv.at[0], {"cols": across})
    y_copies = []

    def send_turn():
        t = len(y_copies)
        part = turned.at[me_c, pl.ds(*turns[t]), rest]
        y_copies.append(remote(part, part, bulk_sem, y_recv.at[1 + t], {"cols": across}))

    greet(greet_sem.at[0])
    load_panel.wait()
    cut = depth // 16

    def turn_step(i, carry):
        rows = pl.ds(pl.multiple_of(i * cut, cut), cut)
        turned[me_c, :, rows] = block[me_c, rows, :].T
        return carry

    lax.fori_loop(0, 16, turn_step, 0)
    for met in range(len(near) - 2):
        pl.semaphore_wait(greet_sem.at[met], len(near))
        greet(greet_sem.at[met + 1])
    for _ in range(AHEAD):
        send_turn()
    gram[...] = jnp.zeros_like(gram)
    step_rows = depth // 4

    def gram_step(i, carry):
        rows = pl.ds(pl.multiple_of(i * step_rows, step_rows), step_rows)
        gram[...] += dot(turned[me_c, :, rows], block[me_c, rows, :])
        return carry

    lax.fori_loop(0, 4, gram_step, 0)
    pl.semaphore_wait(greet_sem.at[len(near) - 2], len(near))

    def scatter(total, stage, recv, where):
        for d in range(1, nr):
            peer = lax.rem(me_r + d, nr)
            small(total.at[where(peer)], stage.at[d], recv, {"rows": peer})

    def gather(total, recv, where):
        part = total.at[where(me_r)]
        for d in range(1, nr):
            small(part, part, recv, {"rows": lax.rem(me_r + d, nr)})

    def arrived(stage, recv):
        drain(stage.at[pl.ds(1, nr - 1)], recv)

    def summed(total, stage, where):
        value = total[where(me_r)]
        for d in range(1, nr):
            value = value + stage[d]
        return value

    def bands(count):
        return lambda peer: (pl.ds(pl.multiple_of(peer * count, count), count), slice(None))

    def tiles(count):
        half = cross.shape[1] // 2
        return lambda peer: (
            pl.ds(pl.multiple_of(peer // 2 * count, count), count),
            pl.ds(pl.multiple_of(lax.rem(peer, 2) * half, half), half),
        )

    def long(source, first, count):
        return pl.ds(pl.multiple_of(source * depth + first, head), count)

    def add_all(source):
        def step(i, carry):
            first = i * step_rows
            rows = pl.ds(pl.multiple_of(first, step_rows), step_rows)
            cross[...] += dot3(turned[source, :, rows], trail[long(source, first, step_rows), :])
            return carry

        lax.fori_loop(0, 4, step, 0)

    def add_head(source):
        cross[...] += dot_t(block[source, top, :], trail[long(source, 0, head), :])

    def add_lanes(source, first, count):
        lanes = pl.ds(first, count)
        cross[lanes, :] += dot3(turned[source, lanes, rest], trail[long(source, head, tall), :])

    known = turns[6][0]
    block_rows = depth // 4

    def mix():
        tile = square[:, hw:]
        lane = lax.broadcasted_iota(jnp.int32, tile.shape, 1)
        m_hi, m_lo = split(jnp.where(lane < hw // 2, pltpu.roll(tile, hw // 2, 1), tile))
        low = lax.broadcasted_iota(jnp.int32, (block_rows, hw), 1) >= hw // 2

        def step(i, carry):
            rows = pl.ds(pl.multiple_of(lax.rem(i, 4) * block_rows, block_rows), block_rows)
            here = pl.ds(pl.multiple_of(i * block_rows, block_rows), block_rows)
            p_hi, p_lo = split(block[side * 2 + i // 4, rows, :])
            product = mul(p_hi, m_hi) + (mul(p_lo, m_hi) + mul(p_hi, m_lo))
            high = product.astype(jnp.bfloat16)
            wide = high.astype(jnp.float32)
            mixed[here, pl.ds(0, hw)] = jnp.where(low, product - wide, wide).astype(jnp.bfloat16)
            mixed[here, pl.ds(hw, hw)] = high
            return carry

        lax.fori_loop(0, 8, step, 0)

    def update_own():
        weights_out[...] += dot3(square[:, hw:known], cross_sum[pl.ds(hw, known - hw), :])
        w_hi, w_lo = split(weights_out[...])
        count = 2 * block_rows

        def step(i, carry):
            rows = pl.ds(pl.multiple_of(lax.rem(i, 2) * count, count), count)
            here = pl.ds(pl.multiple_of(side * 2 * depth + i * count, count), count)
            p_hi, p_lo = split(block[side * 2 + i // 2, rows, :])
            trail[here, :] -= mul(p_hi, w_hi) + (mul(p_lo, w_hi) + mul(p_hi, w_lo))
            return carry

        lax.fori_loop(0, 4, step, 0)

    def turn_back(source, first):
        lanes = pl.ds(first, hw)

        def step(i, carry):
            rows = pl.ds(pl.multiple_of(head + i * head, head), head)
            block[source, rows, lanes] = turned[source, lanes, rows].T
            return carry

        lax.fori_loop(0, tall // head, step, 0)

    mine = pl.ds(pl.multiple_of(place * hw, hw), hw)
    other = pl.ds(pl.multiple_of(hw - place * hw, hw), hw)
    gram_pair = small(gram.at[other], half_stage, gram_recv.at[0], {"cols": partner})
    turned_copy = remote(turned.at[me_c], turned.at[me_c], bulk_sem, half_recv.at[1], {"cols": partner})
    load_trail.wait()
    cross[...] = jnp.zeros_like(cross)
    add_all(me_c)
    gram_pair.wait_recv()
    half_sum[...] = gram[mine, :] + half_stage[...]
    scatter(half_sum, gram_stage, gram_recv.at[1], bands(piece))
    head_copy.wait_recv()
    part = block.at[across, top]
    head_forward = remote(part, part, bulk_sem, fwd_recv.at[0], {"cols": partner})
    add_head(across)
    turned_copy.wait_recv()
    add_all(partner)
    arrived(gram_stage, gram_recv.at[1])
    col_stage[side] = summed(half_sum, gram_stage, bands(piece))
    exchange = small(col_stage.at[side], col_stage.at[side], gram_recv.at[2], {"cols": across})
    while len(y_copies) < len(turns):
        send_turn()
    head_forward.wait_recv()
    add_head(behind)

    forwards = {}

    def take(t):
        y_copies[t].wait_recv()
        part = turned.at[across, pl.ds(*turns[t]), rest]
        forwards[t] = remote(part, part, bulk_sem, fwd_recv.at[1 + t], {"cols": partner})

    def take_forward(t):
        forwards[t].wait_recv()

    late_first = turns[7][0]
    twin = me_r + 1 - 2 * lax.rem(me_r, 2)
    bounds = ((0, hw), turns[4], turns[5], turns[6])
    stages = (early_stage, tile_stage.at[0], tile_stage.at[1], tile_stage.at[2])
    wheres = (bands(hw // nr),) + (tiles(turns[6][1] * 2 // nr),) * 3

    def start_cross(g):
        scatter(cross.at[pl.ds(*bounds[g])], stages[g], cross_recv.at[2 * g], wheres[g])

    def share_cross(g):
        arrived(stages[g], cross_recv.at[2 * g])
        total = cross_sum.at[pl.ds(*bounds[g])]
        total[wheres[g](me_r)] = summed(cross.at[pl.ds(*bounds[g])], stages[g], wheres[g])
        gather(total, cross_recv.at[2 * g + 1], wheres[g])

    def shared(g):
        arrived(stages[g], cross_recv.at[2 * g + 1])

    def lanes_of(t):
        first, count = turns[t]
        return pl.ds(first, count), pl.ds(first - late_first, count)

    def start_pair(t):
        lanes, late = lanes_of(t)
        mine = pair_stage.at[lax.rem(me_r, 2), late]
        mine[...] = cross[lanes, :]
        return small(mine, mine, cross_recv.at[8], {"rows": twin})

    def spread_pair(t, pair):
        _, late = lanes_of(t)
        pair.wait_recv()
        mine = late_stage.at[me_r, late]
        mine[...] = pair_stage[0, late, :] + pair_stage[1, late, :]
        for d in range(2, nr, 2):
            small(mine, mine, cross_recv.at[9], {"rows": lax.rem(me_r + d, nr)})

    def finish_pair(t):
        lanes, late = lanes_of(t)
        drain(late_stage.at[pl.ds(1, nr // 2 - 1), late], cross_recv.at[9])
        value = late_stage[lax.rem(me_r, 2), late, :]
        for step in range(2, nr, 2):
            value = value + late_stage[lax.rem(me_r, 2) + step, late, :]
        cross_sum[lanes, :] = value

    def spread(t):
        lanes, late = lanes_of(t)
        mine = late_stage.at[me_r, late]
        mine[...] = cross[lanes, :]
        for d in range(1, nr):
            small(mine, mine, cross_recv.at[10], {"rows": lax.rem(me_r + d, nr)})

    def finish(t):
        lanes, late = lanes_of(t)
        drain(late_stage.at[pl.ds(1, nr - 1), late], cross_recv.at[10])
        value = late_stage[0, late, :]
        for step in range(1, nr):
            value = value + late_stage[step, late, :]
        cross_sum[lanes, :] = value

    exchange.wait_recv()
    gram_half = gram_sum.at[mine]
    gram_half[pl.ds(pl.multiple_of(me_r * piece, piece), piece), :] = col_stage[0] + col_stage[1]
    gather(gram_half, gram_recv.at[3], bands(piece))
    take(0)
    arrived(gram_stage, gram_recv.at[3])
    gram_swap = small(gram_half, gram_half, gram_recv.at[4], {"cols": partner})
    half_copy = remote(panel, block.at[me_c], bulk_sem, half_recv.at[0], {"cols": partner})
    gram_swap.wait_recv()
    work[...] = gram_sum[pl.ds(0, hw), pl.ds(0, hw)]
    minv[...] = unit(hw)
    eighth = hw // 8
    take_forward(0)
    eliminate(work, minv, 0, 2 * eighth)
    take(1)
    eliminate(work, minv, 2 * eighth, 8 * eighth)
    take_forward(1)
    upper1, inverse1 = scale_rows(work, minv)
    cross1 = dot(inverse1, gram_sum[pl.ds(0, hw), pl.ds(hw, hw)])
    upper_out[pl.ds(0, hw), pl.ds(0, hw)] = upper1
    upper_out[pl.ds(0, hw), pl.ds(hw, hw)] = cross1
    upper_out[pl.ds(hw, hw), pl.ds(0, hw)] = jnp.zeros_like(upper1)
    work[...] = gram_sum[pl.ds(hw, hw), pl.ds(hw, hw)] - dot_t(cross1, cross1)
    inv[pl.ds(0, hw), pl.ds(0, hw)] = inverse1
    minv[...] = unit(hw)
    take(2)
    eliminate(work, minv, 0, 5 * eighth)
    take_forward(2)
    take(3)
    add_lanes(across, 0, hw)
    eliminate(work, minv, 5 * eighth, 6 * eighth)
    take_forward(3)
    add_lanes(behind, 0, hw)
    start_cross(0)
    eliminate(work, minv, 6 * eighth, 8 * eighth)
    take(4)
    upper2, inverse2 = scale_rows(work, minv)
    upper_out[pl.ds(hw, hw), pl.ds(hw, hw)] = upper2
    inverse1 = inv[pl.ds(0, hw), pl.ds(0, hw)]
    corner = -dot(inverse2, dot_t(upper_out[pl.ds(0, hw), pl.ds(hw, hw)], inverse1))
    inv[pl.ds(0, hw), pl.ds(hw, hw)] = jnp.zeros_like(inverse1)
    inv[pl.ds(hw, hw), pl.ds(0, hw)] = corner
    inv[pl.ds(hw, hw), pl.ds(hw, hw)] = inverse2
    inverse = inv[...]
    square[...] = dot_t(inverse, inverse)
    add_lanes(across, *turns[4])
    take_forward(4)
    add_lanes(behind, *turns[4])
    start_cross(1)
    turn_back(across, 0)
    share_cross(0)
    take(5)
    add_lanes(across, *turns[5])
    turn_back(behind, 0)
    take_forward(5)
    add_lanes(behind, *turns[5])
    start_cross(2)
    half_copy.wait_recv()
    share_cross(1)
    mix()
    take(6)
    add_lanes(across, *turns[6])
    shared(0)
    weights_out[...] = dot(square[:, :hw], cross_sum[pl.ds(0, hw), :])
    coupling_out[...] = dot(inv[:, :hw], cross_sum[pl.ds(0, hw), :])
    take_forward(6)
    add_lanes(behind, *turns[6])
    start_cross(3)
    share_cross(2)
    take(7)
    add_lanes(across, *turns[7])
    take(8)
    add_lanes(across, *turns[8])
    take_forward(7)
    add_lanes(behind, *turns[7])
    pair = start_pair(7)
    take_forward(8)
    add_lanes(behind, *turns[8])
    spread(8)
    turn_back(across, hw)
    share_cross(3)
    turn_back(behind, hw)
    spread_pair(7, pair)
    shared(1)
    shared(2)
    update_own()
    shared(3)
    finish_pair(7)
    finish(8)
    drain(turned, bulk_sem)
    total = sum(small_rows)
    drain(block.at[0, pl.ds(0, total)], small_sem)


def update_kernel(
    shrink, block, trailing, upper, coupling, weights, r_factor, r_cross, updated,
    small, w_hi, w_lo, out, small_sem, out_sem,
):
    small[0] = upper[...] * shrink
    small[1] = coupling[...] * shrink
    copies = [
        pltpu.make_async_copy(small.at[0], r_factor, small_sem.at[0]),
        pltpu.make_async_copy(small.at[1], r_cross, small_sem.at[1]),
    ]
    for copy in copies:
        copy.start()
    w = weights[...]
    high = w.astype(jnp.bfloat16)
    w_hi[...] = high
    w_lo[...] = (w - high.astype(jnp.float32)).astype(jnp.bfloat16)
    tile = out.shape[0] // TILES

    def mul(left, right):
        return jnp.dot(left, right, preferred_element_type=jnp.float32)

    def window(i):
        return pl.ds(pl.multiple_of(i * tile, tile), tile)

    def store(i):
        return pltpu.make_async_copy(out.at[window(i)], updated.at[window(i)], out_sem.at[i])

    def step(i, carry):
        rows = window(i)
        p = block[rows, :]
        p_hi = p.astype(jnp.bfloat16)
        p_lo = (p - p_hi.astype(jnp.float32)).astype(jnp.bfloat16)
        product = mul(p_hi, w_hi[...]) + (mul(p_lo, w_hi[...]) + mul(p_hi, w_lo[...]))
        out[rows, :] = trailing[rows, :] - product
        store(i).start()
        return carry

    lax.fori_loop(0, TILES, step, 0)
    for i in range(TILES):
        store(i).wait()
    for copy in copies:
        copy.wait()


def finish_kernel(
    shrink, block, trailing, upper, coupling, weights, inv, total, square, mixed, r_factor, r_cross, updated,
    small, w_hi, w_lo, c_all, out, small_sem, out_sem,
):
    small[0] = upper[...] * shrink
    factor_copy = pltpu.make_async_copy(small.at[0], r_factor, small_sem.at[0])
    factor_copy.start()
    hw = inv.shape[0] // 2
    part = hw // 2
    c_hi, c_lo = split(total[pl.ds(hw + part, part), :])
    c_all[pl.ds(0, part), :] = c_hi
    c_all[pl.ds(part, part), :] = c_hi
    c_all[pl.ds(hw, part), :] = c_lo
    c_all[pl.ds(hw + part, part), :] = jnp.zeros_like(c_lo)
    depth = out.shape[0]
    own = depth // 2
    side = lax.axis_index("cols") // 2
    tile = depth // TILES

    def window(start, first, count):
        return pl.ds(pl.multiple_of(start + first, tile // 2), count)

    def store(rows):
        pltpu.make_async_copy(out.at[rows], updated.at[rows], out_sem).start()

    first = 0
    for count in (tile // 2,) + (tile,) * (TILES // 2 - 1) + (tile // 2,):
        rows = window(side * own, first, count)
        out[rows, :] = trailing[rows, :] - mul(mixed[pl.ds(first, count), :], c_all[...])
        store(rows)
        first += count
    row = lax.broadcasted_iota(jnp.int32, (hw, total.shape[1]), 0)
    late = jnp.where(row < part, 0.0, total[pl.ds(hw, hw), :])
    w_hi[...], w_lo[...] = split(weights[...] + dot3(square[:, hw:], late))
    first = 0
    for count in (tile,) * (TILES // 2 - 1) + (tile // 2,) * 2:
        rows = window((1 - side) * own, first, count)
        p_hi, p_lo = split(block[rows, :])
        product = mul(p_hi, w_hi[...]) + (mul(p_lo, w_hi[...]) + mul(p_hi, w_lo[...]))
        out[rows, :] = trailing[rows, :] - product
        store(rows)
        first += count
    small[1] = (coupling[...] + dot3(inv[:, hw:], total[hw:, :])) * shrink
    cross_copy = pltpu.make_async_copy(small.at[1], r_cross, small_sem.at[1])
    cross_copy.start()
    pltpu.make_async_copy(out, updated, out_sem).wait()
    factor_copy.wait()
    cross_copy.wait()


def local(nr, nc, panel_cols, trailing):
    depth, width = panel_cols.shape
    rows, cols = trailing.shape
    half = nc // 2
    piece = width // nr
    groups = 2 if width % (2 * 8 * nr) == 0 else 1
    wide = width // groups
    f32 = jnp.float32
    square = jax.ShapeDtypeStruct((width, width), f32)
    tall = jax.ShapeDtypeStruct((width, cols), f32)
    dma = pltpu.SemaphoreType.DMA
    vmem = pl.BlockSpec(memory_space=pltpu.VMEM)
    hbm = pl.BlockSpec(memory_space=pltpu.HBM)
    fine = nc == 4 and nr >= 4 and nr & (nr - 1) == 0 and width % 256 == 0 and (width // 2) % (8 * nr) == 0 and (width // 4) % (8 * nr) == 0 and depth % 2048 == 0 and width // 8 == 4 * nr and cols % 256 == 0
    if fine:
        gram_scratch = [
            pltpu.VMEM((width // 2, width), f32),
            pltpu.VMEM((width // 2, width), f32),
            pltpu.VMEM((nr, piece // 2, width), f32),
            pltpu.VMEM((2, piece // 2, width), f32),
        ]
        body, turns = transposed_kernel, len(turn_plan(width))
        cross_scratch = [
            pltpu.VMEM((width, cols), f32),
            pltpu.VMEM((nr, width // 2 // nr, cols), f32),
            pltpu.VMEM((3, nr, width // 4 // nr, cols // 2), f32),
            pltpu.VMEM((2, width // 4, cols), f32),
            pltpu.VMEM((nr, width // 4, cols), f32),
            pltpu.VMEM((nc, width, depth), f32),
        ]
        items = 1 + turns
        sems = [dma((2,)), pltpu.SemaphoreType.REGULAR((nr.bit_length() - 2,)), dma, dma, dma((items,)), dma((2,)), dma((items,)), dma((5,)), dma((11,))]
    else:
        body = factor_kernel
        gram_scratch = [pltpu.VMEM((nr, piece, width), f32), pltpu.VMEM((nc, piece, width), f32)]
        sems = [
            dma((2,)),
            dma((ITEMS,)), dma((ITEMS,)),
            dma((half,)), dma((half,)),
            dma((ITEMS * half,)), dma((ITEMS * half,)),
            dma((nr,)), dma((nr,)),
            dma((nc,)), dma((nc,)),
            dma((nr,)), dma((nr,)),
            dma((groups, nr)), dma((groups, nr)),
            dma((groups, nr)), dma((groups, nr)),
        ]
        cross_scratch = [
            pltpu.VMEM((groups, wide, cols), f32),
            pltpu.VMEM((groups, nr, wide // nr, cols), f32),
            pltpu.VMEM((groups, wide, cols), f32),
        ]
    shapes = (jax.ShapeDtypeStruct((nc, depth, width), f32), jax.ShapeDtypeStruct((rows, cols), f32), square, tall, tall)
    shapes += (square, tall, square, jax.ShapeDtypeStruct((2 * depth, width), jnp.bfloat16)) if fine else ()
    block, *results = pl.pallas_call(
        functools.partial(body, nr, nc),
        out_shape=shapes,
        in_specs=[hbm, hbm],
        out_specs=(vmem,) * len(shapes),
        scratch_shapes=[
            pltpu.VMEM((width, width), f32),
            *gram_scratch,
            pltpu.VMEM((width, width), f32),
            *cross_scratch,
            pltpu.VMEM((width // 2, width // 2), f32),
            pltpu.VMEM((width // 2, width // 2), f32),
            *[pltpu.VMEM((width, width), f32)] * (0 if fine else 2),
            *sems,
        ],
        compiler_params=pltpu.CompilerParams(
            collective_id=0, has_side_effects=True, vmem_limit_bytes=(32 if fine else 20) * 1024 * 1024
        ),
        name="factor",
    )(*(pltpu.with_memory_space_constraint(x, pltpu.HBM) for x in (panel_cols, trailing)))

    shrink = 1.0 / math.sqrt(rows * nr)
    r_factor, r_cross, updated = pl.pallas_call(
        functools.partial(finish_kernel if fine else update_kernel, shrink),
        out_shape=(square, tall, jax.ShapeDtypeStruct((rows, cols), f32)),
        in_specs=[vmem] * len(shapes),
        out_specs=(hbm,) * 3,
        scratch_shapes=[
            pltpu.VMEM((2, width, cols), f32),
            *[pltpu.VMEM((width, cols), jnp.bfloat16)] * (3 if fine else 2),
            pltpu.VMEM((rows, cols), f32),
            dma((2,)),
            dma if fine else dma((TILES,)),
        ],
        compiler_params=pltpu.CompilerParams(vmem_limit_bytes=24 * 1024 * 1024),
        name="update",
    )(block.reshape(rows, width), *results)
    return r_factor, r_cross, updated


def solution(mesh):
    P = jax.sharding.PartitionSpec
    body = functools.partial(local, mesh.shape["rows"], mesh.shape["cols"])
    in_specs = (P(("rows", "cols"), None), P("rows", "cols"))
    out_specs = (P(), P(None, "cols"), P("rows", "cols"))
    return jax.shard_map(body, mesh=mesh, in_specs=in_specs, out_specs=out_specs, check_vma=False)
```

```python
import functools
import math

import jax
import jax.numpy as jnp
from jax import lax
from jax.experimental import pallas as pl
from jax.experimental.pallas import tpu as pltpu

MESH = pl.DeviceIdType.MESH
HIGHEST = lax.Precision.HIGHEST
CHUNKS = 8
ITEMS = 8
EARLY = 3
MORE = (1, 1, 1, 0, 1, 0, 1, 0)
GROUP = 4
TILES = 8
AHEAD = 1


def dot(left, right):
    return lax.dot_general(left, right, (((1,), (0,)), ((), ())), precision=HIGHEST, preferred_element_type=jnp.float32)


def dot_t(left, right):
    return lax.dot_general(left, right, (((0,), (0,)), ((), ())), precision=HIGHEST, preferred_element_type=jnp.float32)


def split(x):
    high = x.astype(jnp.bfloat16)
    return high, (x - high.astype(jnp.float32)).astype(jnp.bfloat16)


def mul(left, right):
    return jnp.dot(left, right, preferred_element_type=jnp.float32)


def dot3(left, right):
    left_hi, left_lo = split(left)
    right_hi, right_lo = split(right)
    count = left.shape[0]
    both = mul(jnp.concatenate([left_hi, left_lo], axis=0), right_hi)
    return both[:count] + (both[count:] + mul(left_hi, right_lo))


def turn_plan(width):
    eighth = width // 8
    counts = (eighth,) * 7 + (eighth - eighth // 4, eighth // 4)
    return [(sum(counts[:t]), counts[t]) for t in range(len(counts))]


def eliminate(a_ref, m_ref, first, last):
    size = a_ref.shape[0]
    sub = lax.broadcasted_iota(jnp.int32, (size, 1), 0)
    lane = lax.broadcasted_iota(jnp.int32, (size, size), 1)
    lane_row = lax.broadcasted_iota(jnp.int32, (1, size), 1)

    def step(index, carry):
        j = index * GROUP
        a = a_ref[...]
        rows = [a_ref[pl.ds(j + t, 1), :] for t in range(GROUP)]
        mrows = [m_ref[pl.ds(j + t, 1), :] for t in range(GROUP)]
        cols = [jnp.sum(jnp.where(lane == j + t, a, 0.0), axis=1, keepdims=True) for t in range(GROUP)]
        head = {
            (t, u): jnp.sum(jnp.where(lane_row == j + u, rows[t], 0.0), axis=1, keepdims=True)
            for t in range(GROUP)
            for u in range(t, GROUP)
        }
        m = m_ref[...]
        for t in range(GROUP):
            inverse = 1.0 / head[t, t]
            factor = jnp.where(sub > j + t, cols[t] * inverse, 0.0)
            ratio = {u: head[t, u] * inverse for u in range(t + 1, GROUP)}
            for u in range(t + 1, GROUP):
                cols[u] = cols[u] - factor * head[t, u]
            for u in range(t + 1, GROUP):
                for v in range(u, GROUP):
                    head[u, v] = head[u, v] - ratio[u] * head[t, v]
            for u in range(t + 1, GROUP):
                rows[u] = rows[u] - ratio[u] * rows[t]
                mrows[u] = mrows[u] - ratio[u] * mrows[t]
            a = a - factor * rows[t]
            m = m - factor * mrows[t]
        a_ref[...] = a
        m_ref[...] = m
        return carry

    lax.fori_loop(first // GROUP, last // GROUP, step, 0)


def scale_rows(a_ref, m_ref):
    size = a_ref.shape[0]
    sub = lax.broadcasted_iota(jnp.int32, (size, size), 0)
    lane = lax.broadcasted_iota(jnp.int32, (size, size), 1)
    a = a_ref[...]
    diagonal = jnp.sum(jnp.where(lane == sub, a, 0.0), axis=1, keepdims=True)
    scale = 1.0 / jnp.sqrt(diagonal)
    return jnp.where(lane >= sub, a * scale, 0.0), m_ref[...] * scale


def unit(size):
    sub = lax.broadcasted_iota(jnp.int32, (size, size), 0)
    lane = lax.broadcasted_iota(jnp.int32, (size, size), 1)
    return jnp.where(lane == sub, 1.0, 0.0).astype(jnp.float32)


def factor_kernel(
    nr, nc,
    panel, trailing, block, trail, upper_out, coupling_out, weights_out,
    gram, gram_stage, col_stage, gram_sum, cross, cross_stage, cross_sum, work, minv, inv, square,
    load_sem, y_send, y_recv, half_send, half_recv, fwd_send, fwd_recv,
    rs_send, rs_recv, cx_send, cx_recv, ag_send, ag_recv, xrs_send, xrs_recv, xag_send, xag_recv,
):
    me_r, me_c = lax.axis_index("rows"), lax.axis_index("cols")
    depth, width = panel.shape
    half = nc // 2
    side, place = me_c // half, lax.rem(me_c, half)
    across = lax.rem(me_c + half, nc)
    chunk = depth // CHUNKS
    piece = width // nr
    groups = cross.shape[0]
    per_group = ITEMS // groups
    deep = depth // per_group
    wide = width // groups
    cross_piece = wide // nr
    hw = width // 2
    sends = []

    def remote(src, dst, send, recv, where):
        copy = pltpu.make_async_remote_copy(
            src_ref=src, dst_ref=dst, send_sem=send, recv_sem=recv, device_id=where, device_id_type=MESH
        )
        copy.start()
        sends.append(copy)
        return copy

    load_panel = pltpu.make_async_copy(panel, block.at[me_c], load_sem.at[0])
    load_panel.start()
    load_trail = pltpu.make_async_copy(trailing, trail, load_sem.at[1])
    load_trail.start()

    barrier = pltpu.get_barrier_semaphore()
    for d in range(1, nr):
        pl.semaphore_signal(barrier, inc=1, device_id={"rows": lax.rem(me_r + d, nr)}, device_id_type=MESH)
    for d in range(1, nc):
        pl.semaphore_signal(barrier, inc=1, device_id={"cols": lax.rem(me_c + d, nc)}, device_id_type=MESH)
    pl.semaphore_wait(barrier, nr + nc - 2)

    def item(k):
        return pl.ds((k % per_group) * deep, deep), pl.ds((k // per_group) * wide, wide)

    y_copies = []

    def send_across(k):
        rows, lanes = item(k)
        y_copies.append(
            remote(panel.at[rows, lanes], block.at[me_c, rows, lanes], y_send.at[k], y_recv.at[k], {"cols": across})
        )

    for k in range(EARLY):
        send_across(k)
    half_copies = []
    for d in range(1, half):
        peer = side * half + lax.rem(place + d, half)
        half_copies.append(remote(panel, block.at[me_c], half_send.at[d], half_recv.at[d], {"cols": peer}))

    def add_cross(source):
        def step(i, carry):
            rows = pl.ds(pl.multiple_of(i * chunk, chunk), chunk)
            long = pl.ds(pl.multiple_of(source * depth + i * chunk, chunk), chunk)
            product = dot_t(block[source, rows, :], trail[long, :])
            for g in range(groups):
                cross[g] += product[g * wide : (g + 1) * wide, :]
            return carry

        lax.fori_loop(0, CHUNKS, step, 0)

    def add_item(source, k):
        rows, lanes = item(k)
        long = pl.ds(pl.multiple_of(source * depth + (k % per_group) * deep, deep), deep)
        cross[k // per_group] += dot_t(block[source, rows, lanes], trail[long, :])

    load_panel.wait()
    gram[...] = jnp.zeros_like(gram)

    def gram_step(i, carry):
        rows = block[me_c, pl.ds(pl.multiple_of(i * chunk, chunk), chunk), :]
        gram[...] += dot_t(rows, rows)
        return carry

    lax.fori_loop(0, CHUNKS, gram_step, 0)

    def scatter(total, stage, send, recv, piece=piece):
        copies = []
        for d in range(1, nr):
            peer = lax.rem(me_r + d, nr)
            rows = pl.ds(pl.multiple_of(peer * piece, piece), piece)
            copies.append(remote(total.at[rows], stage.at[d], send.at[d], recv.at[d], {"rows": peer}))
        return copies

    def gather(total, send, recv, piece=piece):
        rows = pl.ds(pl.multiple_of(me_r * piece, piece), piece)
        return [
            remote(total.at[rows], total.at[rows], send.at[d], recv.at[d], {"rows": lax.rem(me_r + d, nr)})
            for d in range(1, nr)
        ]

    def arrived(copies):
        for copy in copies:
            copy.wait_recv()

    mine = pl.ds(pl.multiple_of(me_r * piece, piece), piece)
    cross_mine = pl.ds(pl.multiple_of(me_r * cross_piece, cross_piece), cross_piece)

    def summed(total, stage, mine=mine):
        value = total[mine, :]
        for d in range(1, nr):
            value = value + stage[d]
        return value

    gram_rs = scatter(gram, gram_stage, rs_send, rs_recv)
    load_trail.wait()
    cross[...] = jnp.zeros_like(cross)
    add_cross(me_c)
    arrived(gram_rs)
    col_stage[me_c] = summed(gram, gram_stage)
    exchange = [
        remote(col_stage.at[me_c], col_stage.at[me_c], cx_send.at[d], cx_recv.at[d], {"cols": lax.rem(me_c + d, nc)})
        for d in range(1, nc)
    ]
    for k in range(EARLY, ITEMS):
        send_across(k)
    for d in range(1, half):
        half_copies[d - 1].wait_recv()
        source = side * half + lax.rem(place + half - d, half)
        add_cross(source)
    arrived(exchange)
    value = col_stage[0]
    for c in range(1, nc):
        value = value + col_stage[c]
    gram_sum[mine, :] = value
    gram_ag = gather(gram_sum, ag_send, ag_recv)

    forwards = {}

    def take(k):
        y_copies[k].wait_recv()
        rows, lanes = item(k)
        for d in range(1, half):
            peer = side * half + lax.rem(place + d, half)
            slot = (d - 1) * ITEMS + k
            part = block.at[across, rows, lanes]
            forwards[d, k] = remote(part, part, fwd_send.at[slot], fwd_recv.at[slot], {"cols": peer})
        add_item(across, k)

    def take_forward(k):
        for d in range(1, half):
            forwards[d, k].wait_recv()
            source = (1 - side) * half + lax.rem(place + half - d, half)
            add_item(source, k)

    cross_rs, cross_ag = {}, {}

    def start_cross(g):
        cross_rs[g] = scatter(cross.at[g], cross_stage.at[g], xrs_send.at[g], xrs_recv.at[g], cross_piece)

    def share_cross(g):
        arrived(cross_rs[g])
        cross_sum[g, cross_mine, :] = summed(cross.at[g], cross_stage.at[g], cross_mine)
        cross_ag[g] = gather(cross_sum.at[g], xag_send.at[g], xag_recv.at[g], cross_piece)

    pending = []
    for k in range(ITEMS):
        pending.append(([functools.partial(take_forward, k - 1)] if k % per_group else []) + [functools.partial(take, k)])
        if k % per_group == per_group - 1:
            pending[-1].append(functools.partial(take_forward, k))
            pending[-1].append(functools.partial(start_cross, k // per_group))
    for g in range(groups - 1):
        pending[(g + 1) * per_group + 2].append(functools.partial(share_cross, g))

    def advance():
        for task in pending.pop(0):
            task()

    def run(first, last, more):
        eliminate(work, minv, first, last)
        for _ in range(more):
            advance()

    for _ in range(EARLY):
        advance()
    arrived(gram_ag)
    work[...] = gram_sum[pl.ds(0, hw), pl.ds(0, hw)]
    minv[...] = unit(hw)
    quarter = hw // 4
    for q in range(4):
        run(q * quarter, (q + 1) * quarter, MORE[q])
    upper1, inverse1 = scale_rows(work, minv)
    cross1 = dot(inverse1, gram_sum[pl.ds(0, hw), pl.ds(hw, hw)])
    upper_out[pl.ds(0, hw), pl.ds(0, hw)] = upper1
    upper_out[pl.ds(0, hw), pl.ds(hw, hw)] = cross1
    upper_out[pl.ds(hw, hw), pl.ds(0, hw)] = jnp.zeros_like(upper1)
    work[...] = gram_sum[pl.ds(hw, hw), pl.ds(hw, hw)] - dot_t(cross1, cross1)
    inv[pl.ds(0, hw), pl.ds(0, hw)] = inverse1
    minv[...] = unit(hw)
    for q in range(4):
        run(q * quarter, (q + 1) * quarter, MORE[4 + q])
    upper2, inverse2 = scale_rows(work, minv)
    upper_out[pl.ds(hw, hw), pl.ds(hw, hw)] = upper2
    inverse1 = inv[pl.ds(0, hw), pl.ds(0, hw)]
    corner = -dot(inverse2, dot_t(upper_out[pl.ds(0, hw), pl.ds(hw, hw)], inverse1))
    inv[pl.ds(0, hw), pl.ds(hw, hw)] = jnp.zeros_like(inverse1)
    inv[pl.ds(hw, hw), pl.ds(0, hw)] = corner
    inv[pl.ds(hw, hw), pl.ds(hw, hw)] = inverse2
    while pending:
        advance()
    inverse = inv[...]
    square[...] = dot_t(inverse, inverse)
    last = slice((groups - 1) * wide, groups * wide)
    coupling_out[...] = jnp.zeros_like(coupling_out)
    weights_out[...] = jnp.zeros_like(weights_out)
    for g in range(groups - 1):
        arrived(cross_ag[g])
        part = cross_sum[g]
        coupling_out[...] += dot(inv[:, g * wide : (g + 1) * wide], part)
        weights_out[...] += dot(square[:, g * wide : (g + 1) * wide], part)
    share_cross(groups - 1)
    arrived(cross_ag[groups - 1])
    part = cross_sum[groups - 1]
    weights_out[...] += dot(square[:, last], part)
    coupling_out[...] += dot(inv[:, last], part)
    for copy in sends:
        copy.wait_send()


def transposed_kernel(
    nr, nc,
    panel, trailing, block, trail, upper_out, coupling_out, weights_out, inv, cross_sum, square, mixed,
    gram, half_stage, half_sum, gram_stage, col_stage, gram_sum, cross, early_stage, tile_stage, pair_stage, late_stage, turned,
    work, minv,
    load_sem, greet_sem, bulk_sem, small_sem, y_recv, half_recv, fwd_recv, gram_recv, cross_recv,
):
    me_r, me_c = lax.axis_index("rows"), lax.axis_index("cols")
    depth, width = panel.shape
    side, place = me_c // 2, lax.rem(me_c, 2)
    partner = side * 2 + 1 - place
    across = (1 - side) * 2 + place
    behind = (1 - side) * 2 + 1 - place
    hw = width // 2
    piece = hw // nr
    head = depth // 8
    tall = depth - head
    turns = turn_plan(width)
    small_rows = []

    def remote(src, dst, send, recv, where):
        copy = pltpu.make_async_remote_copy(
            src_ref=src, dst_ref=dst, send_sem=send, recv_sem=recv, device_id=where, device_id_type=MESH
        )
        copy.start()
        return copy

    def small(src, dst, recv, where):
        small_rows.append(math.prod(src.shape) // width)
        return remote(src, dst, small_sem, recv, where)

    def drain(ref, sem):
        pltpu.make_async_copy(ref, ref, sem).wait()

    load_panel = pltpu.make_async_copy(panel, block.at[me_c], load_sem.at[0])
    load_panel.start()
    load_trail = pltpu.make_async_copy(trailing, trail, load_sem.at[1])
    load_trail.start()

    barrier = pltpu.get_barrier_semaphore()
    bits = [1 << b for b in range(nr.bit_length() - 1)]
    near = [me_r + bit - 2 * bit * lax.rem(me_r // bit, 2) for bit in bits]

    def greet(semaphore):
        for peer in near:
            pl.semaphore_signal(semaphore, inc=1, device_id={"rows": peer}, device_id_type=MESH)

    greet(barrier)
    for peer in (partner, across):
        pl.semaphore_signal(barrier, inc=1, device_id={"cols": peer}, device_id_type=MESH)
    pl.semaphore_wait(barrier, len(near) + 2)

    top = pl.ds(0, head)
    rest = pl.ds(head, tall)
    head_copy = remote(panel.at[top], block.at[me_c, top], bulk_sem, y_recv.at[0], {"cols": across})
    y_copies = []

    def send_turn():
        t = len(y_copies)
        part = turned.at[me_c, pl.ds(*turns[t]), rest]
        y_copies.append(remote(part, part, bulk_sem, y_recv.at[1 + t], {"cols": across}))

    greet(greet_sem.at[0])
    load_panel.wait()
    cut = depth // 16

    def turn_step(i, carry):
        rows = pl.ds(pl.multiple_of(i * cut, cut), cut)
        turned[me_c, :, rows] = block[me_c, rows, :].T
        return carry

    lax.fori_loop(0, 16, turn_step, 0)
    for met in range(len(near) - 2):
        pl.semaphore_wait(greet_sem.at[met], len(near))
        greet(greet_sem.at[met + 1])
    for _ in range(AHEAD):
        send_turn()
    gram[...] = jnp.zeros_like(gram)
    step_rows = depth // 4

    def gram_step(i, carry):
        rows = pl.ds(pl.multiple_of(i * step_rows, step_rows), step_rows)
        gram[...] += dot(turned[me_c, :, rows], block[me_c, rows, :])
        return carry

    lax.fori_loop(0, 4, gram_step, 0)
    pl.semaphore_wait(greet_sem.at[len(near) - 2], len(near))

    def scatter(total, stage, recv, where):
        for d in range(1, nr):
            peer = lax.rem(me_r + d, nr)
            small(total.at[where(peer)], stage.at[d], recv, {"rows": peer})

    def gather(total, recv, where):
        part = total.at[where(me_r)]
        for d in range(1, nr):
            small(part, part, recv, {"rows": lax.rem(me_r + d, nr)})

    def arrived(stage, recv):
        drain(stage.at[pl.ds(1, nr - 1)], recv)

    def summed(total, stage, where):
        value = total[where(me_r)]
        for d in range(1, nr):
            value = value + stage[d]
        return value

    def bands(count):
        return lambda peer: (pl.ds(pl.multiple_of(peer * count, count), count), slice(None))

    def tiles(count):
        half = cross.shape[1] // 2
        return lambda peer: (
            pl.ds(pl.multiple_of(peer // 2 * count, count), count),
            pl.ds(pl.multiple_of(lax.rem(peer, 2) * half, half), half),
        )

    def long(source, first, count):
        return pl.ds(pl.multiple_of(source * depth + first, head), count)

    def add_all(source):
        def step(i, carry):
            first = i * step_rows
            rows = pl.ds(pl.multiple_of(first, step_rows), step_rows)
            cross[...] += dot3(turned[source, :, rows], trail[long(source, first, step_rows), :])
            return carry

        lax.fori_loop(0, 4, step, 0)

    def add_head(source):
        cross[...] += dot_t(block[source, top, :], trail[long(source, 0, head), :])

    def add_lanes(source, first, count):
        lanes = pl.ds(first, count)
        cross[lanes, :] += dot3(turned[source, lanes, rest], trail[long(source, head, tall), :])

    known = turns[6][0]
    block_rows = depth // 4

    def mix(start):
        tile = square[:, hw:]
        lane = lax.broadcasted_iota(jnp.int32, tile.shape, 1)
        m_hi, m_lo = split(jnp.where(lane < hw // 2, pltpu.roll(tile, hw // 2, 1), tile))
        low = lax.broadcasted_iota(jnp.int32, (block_rows, hw), 1) >= hw // 2

        def step(i, carry):
            i = i + start
            rows = pl.ds(pl.multiple_of(lax.rem(i, 4) * block_rows, block_rows), block_rows)
            here = pl.ds(pl.multiple_of(i * block_rows, block_rows), block_rows)
            p_hi, p_lo = split(block[side * 2 + i // 4, rows, :])
            product = mul(p_hi, m_hi) + (mul(p_lo, m_hi) + mul(p_hi, m_lo))
            high = product.astype(jnp.bfloat16)
            wide = high.astype(jnp.float32)
            mixed[here, pl.ds(0, hw)] = jnp.where(low, product - wide, wide).astype(jnp.bfloat16)
            mixed[here, pl.ds(hw, hw)] = high
            return carry

        lax.fori_loop(0, 4, step, 0)

    def update_own():
        weights_out[...] += dot3(square[:, hw:known], cross_sum[pl.ds(hw, known - hw), :])
        w_hi, w_lo = split(weights_out[...])
        count = 2 * block_rows

        def step(i, carry):
            rows = pl.ds(pl.multiple_of(lax.rem(i, 2) * count, count), count)
            here = pl.ds(pl.multiple_of(side * 2 * depth + i * count, count), count)
            p_hi, p_lo = split(block[side * 2 + i // 2, rows, :])
            trail[here, :] -= mul(p_hi, w_hi) + (mul(p_lo, w_hi) + mul(p_hi, w_lo))
            return carry

        lax.fori_loop(0, 4, step, 0)

    def turn_back(source, first):
        lanes = pl.ds(first, hw)

        def step(i, carry):
            rows = pl.ds(pl.multiple_of(head + i * head, head), head)
            block[source, rows, lanes] = turned[source, lanes, rows].T
            return carry

        lax.fori_loop(0, tall // head, step, 0)

    mine = pl.ds(pl.multiple_of(place * hw, hw), hw)
    other = pl.ds(pl.multiple_of(hw - place * hw, hw), hw)
    gram_pair = small(gram.at[other], half_stage, gram_recv.at[0], {"cols": partner})
    turned_copy = remote(turned.at[me_c], turned.at[me_c], bulk_sem, half_recv.at[1], {"cols": partner})
    load_trail.wait()
    cross[...] = jnp.zeros_like(cross)
    add_all(me_c)
    gram_pair.wait_recv()
    half_sum[...] = gram[mine, :] + half_stage[...]
    scatter(half_sum, gram_stage, gram_recv.at[1], bands(piece))
    head_copy.wait_recv()
    part = block.at[across, top]
    head_forward = remote(part, part, bulk_sem, fwd_recv.at[0], {"cols": partner})
    add_head(across)
    turned_copy.wait_recv()
    add_all(partner)
    arrived(gram_stage, gram_recv.at[1])
    col_stage[side] = summed(half_sum, gram_stage, bands(piece))
    exchange = small(col_stage.at[side], col_stage.at[side], gram_recv.at[2], {"cols": across})
    while len(y_copies) < len(turns):
        send_turn()
    head_forward.wait_recv()
    add_head(behind)

    forwards = {}

    def take(t):
        y_copies[t].wait_recv()
        part = turned.at[across, pl.ds(*turns[t]), rest]
        forwards[t] = remote(part, part, bulk_sem, fwd_recv.at[1 + t], {"cols": partner})

    def take_forward(t):
        forwards[t].wait_recv()

    late_first = turns[7][0]
    twin = me_r + 1 - 2 * lax.rem(me_r, 2)
    bounds = ((0, hw), turns[4], turns[5], turns[6])
    stages = (early_stage, tile_stage.at[0], tile_stage.at[1], tile_stage.at[2])
    wheres = (bands(hw // nr),) + (tiles(turns[6][1] * 2 // nr),) * 3

    def start_cross(g):
        scatter(cross.at[pl.ds(*bounds[g])], stages[g], cross_recv.at[2 * g], wheres[g])

    def share_cross(g):
        arrived(stages[g], cross_recv.at[2 * g])
        total = cross_sum.at[pl.ds(*bounds[g])]
        total[wheres[g](me_r)] = summed(cross.at[pl.ds(*bounds[g])], stages[g], wheres[g])
        gather(total, cross_recv.at[2 * g + 1], wheres[g])

    def shared(g):
        arrived(stages[g], cross_recv.at[2 * g + 1])

    def lanes_of(t):
        first, count = turns[t]
        return pl.ds(first, count), pl.ds(first - late_first, count)

    def start_pair(t):
        lanes, late = lanes_of(t)
        mine = pair_stage.at[lax.rem(me_r, 2), late]
        mine[...] = cross[lanes, :]
        return small(mine, mine, cross_recv.at[8], {"rows": twin})

    def spread_pair(t, pair):
        _, late = lanes_of(t)
        pair.wait_recv()
        mine = late_stage.at[me_r, late]
        mine[...] = pair_stage[0, late, :] + pair_stage[1, late, :]
        for d in range(2, nr, 2):
            small(mine, mine, cross_recv.at[9], {"rows": lax.rem(me_r + d, nr)})

    def finish_pair(t):
        lanes, late = lanes_of(t)
        drain(late_stage.at[pl.ds(1, nr // 2 - 1), late], cross_recv.at[9])
        value = late_stage[lax.rem(me_r, 2), late, :]
        for step in range(2, nr, 2):
            value = value + late_stage[lax.rem(me_r, 2) + step, late, :]
        cross_sum[lanes, :] = value

    def spread(t):
        lanes, late = lanes_of(t)
        mine = late_stage.at[me_r, late]
        mine[...] = cross[lanes, :]
        for d in range(1, nr):
            small(mine, mine, cross_recv.at[10], {"rows": lax.rem(me_r + d, nr)})

    def finish(t):
        lanes, late = lanes_of(t)
        drain(late_stage.at[pl.ds(1, nr - 1), late], cross_recv.at[10])
        value = late_stage[0, late, :]
        for step in range(1, nr):
            value = value + late_stage[step, late, :]
        cross_sum[lanes, :] = value

    exchange.wait_recv()
    gram_half = gram_sum.at[mine]
    gram_half[pl.ds(pl.multiple_of(me_r * piece, piece), piece), :] = col_stage[0] + col_stage[1]
    gather(gram_half, gram_recv.at[3], bands(piece))
    take(0)
    arrived(gram_stage, gram_recv.at[3])
    gram_swap = small(gram_half, gram_half, gram_recv.at[4], {"cols": partner})
    half_copy = remote(panel, block.at[me_c], bulk_sem, half_recv.at[0], {"cols": partner})
    gram_swap.wait_recv()
    work[...] = gram_sum[pl.ds(0, hw), pl.ds(0, hw)]
    minv[...] = unit(hw)
    eighth = hw // 8
    take_forward(0)
    eliminate(work, minv, 0, 2 * eighth)
    take(1)
    eliminate(work, minv, 2 * eighth, 8 * eighth)
    take_forward(1)
    upper1, inverse1 = scale_rows(work, minv)
    cross1 = dot(inverse1, gram_sum[pl.ds(0, hw), pl.ds(hw, hw)])
    upper_out[pl.ds(0, hw), pl.ds(0, hw)] = upper1
    upper_out[pl.ds(0, hw), pl.ds(hw, hw)] = cross1
    upper_out[pl.ds(hw, hw), pl.ds(0, hw)] = jnp.zeros_like(upper1)
    work[...] = gram_sum[pl.ds(hw, hw), pl.ds(hw, hw)] - dot_t(cross1, cross1)
    inv[pl.ds(0, hw), pl.ds(0, hw)] = inverse1
    minv[...] = unit(hw)
    take(2)
    eliminate(work, minv, 0, 5 * eighth)
    take_forward(2)
    take(3)
    add_lanes(across, 0, hw)
    eliminate(work, minv, 5 * eighth, 6 * eighth)
    take_forward(3)
    add_lanes(behind, 0, hw)
    start_cross(0)
    eliminate(work, minv, 6 * eighth, 8 * eighth)
    take(4)
    upper2, inverse2 = scale_rows(work, minv)
    upper_out[pl.ds(hw, hw), pl.ds(hw, hw)] = upper2
    inverse1 = inv[pl.ds(0, hw), pl.ds(0, hw)]
    corner = -dot(inverse2, dot_t(upper_out[pl.ds(0, hw), pl.ds(hw, hw)], inverse1))
    inv[pl.ds(0, hw), pl.ds(hw, hw)] = jnp.zeros_like(inverse1)
    inv[pl.ds(hw, hw), pl.ds(0, hw)] = corner
    inv[pl.ds(hw, hw), pl.ds(hw, hw)] = inverse2
    inverse = inv[...]
    square[...] = dot_t(inverse, inverse)
    add_lanes(across, *turns[4])
    take_forward(4)
    add_lanes(behind, *turns[4])
    start_cross(1)
    turn_back(across, 0)
    share_cross(0)
    take(5)
    add_lanes(across, *turns[5])
    turn_back(behind, 0)
    take_forward(5)
    add_lanes(behind, *turns[5])
    start_cross(2)
    half_copy.wait_recv()
    share_cross(1)
    mix(0)
    take(6)
    add_lanes(across, *turns[6])
    mix(4)
    take_forward(6)
    add_lanes(behind, *turns[6])
    start_cross(3)
    share_cross(2)
    shared(0)
    weights_out[...] = dot(square[:, :hw], cross_sum[pl.ds(0, hw), :])
    take(7)
    add_lanes(across, *turns[7])
    take(8)
    add_lanes(across, *turns[8])
    take_forward(7)
    add_lanes(behind, *turns[7])
    pair = start_pair(7)
    take_forward(8)
    add_lanes(behind, *turns[8])
    spread(8)
    turn_back(across, hw)
    share_cross(3)
    turn_back(behind, hw)
    spread_pair(7, pair)
    shared(1)
    shared(2)
    update_own()
    coupling_out[...] = dot(inv[:, :hw], cross_sum[pl.ds(0, hw), :])
    shared(3)
    finish_pair(7)
    finish(8)
    drain(turned, bulk_sem)
    total = sum(small_rows)
    drain(block.at[0, pl.ds(0, total)], small_sem)


def update_kernel(
    shrink, block, trailing, upper, coupling, weights, r_factor, r_cross, updated,
    small, w_hi, w_lo, out, small_sem, out_sem,
):
    small[0] = upper[...] * shrink
    small[1] = coupling[...] * shrink
    copies = [
        pltpu.make_async_copy(small.at[0], r_factor, small_sem.at[0]),
        pltpu.make_async_copy(small.at[1], r_cross, small_sem.at[1]),
    ]
    for copy in copies:
        copy.start()
    w = weights[...]
    high = w.astype(jnp.bfloat16)
    w_hi[...] = high
    w_lo[...] = (w - high.astype(jnp.float32)).astype(jnp.bfloat16)
    tile = out.shape[0] // TILES

    def mul(left, right):
        return jnp.dot(left, right, preferred_element_type=jnp.float32)

    def window(i):
        return pl.ds(pl.multiple_of(i * tile, tile), tile)

    def store(i):
        return pltpu.make_async_copy(out.at[window(i)], updated.at[window(i)], out_sem.at[i])

    def step(i, carry):
        rows = window(i)
        p = block[rows, :]
        p_hi = p.astype(jnp.bfloat16)
        p_lo = (p - p_hi.astype(jnp.float32)).astype(jnp.bfloat16)
        product = mul(p_hi, w_hi[...]) + (mul(p_lo, w_hi[...]) + mul(p_hi, w_lo[...]))
        out[rows, :] = trailing[rows, :] - product
        store(i).start()
        return carry

    lax.fori_loop(0, TILES, step, 0)
    for i in range(TILES):
        store(i).wait()
    for copy in copies:
        copy.wait()


def finish_kernel(
    shrink, block, trailing, upper, coupling, weights, inv, total, square, mixed, r_factor, r_cross, updated,
    small, w_hi, w_lo, c_all, out, small_sem, out_sem,
):
    small[0] = upper[...] * shrink
    factor_copy = pltpu.make_async_copy(small.at[0], r_factor, small_sem.at[0])
    factor_copy.start()
    hw = inv.shape[0] // 2
    part = hw // 2
    c_hi, c_lo = split(total[pl.ds(hw + part, part), :])
    c_all[pl.ds(0, part), :] = c_hi
    c_all[pl.ds(part, part), :] = c_hi
    c_all[pl.ds(hw, part), :] = c_lo
    c_all[pl.ds(hw + part, part), :] = jnp.zeros_like(c_lo)
    depth = out.shape[0]
    own = depth // 2
    side = lax.axis_index("cols") // 2
    tile = depth // TILES

    def window(start, first, count):
        return pl.ds(pl.multiple_of(start + first, tile // 2), count)

    def store(rows):
        pltpu.make_async_copy(out.at[rows], updated.at[rows], out_sem).start()

    first = 0
    for count in (tile // 2,) * TILES:
        rows = window(side * own, first, count)
        out[rows, :] = trailing[rows, :] - mul(mixed[pl.ds(first, count), :], c_all[...])
        store(rows)
        first += count
    row = lax.broadcasted_iota(jnp.int32, (hw, total.shape[1]), 0)
    late = jnp.where(row < part, 0.0, total[pl.ds(hw, hw), :])
    w_hi[...], w_lo[...] = split(weights[...] + dot3(square[:, hw:], late))
    first = 0
    for count in (tile // 2,) + (tile,) * (TILES // 2 - 1) + (tile // 2,):
        rows = window((1 - side) * own, first, count)
        p_hi, p_lo = split(block[rows, :])
        product = mul(p_hi, w_hi[...]) + (mul(p_lo, w_hi[...]) + mul(p_hi, w_lo[...]))
        out[rows, :] = trailing[rows, :] - product
        store(rows)
        first += count
    small[1] = (coupling[...] + dot3(inv[:, hw:], total[hw:, :])) * shrink
    cross_copy = pltpu.make_async_copy(small.at[1], r_cross, small_sem.at[1])
    cross_copy.start()
    pltpu.make_async_copy(out, updated, out_sem).wait()
    factor_copy.wait()
    cross_copy.wait()


def local(nr, nc, panel_cols, trailing):
    depth, width = panel_cols.shape
    rows, cols = trailing.shape
    half = nc // 2
    piece = width // nr
    groups = 2 if width % (2 * 8 * nr) == 0 else 1
    wide = width // groups
    f32 = jnp.float32
    square = jax.ShapeDtypeStruct((width, width), f32)
    tall = jax.ShapeDtypeStruct((width, cols), f32)
    dma = pltpu.SemaphoreType.DMA
    vmem = pl.BlockSpec(memory_space=pltpu.VMEM)
    hbm = pl.BlockSpec(memory_space=pltpu.HBM)
    fine = nc == 4 and nr >= 4 and nr & (nr - 1) == 0 and width % 256 == 0 and (width // 2) % (8 * nr) == 0 and (width // 4) % (8 * nr) == 0 and depth % 2048 == 0 and width // 8 == 4 * nr and cols % 256 == 0
    if fine:
        gram_scratch = [
            pltpu.VMEM((width // 2, width), f32),
            pltpu.VMEM((width // 2, width), f32),
            pltpu.VMEM((nr, piece // 2, width), f32),
            pltpu.VMEM((2, piece // 2, width), f32),
        ]
        body, turns = transposed_kernel, len(turn_plan(width))
        cross_scratch = [
            pltpu.VMEM((width, cols), f32),
            pltpu.VMEM((nr, width // 2 // nr, cols), f32),
            pltpu.VMEM((3, nr, width // 4 // nr, cols // 2), f32),
            pltpu.VMEM((2, width // 4, cols), f32),
            pltpu.VMEM((nr, width // 4, cols), f32),
            pltpu.VMEM((nc, width, depth), f32),
        ]
        items = 1 + turns
        sems = [dma((2,)), pltpu.SemaphoreType.REGULAR((nr.bit_length() - 2,)), dma, dma, dma((items,)), dma((2,)), dma((items,)), dma((5,)), dma((11,))]
    else:
        body = factor_kernel
        gram_scratch = [pltpu.VMEM((nr, piece, width), f32), pltpu.VMEM((nc, piece, width), f32)]
        sems = [
            dma((2,)),
            dma((ITEMS,)), dma((ITEMS,)),
            dma((half,)), dma((half,)),
            dma((ITEMS * half,)), dma((ITEMS * half,)),
            dma((nr,)), dma((nr,)),
            dma((nc,)), dma((nc,)),
            dma((nr,)), dma((nr,)),
            dma((groups, nr)), dma((groups, nr)),
            dma((groups, nr)), dma((groups, nr)),
        ]
        cross_scratch = [
            pltpu.VMEM((groups, wide, cols), f32),
            pltpu.VMEM((groups, nr, wide // nr, cols), f32),
            pltpu.VMEM((groups, wide, cols), f32),
        ]
    shapes = (jax.ShapeDtypeStruct((nc, depth, width), f32), jax.ShapeDtypeStruct((rows, cols), f32), square, tall, tall)
    shapes += (square, tall, square, jax.ShapeDtypeStruct((2 * depth, width), jnp.bfloat16)) if fine else ()
    block, *results = pl.pallas_call(
        functools.partial(body, nr, nc),
        out_shape=shapes,
        in_specs=[hbm, hbm],
        out_specs=(vmem,) * len(shapes),
        scratch_shapes=[
            pltpu.VMEM((width, width), f32),
            *gram_scratch,
            pltpu.VMEM((width, width), f32),
            *cross_scratch,
            pltpu.VMEM((width // 2, width // 2), f32),
            pltpu.VMEM((width // 2, width // 2), f32),
            *[pltpu.VMEM((width, width), f32)] * (0 if fine else 2),
            *sems,
        ],
        compiler_params=pltpu.CompilerParams(
            collective_id=0, has_side_effects=True, vmem_limit_bytes=(32 if fine else 20) * 1024 * 1024
        ),
        name="factor",
    )(*(pltpu.with_memory_space_constraint(x, pltpu.HBM) for x in (panel_cols, trailing)))

    shrink = 1.0 / math.sqrt(rows * nr)
    r_factor, r_cross, updated = pl.pallas_call(
        functools.partial(finish_kernel if fine else update_kernel, shrink),
        out_shape=(square, tall, jax.ShapeDtypeStruct((rows, cols), f32)),
        in_specs=[vmem] * len(shapes),
        out_specs=(hbm,) * 3,
        scratch_shapes=[
            pltpu.VMEM((2, width, cols), f32),
            *[pltpu.VMEM((width, cols), jnp.bfloat16)] * (3 if fine else 2),
            pltpu.VMEM((rows, cols), f32),
            dma((2,)),
            dma if fine else dma((TILES,)),
        ],
        compiler_params=pltpu.CompilerParams(vmem_limit_bytes=24 * 1024 * 1024),
        name="update",
    )(block.reshape(rows, width), *results)
    return r_factor, r_cross, updated


def solution(mesh):
    P = jax.sharding.PartitionSpec
    body = functools.partial(local, mesh.shape["rows"], mesh.shape["cols"])
    in_specs = (P(("rows", "cols"), None), P("rows", "cols"))
    out_specs = (P(), P(None, "cols"), P("rows", "cols"))
    return jax.shard_map(body, mesh=mesh, in_specs=in_specs, out_specs=out_specs, check_vma=False)
```

```python
import functools
import math

import jax
import jax.numpy as jnp
from jax import lax
from jax.experimental import pallas as pl
from jax.experimental.pallas import tpu as pltpu

MESH = pl.DeviceIdType.MESH
HIGHEST = lax.Precision.HIGHEST
CHUNKS = 8
ITEMS = 8
EARLY = 3
MORE = (1, 1, 1, 0, 1, 0, 1, 0)
GROUP = 4
TILES = 8
AHEAD = 1


def dot(left, right):
    return lax.dot_general(left, right, (((1,), (0,)), ((), ())), precision=HIGHEST, preferred_element_type=jnp.float32)


def dot_t(left, right):
    return lax.dot_general(left, right, (((0,), (0,)), ((), ())), precision=HIGHEST, preferred_element_type=jnp.float32)


def split(x):
    high = x.astype(jnp.bfloat16)
    return high, (x - high.astype(jnp.float32)).astype(jnp.bfloat16)


def mul(left, right):
    return jnp.dot(left, right, preferred_element_type=jnp.float32)


def dot3(left, right):
    left_hi, left_lo = split(left)
    right_hi, right_lo = split(right)
    count = left.shape[0]
    both = mul(jnp.concatenate([left_hi, left_lo], axis=0), right_hi)
    return both[:count] + (both[count:] + mul(left_hi, right_lo))


def turn_plan(width):
    eighth = width // 8
    counts = (eighth,) * 7 + (eighth - eighth // 4, eighth // 4)
    return [(sum(counts[:t]), counts[t]) for t in range(len(counts))]


def eliminate(a_ref, m_ref, first, last):
    size = a_ref.shape[0]
    sub = lax.broadcasted_iota(jnp.int32, (size, 1), 0)
    lane = lax.broadcasted_iota(jnp.int32, (size, size), 1)
    lane_row = lax.broadcasted_iota(jnp.int32, (1, size), 1)

    def step(index, carry):
        j = index * GROUP
        a = a_ref[...]
        rows = [a_ref[pl.ds(j + t, 1), :] for t in range(GROUP)]
        mrows = [m_ref[pl.ds(j + t, 1), :] for t in range(GROUP)]
        cols = [jnp.sum(jnp.where(lane == j + t, a, 0.0), axis=1, keepdims=True) for t in range(GROUP)]
        head = {
            (t, u): jnp.sum(jnp.where(lane_row == j + u, rows[t], 0.0), axis=1, keepdims=True)
            for t in range(GROUP)
            for u in range(t, GROUP)
        }
        m = m_ref[...]
        for t in range(GROUP):
            inverse = 1.0 / head[t, t]
            factor = jnp.where(sub > j + t, cols[t] * inverse, 0.0)
            ratio = {u: head[t, u] * inverse for u in range(t + 1, GROUP)}
            for u in range(t + 1, GROUP):
                cols[u] = cols[u] - factor * head[t, u]
            for u in range(t + 1, GROUP):
                for v in range(u, GROUP):
                    head[u, v] = head[u, v] - ratio[u] * head[t, v]
            for u in range(t + 1, GROUP):
                rows[u] = rows[u] - ratio[u] * rows[t]
                mrows[u] = mrows[u] - ratio[u] * mrows[t]
            a = a - factor * rows[t]
            m = m - factor * mrows[t]
        a_ref[...] = a
        m_ref[...] = m
        return carry

    lax.fori_loop(first // GROUP, last // GROUP, step, 0)


def scale_rows(a_ref, m_ref):
    size = a_ref.shape[0]
    sub = lax.broadcasted_iota(jnp.int32, (size, size), 0)
    lane = lax.broadcasted_iota(jnp.int32, (size, size), 1)
    a = a_ref[...]
    diagonal = jnp.sum(jnp.where(lane == sub, a, 0.0), axis=1, keepdims=True)
    scale = 1.0 / jnp.sqrt(diagonal)
    return jnp.where(lane >= sub, a * scale, 0.0), m_ref[...] * scale


def unit(size):
    sub = lax.broadcasted_iota(jnp.int32, (size, size), 0)
    lane = lax.broadcasted_iota(jnp.int32, (size, size), 1)
    return jnp.where(lane == sub, 1.0, 0.0).astype(jnp.float32)


def factor_kernel(
    nr, nc,
    panel, trailing, block, trail, upper_out, coupling_out, weights_out,
    gram, gram_stage, col_stage, gram_sum, cross, cross_stage, cross_sum, work, minv, inv, square,
    load_sem, y_send, y_recv, half_send, half_recv, fwd_send, fwd_recv,
    rs_send, rs_recv, cx_send, cx_recv, ag_send, ag_recv, xrs_send, xrs_recv, xag_send, xag_recv,
):
    me_r, me_c = lax.axis_index("rows"), lax.axis_index("cols")
    depth, width = panel.shape
    half = nc // 2
    side, place = me_c // half, lax.rem(me_c, half)
    across = lax.rem(me_c + half, nc)
    chunk = depth // CHUNKS
    piece = width // nr
    groups = cross.shape[0]
    per_group = ITEMS // groups
    deep = depth // per_group
    wide = width // groups
    cross_piece = wide // nr
    hw = width // 2
    sends = []

    def remote(src, dst, send, recv, where):
        copy = pltpu.make_async_remote_copy(
            src_ref=src, dst_ref=dst, send_sem=send, recv_sem=recv, device_id=where, device_id_type=MESH
        )
        copy.start()
        sends.append(copy)
        return copy

    load_panel = pltpu.make_async_copy(panel, block.at[me_c], load_sem.at[0])
    load_panel.start()
    load_trail = pltpu.make_async_copy(trailing, trail, load_sem.at[1])
    load_trail.start()

    barrier = pltpu.get_barrier_semaphore()
    for d in range(1, nr):
        pl.semaphore_signal(barrier, inc=1, device_id={"rows": lax.rem(me_r + d, nr)}, device_id_type=MESH)
    for d in range(1, nc):
        pl.semaphore_signal(barrier, inc=1, device_id={"cols": lax.rem(me_c + d, nc)}, device_id_type=MESH)
    pl.semaphore_wait(barrier, nr + nc - 2)

    def item(k):
        return pl.ds((k % per_group) * deep, deep), pl.ds((k // per_group) * wide, wide)

    y_copies = []

    def send_across(k):
        rows, lanes = item(k)
        y_copies.append(
            remote(panel.at[rows, lanes], block.at[me_c, rows, lanes], y_send.at[k], y_recv.at[k], {"cols": across})
        )

    for k in range(EARLY):
        send_across(k)
    half_copies = []
    for d in range(1, half):
        peer = side * half + lax.rem(place + d, half)
        half_copies.append(remote(panel, block.at[me_c], half_send.at[d], half_recv.at[d], {"cols": peer}))

    def add_cross(source):
        def step(i, carry):
            rows = pl.ds(pl.multiple_of(i * chunk, chunk), chunk)
            long = pl.ds(pl.multiple_of(source * depth + i * chunk, chunk), chunk)
            product = dot_t(block[source, rows, :], trail[long, :])
            for g in range(groups):
                cross[g] += product[g * wide : (g + 1) * wide, :]
            return carry

        lax.fori_loop(0, CHUNKS, step, 0)

    def add_item(source, k):
        rows, lanes = item(k)
        long = pl.ds(pl.multiple_of(source * depth + (k % per_group) * deep, deep), deep)
        cross[k // per_group] += dot_t(block[source, rows, lanes], trail[long, :])

    load_panel.wait()
    gram[...] = jnp.zeros_like(gram)

    def gram_step(i, carry):
        rows = block[me_c, pl.ds(pl.multiple_of(i * chunk, chunk), chunk), :]
        gram[...] += dot_t(rows, rows)
        return carry

    lax.fori_loop(0, CHUNKS, gram_step, 0)

    def scatter(total, stage, send, recv, piece=piece):
        copies = []
        for d in range(1, nr):
            peer = lax.rem(me_r + d, nr)
            rows = pl.ds(pl.multiple_of(peer * piece, piece), piece)
            copies.append(remote(total.at[rows], stage.at[d], send.at[d], recv.at[d], {"rows": peer}))
        return copies

    def gather(total, send, recv, piece=piece):
        rows = pl.ds(pl.multiple_of(me_r * piece, piece), piece)
        return [
            remote(total.at[rows], total.at[rows], send.at[d], recv.at[d], {"rows": lax.rem(me_r + d, nr)})
            for d in range(1, nr)
        ]

    def arrived(copies):
        for copy in copies:
            copy.wait_recv()

    mine = pl.ds(pl.multiple_of(me_r * piece, piece), piece)
    cross_mine = pl.ds(pl.multiple_of(me_r * cross_piece, cross_piece), cross_piece)

    def summed(total, stage, mine=mine):
        value = total[mine, :]
        for d in range(1, nr):
            value = value + stage[d]
        return value

    gram_rs = scatter(gram, gram_stage, rs_send, rs_recv)
    load_trail.wait()
    cross[...] = jnp.zeros_like(cross)
    add_cross(me_c)
    arrived(gram_rs)
    col_stage[me_c] = summed(gram, gram_stage)
    exchange = [
        remote(col_stage.at[me_c], col_stage.at[me_c], cx_send.at[d], cx_recv.at[d], {"cols": lax.rem(me_c + d, nc)})
        for d in range(1, nc)
    ]
    for k in range(EARLY, ITEMS):
        send_across(k)
    for d in range(1, half):
        half_copies[d - 1].wait_recv()
        source = side * half + lax.rem(place + half - d, half)
        add_cross(source)
    arrived(exchange)
    value = col_stage[0]
    for c in range(1, nc):
        value = value + col_stage[c]
    gram_sum[mine, :] = value
    gram_ag = gather(gram_sum, ag_send, ag_recv)

    forwards = {}

    def take(k):
        y_copies[k].wait_recv()
        rows, lanes = item(k)
        for d in range(1, half):
            peer = side * half + lax.rem(place + d, half)
            slot = (d - 1) * ITEMS + k
            part = block.at[across, rows, lanes]
            forwards[d, k] = remote(part, part, fwd_send.at[slot], fwd_recv.at[slot], {"cols": peer})
        add_item(across, k)

    def take_forward(k):
        for d in range(1, half):
            forwards[d, k].wait_recv()
            source = (1 - side) * half + lax.rem(place + half - d, half)
            add_item(source, k)

    cross_rs, cross_ag = {}, {}

    def start_cross(g):
        cross_rs[g] = scatter(cross.at[g], cross_stage.at[g], xrs_send.at[g], xrs_recv.at[g], cross_piece)

    def share_cross(g):
        arrived(cross_rs[g])
        cross_sum[g, cross_mine, :] = summed(cross.at[g], cross_stage.at[g], cross_mine)
        cross_ag[g] = gather(cross_sum.at[g], xag_send.at[g], xag_recv.at[g], cross_piece)

    pending = []
    for k in range(ITEMS):
        pending.append(([functools.partial(take_forward, k - 1)] if k % per_group else []) + [functools.partial(take, k)])
        if k % per_group == per_group - 1:
            pending[-1].append(functools.partial(take_forward, k))
            pending[-1].append(functools.partial(start_cross, k // per_group))
    for g in range(groups - 1):
        pending[(g + 1) * per_group + 2].append(functools.partial(share_cross, g))

    def advance():
        for task in pending.pop(0):
            task()

    def run(first, last, more):
        eliminate(work, minv, first, last)
        for _ in range(more):
            advance()

    for _ in range(EARLY):
        advance()
    arrived(gram_ag)
    work[...] = gram_sum[pl.ds(0, hw), pl.ds(0, hw)]
    minv[...] = unit(hw)
    quarter = hw // 4
    for q in range(4):
        run(q * quarter, (q + 1) * quarter, MORE[q])
    upper1, inverse1 = scale_rows(work, minv)
    cross1 = dot(inverse1, gram_sum[pl.ds(0, hw), pl.ds(hw, hw)])
    upper_out[pl.ds(0, hw), pl.ds(0, hw)] = upper1
    upper_out[pl.ds(0, hw), pl.ds(hw, hw)] = cross1
    upper_out[pl.ds(hw, hw), pl.ds(0, hw)] = jnp.zeros_like(upper1)
    work[...] = gram_sum[pl.ds(hw, hw), pl.ds(hw, hw)] - dot_t(cross1, cross1)
    inv[pl.ds(0, hw), pl.ds(0, hw)] = inverse1
    minv[...] = unit(hw)
    for q in range(4):
        run(q * quarter, (q + 1) * quarter, MORE[4 + q])
    upper2, inverse2 = scale_rows(work, minv)
    upper_out[pl.ds(hw, hw), pl.ds(hw, hw)] = upper2
    inverse1 = inv[pl.ds(0, hw), pl.ds(0, hw)]
    corner = -dot(inverse2, dot_t(upper_out[pl.ds(0, hw), pl.ds(hw, hw)], inverse1))
    inv[pl.ds(0, hw), pl.ds(hw, hw)] = jnp.zeros_like(inverse1)
    inv[pl.ds(hw, hw), pl.ds(0, hw)] = corner
    inv[pl.ds(hw, hw), pl.ds(hw, hw)] = inverse2
    while pending:
        advance()
    inverse = inv[...]
    square[...] = dot_t(inverse, inverse)
    last = slice((groups - 1) * wide, groups * wide)
    coupling_out[...] = jnp.zeros_like(coupling_out)
    weights_out[...] = jnp.zeros_like(weights_out)
    for g in range(groups - 1):
        arrived(cross_ag[g])
        part = cross_sum[g]
        coupling_out[...] += dot(inv[:, g * wide : (g + 1) * wide], part)
        weights_out[...] += dot(square[:, g * wide : (g + 1) * wide], part)
    share_cross(groups - 1)
    arrived(cross_ag[groups - 1])
    part = cross_sum[groups - 1]
    weights_out[...] += dot(square[:, last], part)
    coupling_out[...] += dot(inv[:, last], part)
    for copy in sends:
        copy.wait_send()


def transposed_kernel(
    nr, nc,
    panel, trailing, block, trail, upper_out, coupling_out, weights_out, inv, cross_sum, square, mixed,
    gram, half_stage, half_sum, gram_stage, col_stage, gram_sum, cross, early_stage, tile_stage, pair_stage, late_stage, turned,
    work, minv,
    load_sem, greet_sem, bulk_sem, small_sem, y_recv, half_recv, fwd_recv, gram_recv, cross_recv,
):
    me_r, me_c = lax.axis_index("rows"), lax.axis_index("cols")
    depth, width = panel.shape
    side, place = me_c // 2, lax.rem(me_c, 2)
    partner = side * 2 + 1 - place
    across = (1 - side) * 2 + place
    behind = (1 - side) * 2 + 1 - place
    hw = width // 2
    piece = hw // nr
    head = depth // 8
    tall = depth - head
    turns = turn_plan(width)
    small_rows = []

    def remote(src, dst, send, recv, where):
        copy = pltpu.make_async_remote_copy(
            src_ref=src, dst_ref=dst, send_sem=send, recv_sem=recv, device_id=where, device_id_type=MESH
        )
        copy.start()
        return copy

    def small(src, dst, recv, where):
        small_rows.append(math.prod(src.shape) // width)
        return remote(src, dst, small_sem, recv, where)

    def drain(ref, sem):
        pltpu.make_async_copy(ref, ref, sem).wait()

    load_panel = pltpu.make_async_copy(panel, block.at[me_c], load_sem.at[0])
    load_panel.start()
    load_trail = pltpu.make_async_copy(trailing, trail, load_sem.at[1])
    load_trail.start()

    barrier = pltpu.get_barrier_semaphore()
    bits = [1 << b for b in range(nr.bit_length() - 1)]
    near = [me_r + bit - 2 * bit * lax.rem(me_r // bit, 2) for bit in bits]

    def greet(semaphore):
        for peer in near:
            pl.semaphore_signal(semaphore, inc=1, device_id={"rows": peer}, device_id_type=MESH)

    greet(barrier)
    for peer in (partner, across):
        pl.semaphore_signal(barrier, inc=1, device_id={"cols": peer}, device_id_type=MESH)
    pl.semaphore_wait(barrier, len(near) + 2)

    top = pl.ds(0, head)
    rest = pl.ds(head, tall)
    head_copy = remote(panel.at[top], block.at[me_c, top], bulk_sem, y_recv.at[0], {"cols": across})
    y_copies = []

    def send_turn():
        t = len(y_copies)
        part = turned.at[me_c, pl.ds(*turns[t]), rest]
        y_copies.append(remote(part, part, bulk_sem, y_recv.at[1 + t], {"cols": across}))

    greet(greet_sem.at[0])
    load_panel.wait()
    cut = depth // 16

    def turn_step(i, carry):
        rows = pl.ds(pl.multiple_of(i * cut, cut), cut)
        turned[me_c, :, rows] = block[me_c, rows, :].T
        return carry

    lax.fori_loop(0, 16, turn_step, 0)
    for met in range(len(near) - 2):
        pl.semaphore_wait(greet_sem.at[met], len(near))
        greet(greet_sem.at[met + 1])
    for _ in range(AHEAD):
        send_turn()
    gram[...] = jnp.zeros_like(gram)
    step_rows = depth // 4

    def gram_step(i, carry):
        rows = pl.ds(pl.multiple_of(i * step_rows, step_rows), step_rows)
        gram[...] += dot(turned[me_c, :, rows], block[me_c, rows, :])
        return carry

    lax.fori_loop(0, 4, gram_step, 0)
    pl.semaphore_wait(greet_sem.at[len(near) - 2], len(near))

    def scatter(total, stage, recv, where):
        for d in range(1, nr):
            peer = lax.rem(me_r + d, nr)
            small(total.at[where(peer)], stage.at[d], recv, {"rows": peer})

    def gather(total, recv, where):
        part = total.at[where(me_r)]
        for d in range(1, nr):
            small(part, part, recv, {"rows": lax.rem(me_r + d, nr)})

    def arrived(stage, recv):
        drain(stage.at[pl.ds(1, nr - 1)], recv)

    def summed(total, stage, where):
        value = total[where(me_r)]
        for d in range(1, nr):
            value = value + stage[d]
        return value

    def bands(count):
        return lambda peer: (pl.ds(pl.multiple_of(peer * count, count), count), slice(None))

    def tiles(count):
        half = cross.shape[1] // 2
        return lambda peer: (
            pl.ds(pl.multiple_of(peer // 2 * count, count), count),
            pl.ds(pl.multiple_of(lax.rem(peer, 2) * half, half), half),
        )

    def long(source, first, count):
        return pl.ds(pl.multiple_of(source * depth + first, head), count)

    def add_all(source):
        def step(i, carry):
            first = i * step_rows
            rows = pl.ds(pl.multiple_of(first, step_rows), step_rows)
            cross[...] += dot3(turned[source, :, rows], trail[long(source, first, step_rows), :])
            return carry

        lax.fori_loop(0, 4, step, 0)

    def add_head(source):
        cross[...] += dot_t(block[source, top, :], trail[long(source, 0, head), :])

    def add_lanes(source, first, count):
        lanes = pl.ds(first, count)
        cross[lanes, :] += dot3(turned[source, lanes, rest], trail[long(source, head, tall), :])

    known = turns[6][0]
    block_rows = depth // 4

    def mix(start):
        tile = square[:, hw:]
        lane = lax.broadcasted_iota(jnp.int32, tile.shape, 1)
        m_hi, m_lo = split(jnp.where(lane < hw // 2, pltpu.roll(tile, hw // 2, 1), tile))
        low = lax.broadcasted_iota(jnp.int32, (block_rows, hw), 1) >= hw // 2

        def step(i, carry):
            i = i + start
            rows = pl.ds(pl.multiple_of(lax.rem(i, 4) * block_rows, block_rows), block_rows)
            here = pl.ds(pl.multiple_of(i * block_rows, block_rows), block_rows)
            p_hi, p_lo = split(block[side * 2 + i // 4, rows, :])
            product = mul(p_hi, m_hi) + (mul(p_lo, m_hi) + mul(p_hi, m_lo))
            high = product.astype(jnp.bfloat16)
            wide = high.astype(jnp.float32)
            mixed[here, pl.ds(0, hw)] = jnp.where(low, product - wide, wide).astype(jnp.bfloat16)
            mixed[here, pl.ds(hw, hw)] = high
            return carry

        lax.fori_loop(0, 4, step, 0)

    def update_own():
        weights_out[...] += dot3(square[:, hw:known], cross_sum[pl.ds(hw, known - hw), :])
        w_hi, w_lo = split(weights_out[...])
        count = 2 * block_rows

        def step(i, carry):
            rows = pl.ds(pl.multiple_of(lax.rem(i, 2) * count, count), count)
            here = pl.ds(pl.multiple_of(side * 2 * depth + i * count, count), count)
            p_hi, p_lo = split(block[side * 2 + i // 2, rows, :])
            trail[here, :] -= mul(p_hi, w_hi) + (mul(p_lo, w_hi) + mul(p_hi, w_lo))
            return carry

        lax.fori_loop(0, 4, step, 0)

    def turn_back(source, first):
        lanes = pl.ds(first, hw)

        def step(i, carry):
            rows = pl.ds(pl.multiple_of(head + i * head, head), head)
            block[source, rows, lanes] = turned[source, lanes, rows].T
            return carry

        lax.fori_loop(0, tall // head, step, 0)

    mine = pl.ds(pl.multiple_of(place * hw, hw), hw)
    other = pl.ds(pl.multiple_of(hw - place * hw, hw), hw)
    gram_pair = small(gram.at[other], half_stage, gram_recv.at[0], {"cols": partner})
    turned_copy = remote(turned.at[me_c], turned.at[me_c], bulk_sem, half_recv.at[1], {"cols": partner})
    load_trail.wait()
    cross[...] = jnp.zeros_like(cross)
    add_all(me_c)
    gram_pair.wait_recv()
    half_sum[...] = gram[mine, :] + half_stage[...]
    scatter(half_sum, gram_stage, gram_recv.at[1], bands(piece))
    head_copy.wait_recv()
    part = block.at[across, top]
    head_forward = remote(part, part, bulk_sem, fwd_recv.at[0], {"cols": partner})
    add_head(across)
    turned_copy.wait_recv()
    add_all(partner)
    arrived(gram_stage, gram_recv.at[1])
    col_stage[side] = summed(half_sum, gram_stage, bands(piece))
    exchange = small(col_stage.at[side], col_stage.at[side], gram_recv.at[2], {"cols": across})
    while len(y_copies) < len(turns):
        send_turn()
    head_forward.wait_recv()
    add_head(behind)

    forwards = {}

    def take(t):
        y_copies[t].wait_recv()
        part = turned.at[across, pl.ds(*turns[t]), rest]
        forwards[t] = remote(part, part, bulk_sem, fwd_recv.at[1 + t], {"cols": partner})

    def take_forward(t):
        forwards[t].wait_recv()

    late_first = turns[7][0]
    twin = me_r + 1 - 2 * lax.rem(me_r, 2)
    bounds = ((0, hw), turns[4], turns[5], turns[6])
    stages = (early_stage, tile_stage.at[0], tile_stage.at[1], tile_stage.at[2])
    wheres = (bands(hw // nr),) + (tiles(turns[6][1] * 2 // nr),) * 3

    def start_cross(g):
        scatter(cross.at[pl.ds(*bounds[g])], stages[g], cross_recv.at[2 * g], wheres[g])

    def share_cross(g):
        arrived(stages[g], cross_recv.at[2 * g])
        total = cross_sum.at[pl.ds(*bounds[g])]
        total[wheres[g](me_r)] = summed(cross.at[pl.ds(*bounds[g])], stages[g], wheres[g])
        gather(total, cross_recv.at[2 * g + 1], wheres[g])

    def shared(g):
        arrived(stages[g], cross_recv.at[2 * g + 1])

    def lanes_of(t):
        first, count = turns[t]
        return pl.ds(first, count), pl.ds(first - late_first, count)

    def start_pair(t):
        lanes, late = lanes_of(t)
        mine = pair_stage.at[lax.rem(me_r, 2), late]
        mine[...] = cross[lanes, :]
        return small(mine, mine, cross_recv.at[8], {"rows": twin})

    def spread_pair(t, pair):
        _, late = lanes_of(t)
        pair.wait_recv()
        mine = late_stage.at[me_r, late]
        mine[...] = pair_stage[0, late, :] + pair_stage[1, late, :]
        for d in range(2, nr, 2):
            small(mine, mine, cross_recv.at[9], {"rows": lax.rem(me_r + d, nr)})

    def finish_pair(t):
        lanes, late = lanes_of(t)
        drain(late_stage.at[pl.ds(1, nr // 2 - 1), late], cross_recv.at[9])
        value = late_stage[lax.rem(me_r, 2), late, :]
        for step in range(2, nr, 2):
            value = value + late_stage[lax.rem(me_r, 2) + step, late, :]
        cross_sum[lanes, :] = value

    def spread(t):
        lanes, late = lanes_of(t)
        mine = late_stage.at[me_r, late]
        mine[...] = cross[lanes, :]
        for d in range(1, nr):
            small(mine, mine, cross_recv.at[10], {"rows": lax.rem(me_r + d, nr)})

    def finish(t):
        lanes, late = lanes_of(t)
        drain(late_stage.at[pl.ds(1, nr - 1), late], cross_recv.at[10])
        value = late_stage[0, late, :]
        for step in range(1, nr):
            value = value + late_stage[step, late, :]
        cross_sum[lanes, :] = value

    exchange.wait_recv()
    gram_half = gram_sum.at[mine]
    gram_half[pl.ds(pl.multiple_of(me_r * piece, piece), piece), :] = col_stage[0] + col_stage[1]
    gather(gram_half, gram_recv.at[3], bands(piece))
    take(0)
    arrived(gram_stage, gram_recv.at[3])
    gram_swap = small(gram_half, gram_half, gram_recv.at[4], {"cols": partner})
    half_copy = remote(panel, block.at[me_c], bulk_sem, half_recv.at[0], {"cols": partner})
    gram_swap.wait_recv()
    work[...] = gram_sum[pl.ds(0, hw), pl.ds(0, hw)]
    minv[...] = unit(hw)
    eighth = hw // 8
    take_forward(0)
    eliminate(work, minv, 0, 2 * eighth)
    take(1)
    eliminate(work, minv, 2 * eighth, 8 * eighth)
    take_forward(1)
    upper1, inverse1 = scale_rows(work, minv)
    cross1 = dot(inverse1, gram_sum[pl.ds(0, hw), pl.ds(hw, hw)])
    upper_out[pl.ds(0, hw), pl.ds(0, hw)] = upper1
    upper_out[pl.ds(0, hw), pl.ds(hw, hw)] = cross1
    upper_out[pl.ds(hw, hw), pl.ds(0, hw)] = jnp.zeros_like(upper1)
    work[...] = gram_sum[pl.ds(hw, hw), pl.ds(hw, hw)] - dot_t(cross1, cross1)
    inv[pl.ds(0, hw), pl.ds(0, hw)] = inverse1
    minv[...] = unit(hw)
    take(2)
    eliminate(work, minv, 0, 5 * eighth)
    take_forward(2)
    take(3)
    add_lanes(across, 0, hw)
    eliminate(work, minv, 5 * eighth, 6 * eighth)
    take_forward(3)
    add_lanes(behind, 0, hw)
    start_cross(0)
    eliminate(work, minv, 6 * eighth, 8 * eighth)
    take(4)
    upper2, inverse2 = scale_rows(work, minv)
    upper_out[pl.ds(hw, hw), pl.ds(hw, hw)] = upper2
    inverse1 = inv[pl.ds(0, hw), pl.ds(0, hw)]
    corner = -dot(inverse2, dot_t(upper_out[pl.ds(0, hw), pl.ds(hw, hw)], inverse1))
    inv[pl.ds(0, hw), pl.ds(hw, hw)] = jnp.zeros_like(inverse1)
    inv[pl.ds(hw, hw), pl.ds(0, hw)] = corner
    inv[pl.ds(hw, hw), pl.ds(hw, hw)] = inverse2
    inverse = inv[...]
    square[...] = dot_t(inverse, inverse)
    add_lanes(across, *turns[4])
    take_forward(4)
    add_lanes(behind, *turns[4])
    start_cross(1)
    turn_back(across, 0)
    share_cross(0)
    take(5)
    add_lanes(across, *turns[5])
    turn_back(behind, 0)
    take_forward(5)
    add_lanes(behind, *turns[5])
    start_cross(2)
    half_copy.wait_recv()
    share_cross(1)
    mix(0)
    take(6)
    add_lanes(across, *turns[6])
    mix(4)
    take_forward(6)
    add_lanes(behind, *turns[6])
    start_cross(3)
    share_cross(2)
    shared(0)
    weights_out[...] = dot(square[:, :hw], cross_sum[pl.ds(0, hw), :])
    take(7)
    add_lanes(across, *turns[7])
    take(8)
    add_lanes(across, *turns[8])
    take_forward(7)
    add_lanes(behind, *turns[7])
    pair = start_pair(7)
    take_forward(8)
    add_lanes(behind, *turns[8])
    spread(8)
    turn_back(across, hw)
    share_cross(3)
    turn_back(behind, hw)
    spread_pair(7, pair)
    shared(1)
    shared(2)
    update_own()
    coupling_out[...] = dot(inv[:, :hw], cross_sum[pl.ds(0, hw), :])
    shared(3)
    finish_pair(7)
    finish(8)
    drain(turned, bulk_sem)
    total = sum(small_rows)
    drain(block.at[0, pl.ds(0, total)], small_sem)


def update_kernel(
    shrink, block, trailing, upper, coupling, weights, r_factor, r_cross, updated,
    small, w_hi, w_lo, out, small_sem, out_sem,
):
    small[0] = upper[...] * shrink
    small[1] = coupling[...] * shrink
    copies = [
        pltpu.make_async_copy(small.at[0], r_factor, small_sem.at[0]),
        pltpu.make_async_copy(small.at[1], r_cross, small_sem.at[1]),
    ]
    for copy in copies:
        copy.start()
    w = weights[...]
    high = w.astype(jnp.bfloat16)
    w_hi[...] = high
    w_lo[...] = (w - high.astype(jnp.float32)).astype(jnp.bfloat16)
    tile = out.shape[0] // TILES

    def mul(left, right):
        return jnp.dot(left, right, preferred_element_type=jnp.float32)

    def window(i):
        return pl.ds(pl.multiple_of(i * tile, tile), tile)

    def store(i):
        return pltpu.make_async_copy(out.at[window(i)], updated.at[window(i)], out_sem.at[i])

    def step(i, carry):
        rows = window(i)
        p = block[rows, :]
        p_hi = p.astype(jnp.bfloat16)
        p_lo = (p - p_hi.astype(jnp.float32)).astype(jnp.bfloat16)
        product = mul(p_hi, w_hi[...]) + (mul(p_lo, w_hi[...]) + mul(p_hi, w_lo[...]))
        out[rows, :] = trailing[rows, :] - product
        store(i).start()
        return carry

    lax.fori_loop(0, TILES, step, 0)
    for i in range(TILES):
        store(i).wait()
    for copy in copies:
        copy.wait()


def finish_kernel(
    shrink, block, trailing, upper, coupling, weights, inv, total, square, mixed, r_factor, r_cross, updated,
    small, w_hi, w_lo, c_all, out, small_sem, out_sem,
):
    hw = inv.shape[0] // 2
    part = hw // 2
    c_hi, c_lo = split(total[pl.ds(hw + part, part), :])
    c_all[pl.ds(0, part), :] = c_hi
    c_all[pl.ds(part, part), :] = c_hi
    c_all[pl.ds(hw, part), :] = c_lo
    c_all[pl.ds(hw + part, part), :] = jnp.zeros_like(c_lo)
    depth = out.shape[0]
    own = depth // 2
    side = lax.axis_index("cols") // 2
    tile = depth // TILES

    def window(start, first, count):
        return pl.ds(pl.multiple_of(start + first, tile // 2), count)

    def store(rows):
        pltpu.make_async_copy(out.at[rows], updated.at[rows], out_sem).start()

    first = 0
    for count in (tile // 2,) * TILES:
        rows = window(side * own, first, count)
        out[rows, :] = trailing[rows, :] - mul(mixed[pl.ds(first, count), :], c_all[...])
        store(rows)
        first += count
    small[0] = upper[...] * shrink
    factor_copy = pltpu.make_async_copy(small.at[0], r_factor, small_sem.at[0])
    factor_copy.start()
    row = lax.broadcasted_iota(jnp.int32, (hw, total.shape[1]), 0)
    late = jnp.where(row < part, 0.0, total[pl.ds(hw, hw), :])
    w_hi[...], w_lo[...] = split(weights[...] + dot3(square[:, hw:], late))
    first = 0
    for count in (tile // 2,) + (tile,) * (TILES // 2 - 1) + (tile // 2,):
        rows = window((1 - side) * own, first, count)
        p_hi, p_lo = split(block[rows, :])
        product = mul(p_hi, w_hi[...]) + (mul(p_lo, w_hi[...]) + mul(p_hi, w_lo[...]))
        out[rows, :] = trailing[rows, :] - product
        store(rows)
        first += count
    small[1] = (coupling[...] + dot3(inv[:, hw:], total[hw:, :])) * shrink
    cross_copy = pltpu.make_async_copy(small.at[1], r_cross, small_sem.at[1])
    cross_copy.start()
    pltpu.make_async_copy(out, updated, out_sem).wait()
    factor_copy.wait()
    cross_copy.wait()


def local(nr, nc, panel_cols, trailing):
    depth, width = panel_cols.shape
    rows, cols = trailing.shape
    half = nc // 2
    piece = width // nr
    groups = 2 if width % (2 * 8 * nr) == 0 else 1
    wide = width // groups
    f32 = jnp.float32
    square = jax.ShapeDtypeStruct((width, width), f32)
    tall = jax.ShapeDtypeStruct((width, cols), f32)
    dma = pltpu.SemaphoreType.DMA
    vmem = pl.BlockSpec(memory_space=pltpu.VMEM)
    hbm = pl.BlockSpec(memory_space=pltpu.HBM)
    fine = nc == 4 and nr >= 4 and nr & (nr - 1) == 0 and width % 256 == 0 and (width // 2) % (8 * nr) == 0 and (width // 4) % (8 * nr) == 0 and depth % 2048 == 0 and width // 8 == 4 * nr and cols % 256 == 0
    if fine:
        gram_scratch = [
            pltpu.VMEM((width // 2, width), f32),
            pltpu.VMEM((width // 2, width), f32),
            pltpu.VMEM((nr, piece // 2, width), f32),
            pltpu.VMEM((2, piece // 2, width), f32),
        ]
        body, turns = transposed_kernel, len(turn_plan(width))
        cross_scratch = [
            pltpu.VMEM((width, cols), f32),
            pltpu.VMEM((nr, width // 2 // nr, cols), f32),
            pltpu.VMEM((3, nr, width // 4 // nr, cols // 2), f32),
            pltpu.VMEM((2, width // 4, cols), f32),
            pltpu.VMEM((nr, width // 4, cols), f32),
            pltpu.VMEM((nc, width, depth), f32),
        ]
        items = 1 + turns
        sems = [dma((2,)), pltpu.SemaphoreType.REGULAR((nr.bit_length() - 2,)), dma, dma, dma((items,)), dma((2,)), dma((items,)), dma((5,)), dma((11,))]
    else:
        body = factor_kernel
        gram_scratch = [pltpu.VMEM((nr, piece, width), f32), pltpu.VMEM((nc, piece, width), f32)]
        sems = [
            dma((2,)),
            dma((ITEMS,)), dma((ITEMS,)),
            dma((half,)), dma((half,)),
            dma((ITEMS * half,)), dma((ITEMS * half,)),
            dma((nr,)), dma((nr,)),
            dma((nc,)), dma((nc,)),
            dma((nr,)), dma((nr,)),
            dma((groups, nr)), dma((groups, nr)),
            dma((groups, nr)), dma((groups, nr)),
        ]
        cross_scratch = [
            pltpu.VMEM((groups, wide, cols), f32),
            pltpu.VMEM((groups, nr, wide // nr, cols), f32),
            pltpu.VMEM((groups, wide, cols), f32),
        ]
    shapes = (jax.ShapeDtypeStruct((nc, depth, width), f32), jax.ShapeDtypeStruct((rows, cols), f32), square, tall, tall)
    shapes += (square, tall, square, jax.ShapeDtypeStruct((2 * depth, width), jnp.bfloat16)) if fine else ()
    block, *results = pl.pallas_call(
        functools.partial(body, nr, nc),
        out_shape=shapes,
        in_specs=[hbm, hbm],
        out_specs=(vmem,) * len(shapes),
        scratch_shapes=[
            pltpu.VMEM((width, width), f32),
            *gram_scratch,
            pltpu.VMEM((width, width), f32),
            *cross_scratch,
            pltpu.VMEM((width // 2, width // 2), f32),
            pltpu.VMEM((width // 2, width // 2), f32),
            *[pltpu.VMEM((width, width), f32)] * (0 if fine else 2),
            *sems,
        ],
        compiler_params=pltpu.CompilerParams(
            collective_id=0, has_side_effects=True, vmem_limit_bytes=(32 if fine else 20) * 1024 * 1024
        ),
        name="factor",
    )(*(pltpu.with_memory_space_constraint(x, pltpu.HBM) for x in (panel_cols, trailing)))

    shrink = 1.0 / math.sqrt(rows * nr)
    r_factor, r_cross, updated = pl.pallas_call(
        functools.partial(finish_kernel if fine else update_kernel, shrink),
        out_shape=(square, tall, jax.ShapeDtypeStruct((rows, cols), f32)),
        in_specs=[vmem] * len(shapes),
        out_specs=(hbm,) * 3,
        scratch_shapes=[
            pltpu.VMEM((2, width, cols), f32),
            *[pltpu.VMEM((width, cols), jnp.bfloat16)] * (3 if fine else 2),
            pltpu.VMEM((rows, cols), f32),
            dma((2,)),
            dma if fine else dma((TILES,)),
        ],
        compiler_params=pltpu.CompilerParams(vmem_limit_bytes=24 * 1024 * 1024),
        name="update",
    )(block.reshape(rows, width), *results)
    return r_factor, r_cross, updated


def solution(mesh):
    P = jax.sharding.PartitionSpec
    body = functools.partial(local, mesh.shape["rows"], mesh.shape["cols"])
    in_specs = (P(("rows", "cols"), None), P("rows", "cols"))
    out_specs = (P(), P(None, "cols"), P("rows", "cols"))
    return jax.shard_map(body, mesh=mesh, in_specs=in_specs, out_specs=out_specs, check_vma=False)
```
